32 devices in a mesh: dp: 8 (over z, y), tensor: 4 (over x, core).
Axes of the slice: x: 2, y: 2, z: 4, core: 2. Of those that a mesh axis runs over, the one named last changes fastest.
Arguments:
- tokens: bfloat16 [24576, 768], P(('dp', 'tensor')), may hold values from -6 to 6
- mask_bits: int32 [24576], P(('dp', 'tensor')), may hold values from 0 to 1, as said below
- cotangent: bfloat16 [24576, 768], P(('dp', 'tensor')), may hold values from -6 to 6
- mask_vector: float32 [768], replicated, may hold values from -4 to 4
- first_gain: float32 [768], replicated, may hold values from 0.25 to 1.75
- first_shift: float32 [768], replicated, may hold values from -3 to 3
- attn_weight: bfloat16 [768, 3, 768], P(None, None, 'tensor'), may hold values from -0.21875 to 0.21875
- attn_bias: float32 [2, 768], P(None, 'tensor'), may hold values from -3 to 3
- merge_weight: bfloat16 [768, 768], P('tensor'), may hold values from -0.875 to 0.875
- merge_bias: float32 [768], replicated, may hold values from -3 to 3
- second_gain: float32 [768], replicated, may hold values from 0.25 to 1.75
- second_shift: float32 [768], replicated, may hold values from -3 to 3
- up_weight: bfloat16 [768, 3072], P(None, 'tensor'), may hold values from -0.21875 to 0.21875
- up_bias: float32 [3072], P('tensor'), may hold values from -3 to 3
- down_weight: bfloat16 [3072, 768], P('tensor'), may hold values from -0.109375 to 0.109375
- down_bias: float32 [768], replicated, may hold values from -3 to 3
Outputs:
- layer_out: bfloat16 [24576, 768], P(('dp', 'tensor'))
- grad_tokens: float32 [24576, 768], P(('dp', 'tensor'))
- grad_mask_vector: float32 [768], replicated
- grad_first_gain: float32 [768], replicated
- grad_first_shift: float32 [768], replicated
- grad_attn_weight: float32 [768, 3, 768], P(None, None, 'tensor')
- grad_attn_bias: float32 [2, 768], P(None, 'tensor')
- grad_merge_weight: float32 [768, 768], P('tensor')
- grad_merge_bias: float32 [768], replicated
- grad_second_gain: float32 [768], replicated
- grad_second_shift: float32 [768], replicated
- grad_up_weight: float32 [768, 3072], P(None, 'tensor')
- grad_up_bias: float32 [3072], P('tensor')
- grad_down_weight: float32 [3072, 768], P('tensor')
- grad_down_bias: float32 [768], replicated
The draws below stay inside these ranges and needn't reach their ends.
Inputs may be any that keep to these rules, and one draw needn't show every extreme that they name: `mask_bits`: 1 marks a masked token; each clip of 4096 consecutive tokens has its own masking rate, from one half to all.
All inputs are finite; a program needn't handle non-finite values.
Results may differ from the reference program's by a relative error of at most 0.018.
Values may be sent and summed in bfloat16 or wider, within the bound.
No kernel may reach another device: no remote copies, remote signals or barrier semaphores. Data moves between devices by JAX's collectives and lax.ppermute only.
A program may use at most 128 MiB of HBM per device.

```python
import math
import jax
import jax.numpy as jnp
from jax import lax

D = 768
HEADS = 12
HEAD = 64
FF = 3072
WIN = 256
CLIP_FR = 16
TOKENS = 24576
N_TENSOR = 4


def draw_mask_bits(key, part):
    clip_tokens = CLIP_FR * WIN
    clip_count = (TOKENS + clip_tokens - 1) // clip_tokens
    level_key = jax.random.fold_in(key, 11)
    token_key = jax.random.fold_in(key, 23)
    clip_levels = jax.random.randint(level_key, (clip_count,), 512, 1025)
    token_draws = jax.random.randint(token_key, (TOKENS,), 0, 1024)
    clip_owner = jnp.arange(TOKENS) // clip_tokens
    return (token_draws < clip_levels[clip_owner]).astype(jnp.int32)


def block_scale(rng, shape, cuts, smallest, high):
    def one(axis_at, shards_of):
        draws = jax.random.uniform(jax.random.fold_in(jax.random.fold_in(rng, 6), axis_at), (shards_of,), jnp.float32, smallest / len(cuts), high / len(cuts))
        return jnp.repeat(jnp.exp(draws), shape[axis_at] // shards_of).reshape((-1,) + (1,) * (len(shape) - axis_at - 1))

    factor_of = one(*cuts[0])
    for cut in cuts[1:]:
        factor_of = factor_of * one(*cut)
    return factor_of


def scatter_about(stream_key, extent, deviation, limit, cuts=(), dtype=jnp.bfloat16):
    entries = deviation * jax.random.normal(stream_key, extent, jnp.float32)
    if cuts:
        entries = entries * block_scale(stream_key, extent, cuts, -0.22, 0.18)
    return jnp.clip(entries, -limit, limit).astype(dtype)


def setup_inputs(seed: int = 0) -> dict:
    splits = jax.random.split(jax.random.key(seed), 17)
    tokens = scatter_about(splits[0], (TOKENS, D), 1.0, 6.0, ((0, 32),))
    mask_bits = draw_mask_bits(jax.random.fold_in(splits[16], 71), 0)
    cotangent = scatter_about(splits[2], (TOKENS, D), 1.0, 6.0, ((0, 32),))
    mask_vector = scatter_about(splits[3], (D,), 1.0, 4.0, (), jnp.float32)
    first_gain = jnp.clip(1.0 + 0.15 * jax.random.normal(splits[4], (D,), jnp.float32), 0.25, 1.75)
    first_shift = scatter_about(splits[5], (D,), 0.5, 3.0, (), jnp.float32)
    attn_weight = scatter_about(splits[6], (D, 3, D), D ** -0.5, 0.21875, ((2, 4),))
    attn_bias = scatter_about(splits[7], (2, D), 0.5, 3.0, ((1, 4),), jnp.float32)
    merge_weight = scatter_about(splits[8], (D, D), (D // 16) ** -0.5, 0.875, ((0, 4),))
    merge_bias = scatter_about(splits[9], (D,), 0.5, 3.0, (), jnp.float32)
    second_gain = jnp.clip(1.0 + 0.15 * jax.random.normal(splits[10], (D,), jnp.float32), 0.25, 1.75)
    second_shift = scatter_about(splits[11], (D,), 0.5, 3.0, (), jnp.float32)
    up_weight = scatter_about(splits[12], (D, FF), D ** -0.5, 0.21875, ((1, 4),))
    up_bias = scatter_about(splits[13], (FF,), 0.5, 3.0, ((0, 4),), jnp.float32)
    down_weight = scatter_about(splits[14], (FF, D), FF ** -0.5, 0.109375, ((0, 4),))
    down_bias = scatter_about(splits[15], (D,), 0.5, 3.0, (), jnp.float32)
    return {"tokens": tokens, "mask_bits": mask_bits, "cotangent": cotangent, "mask_vector": mask_vector, "first_gain": first_gain, "first_shift": first_shift, "attn_weight": attn_weight, "attn_bias": attn_bias, "merge_weight": merge_weight, "merge_bias": merge_bias, "second_gain": second_gain, "second_shift": second_shift, "up_weight": up_weight, "up_bias": up_bias, "down_weight": down_weight, "down_bias": down_bias}


@jax.custom_vjp
def low(v):
    return lax.optimization_barrier(v.astype(jnp.bfloat16)).astype(jnp.float32)

@jax.custom_vjp
def low_back(v):
    return v

def low_keep(v):
    return (low(v), None)

def low_pass(kept, grad):
    return (grad,)

def back_keep(v):
    return (v, None)

def back_low(kept, grad):
    return (low(grad),)
low.defvjp(low_keep, low_pass)
low_back.defvjp(back_keep, back_low)

def layer_norm(values, norm_gain, norm_shift):
    centre = values - lax.optimization_barrier(jnp.mean(values, axis=-1, keepdims=True))
    spread = lax.optimization_barrier(jnp.mean(centre * centre, axis=-1, keepdims=True))
    return centre * lax.rsqrt(spread + 1e-06) * norm_gain + norm_shift

def attend_block(parts):
    query_part, key_part, value_part = parts
    highest = lax.Precision.HIGHEST
    scores = jnp.einsum('wqhd,wkhd->whqk', query_part, key_part, precision=highest) * HEAD ** (-0.5)
    scores = low_back(scores)
    row_peak = lax.optimization_barrier(jnp.max(scores, axis=-1, keepdims=True))
    raw_weights = jnp.exp(scores - row_peak)
    softmax_out = low(raw_weights / lax.optimization_barrier(jnp.sum(raw_weights, axis=-1, keepdims=True)))
    mixed_heads = jnp.einsum('whqk,wkhd->wqhd', softmax_out, value_part, precision=highest)
    return low_back(low(mixed_heads))

def grouped_product(left, right):
    col_span = left.shape[1] // N_TENSOR
    total_sum = jnp.zeros((left.shape[0], right.shape[1]), jnp.float32)
    for group_index in range(N_TENSOR):
        lower = group_index * col_span
        upper = lower + col_span
        total_sum = total_sum + low(jnp.dot(left[:, lower:upper], right[lower:upper], precision=lax.Precision.HIGHEST))
    return total_sum

def reference(tokens, mask_bits, cotangent, mask_vector, first_gain, first_shift, attn_weight, attn_bias, merge_weight, merge_bias, second_gain, second_shift, up_weight, up_bias, down_weight, down_bias):
    highest = lax.Precision.HIGHEST
    chosen = (mask_bits == 1)[:, None]
    windows = TOKENS // WIN
    per_block = math.gcd(windows, max(1, 1024 // WIN))
    block_shape = (windows // per_block, per_block, WIN, HEADS, HEAD)

    def forward(token_vals, vector, gain_one, shift_one, attn_w, attn_b, merge_w, merge_b, gain_two, shift_two, up_w, up_b, down_w, down_b):
        mixed_rows = jnp.where(chosen, vector[None, :], token_vals)
        normed_one = low(layer_norm(mixed_rows, gain_one, shift_one))
        col_span = D // N_TENSOR
        pieces = []
        for group_index in range(N_TENSOR):
            columns = attn_w[:, :, group_index * col_span:(group_index + 1) * col_span].reshape(D, 3 * col_span)
            pieces.append(jnp.dot(low_back(normed_one), columns, precision=highest).reshape(TOKENS, 3, col_span))
        projected = jnp.concatenate(pieces, axis=2)
        queries = low_back(low(projected[:, 0] + attn_b[0]))
        key_rows = low_back(low(projected[:, 1]))
        value_rows = low_back(low(projected[:, 2] + attn_b[1]))
        attended = lax.map(jax.checkpoint(attend_block), (queries.reshape(block_shape), key_rows.reshape(block_shape), value_rows.reshape(block_shape)))
        attended = attended.reshape(TOKENS, D)
        residual = mixed_rows + low_back(grouped_product(attended, merge_w)) + merge_b
        normed_two = low(layer_norm(residual, gain_two, shift_two))
        hidden_span = FF // N_TENSOR
        up_pieces = []
        for group_index in range(N_TENSOR):
            up_cols = up_w[:, group_index * hidden_span:(group_index + 1) * hidden_span]
            up_pieces.append(jnp.dot(low_back(normed_two), up_cols, precision=highest))
        pre_act = low_back(jnp.concatenate(up_pieces, axis=1) + up_b)
        activated = low(jax.nn.gelu(pre_act, approximate=True))
        return residual + low_back(grouped_product(activated, down_w)) + down_b
    arguments = (tokens.astype(jnp.float32), mask_vector, first_gain, first_shift, attn_weight.astype(jnp.float32), attn_bias, merge_weight.astype(jnp.float32), merge_bias, second_gain, second_shift, up_weight.astype(jnp.float32), up_bias, down_weight.astype(jnp.float32), down_bias)
    layer_out, pull_back = jax.vjp(forward, *arguments)
    gradients = pull_back(jnp.where(chosen, cotangent.astype(jnp.float32), jnp.zeros_like(layer_out)))
    return (layer_out.astype(jnp.bfloat16), gradients[0], gradients[1], gradients[2], gradients[3], gradients[4], gradients[5], gradients[6], gradients[7], gradients[8], gradients[9], gradients[10], gradients[11], gradients[12], gradients[13])
```

```python
import functools

import jax
import jax.numpy as jnp
from jax import lax
from jax.experimental import pallas as pl
from jax.experimental.pallas import tpu as pltpu
from jax.sharding import PartitionSpec as P

HEAD = 64
WIN = 256
EPS = 1e-06
SCALE = HEAD**-0.5
ROWS = 64
F32 = jnp.float32
BF16 = jnp.bfloat16


def dot(a, b):
    return lax.dot_general(a, b, (((1,), (0,)), ((), ())), preferred_element_type=F32)


def dot_nt(a, b):
    return lax.dot_general(a, b, (((1,), (1,)), ((), ())), preferred_element_type=F32)


def dot_tn(a, b):
    return lax.dot_general(a, b, (((0,), (0,)), ((), ())), preferred_element_type=F32)


def call(body, outs, name, flops, vmem=24):
    shapes = tuple(jax.ShapeDtypeStruct(s, d) for s, d in outs)

    def run(*args):
        moved = sum(a.size * a.dtype.itemsize for a in args)
        return pl.pallas_call(
            body,
            out_shape=shapes,
            in_specs=[pl.BlockSpec(memory_space=pltpu.VMEM)] * len(args),
            out_specs=tuple(pl.BlockSpec(memory_space=pltpu.VMEM) for _ in shapes),
            compiler_params=pltpu.CompilerParams(vmem_limit_bytes=vmem << 20),
            cost_estimate=pl.CostEstimate(
                flops=int(flops), bytes_accessed=moved, transcendentals=0
            ),
            name=name,
        )(*args)

    return run


def row_loop(rows, width, sums, body):
    def step(i, carry):
        at = pl.ds(pl.multiple_of(i * ROWS, ROWS), ROWS)
        parts = body(at)
        return tuple(
            c + jnp.sum(p.reshape(ROWS // 8, 8, width), axis=0) for c, p in zip(carry, parts)
        )

    zero = tuple(jnp.zeros((8, width), F32) for _ in range(sums))
    done = lax.fori_loop(0, rows // ROWS, step, zero)
    return [jnp.sum(c, axis=0, keepdims=True) for c in done]


def normalize(v):
    centre = v - jnp.mean(v, axis=-1, keepdims=True)
    scale = lax.rsqrt(jnp.mean(centre * centre, axis=-1, keepdims=True) + EPS)
    return centre * scale, scale


def mix(chosen, vector, tokens):
    return jnp.where(chosen > 0.5, vector, tokens.astype(F32))


def prep_body(tok, msk, cot, vec, gain, shift, n1, top, topt, gdb):
    rows, width = tok.shape

    def body(at):
        chosen = msk[at, :]
        hat, _ = normalize(mix(chosen, vec[...], tok[at, :]))
        n1[at, :] = (hat * gain[...] + shift[...]).astype(BF16)
        grad = jnp.where(chosen > 0.5, cot[at, :].astype(F32), 0.0)
        top[at, :] = grad.astype(BF16)
        return (grad,)

    (total,) = row_loop(rows, width, 1, body)
    gdb[...] = total
    topt[...] = top[...].T


def head_rows(cols):
    lane = lax.broadcasted_iota(jnp.int32, (1, cols), 1)
    return [
        ((lane >= h * HEAD) & (lane < (h + 1) * HEAD)).astype(F32).astype(BF16)
        for h in range(cols // HEAD)
    ]


def attn_fwd_body(slots, n1, bias, *refs):
    ins, outs = refs[:slots], refs[slots:]
    rows = n1.shape[0]
    cols = ins[0].shape[1]
    marks = head_rows(cols)
    for s in range(slots):
        w, qkv, att = ins[s], outs[2 * s], outs[2 * s + 1]
        qkv[0] = (dot_nt(n1[...], w[0]) + bias[s : s + 1, :cols]).astype(BF16)
        qkv[1] = dot_nt(n1[...], w[1]).astype(BF16)
        qkv[2] = (dot_nt(n1[...], w[2]) + bias[s : s + 1, cols : 2 * cols]).astype(BF16)
        for i in range(rows // WIN):
            at = slice(i * WIN, (i + 1) * WIN)
            q, k, v = qkv[0, at, :], qkv[1, at, :], qkv[2, at, :]
            out = None
            for mark in marks:
                p = softmax(dot_nt(q * mark, k))[0].astype(BF16)
                part = dot(p, v * mark)
                out = part if out is None else out + part
            att[at, :] = out.astype(BF16)


def softmax(raw):
    peak = jnp.max(raw, axis=-1, keepdims=True)
    e = jnp.exp((raw - peak) * SCALE)
    return (e * (1.0 / jnp.sum(e, axis=-1, keepdims=True)),)


def mid_body(slots, tok, msk, vec, mbias, gain, shift, *refs):
    atts, merges = refs[:slots], refs[slots : 2 * slots]
    res, n2, n2t = refs[2 * slots :]
    rows, width = tok.shape
    total = dot(atts[0][...], merges[0][...])
    for s in range(1, slots):
        total = total + dot(atts[s][...], merges[s][...])
    res[...] = total

    def body(at):
        r = mix(msk[at, :], vec[...], tok[at, :]) + res[at, :] + mbias[...]
        res[at, :] = r
        hat, _ = normalize(r)
        n2[at, :] = (hat * gain[...] + shift[...]).astype(BF16)
        return ()

    row_loop(rows, width, 0, body)
    n2t[...] = n2[...].T


GELU_C = 0.7978845608028654
GELU_A = 0.044715


def ffn_body(slots, first, n2, n2t, top, topt, bias, *refs):
    ups, downs = refs[:slots], refs[slots : 2 * slots]
    refs = refs[2 * slots :]
    if not first:
        y_in, g_in = refs[:2]
        refs = refs[2:]
    grads, (y, g, gb), act, pg = refs[: 2 * slots], refs[2 * slots : 2 * slots + 3], refs[-2], refs[-1]
    hidden = ups[0].shape[1]
    tile = 256
    for s in range(slots):
        up, down = ups[s], downs[s]
        gd, gu = grads[2 * s], grads[2 * s + 1]
        for t in range(hidden // tile):
            c = slice(t * tile, (t + 1) * tile)
            pre = dot(n2[...], up[:, c]) + bias[s : s + 1, c]
            sq = pre * pre
            th = jnp.tanh(GELU_C * (pre + GELU_A * (sq * pre)))
            half = 0.5 * (1.0 + th)
            a = (pre * half).astype(BF16)
            slope = half + (0.5 * GELU_C) * pre * (1.0 - th * th) * (1.0 + (3.0 * GELU_A) * sq)
            act[:, c] = a
            gd[:, c] = dot(topt[...], a).astype(BF16)
            p = dot_nt(top[...], down[c, :]) * slope
            low = p.astype(BF16)
            pg[:, c] = low
            gb[s : s + 1, c] = jnp.sum(low.astype(F32), axis=0, keepdims=True)
            gu[:, c] = dot(n2t[...], low).astype(BF16)
        yp = dot(act[...], down[...])
        gp = dot_nt(pg[...], up[...])
        if s == 0 and first:
            y[...] = yp
            g[...] = gp
        elif s == 0:
            y[...] = y_in[...] + yp
            g[...] = g_in[...] + gp
        else:
            y[...] += yp
            g[...] += gp


def norm_back(grad, gain, hat, scale):
    e = grad * gain
    back = e - jnp.mean(e, axis=-1, keepdims=True)
    return scale * (back - hat * jnp.mean(e * hat, axis=-1, keepdims=True))


def turn_body(res, y, g, top, dbias, gain, out, rg, rl, sums):
    rows, width = res.shape

    def body(at):
        r = res[at, :]
        out[at, :] = (r + y[at, :] + dbias[...]).astype(BF16)
        hat, scale = normalize(r)
        grad = g[at, :]
        full = top[at, :].astype(F32) + norm_back(grad, gain[...], hat, scale)
        rg[at, :] = full
        rl[at, :] = full.astype(BF16)
        return (grad * hat, grad, full)

    for i, total in enumerate(row_loop(rows, width, 3, body)):
        sums[i : i + 1, :] = total


def attn_bwd_body(slots, first, n1, rl, *refs):
    ws, ms, qkvs, atts = (refs[i * slots : (i + 1) * slots] for i in range(4))
    refs = refs[4 * slots :]
    if not first:
        g_in = refs[0]
        refs = refs[1:]
    grads, (g, gb), (da, dqkv) = refs[:slots], refs[slots : slots + 2], refs[slots + 2 :]
    rows = n1.shape[0]
    cols = ws[0].shape[1]
    marks = head_rows(cols)
    for s in range(slots):
        w, qkv, a = ws[s], qkvs[s], grads[s]
        da[...] = dot_nt(rl[...], ms[s][...]).astype(BF16)
        for i in range(rows // WIN):
            at = slice(i * WIN, (i + 1) * WIN)
            q, k, v, d = qkv[0, at, :], qkv[1, at, :], qkv[2, at, :], da[at, :]
            dq = dk = dv = None
            for mark in marks:
                qm, dm = q * mark, d * mark
                (p,) = softmax(dot_nt(qm, k))
                dp = dot_nt(dm, v)
                ds = (p * (dp - jnp.sum(p * dp, axis=-1, keepdims=True))).astype(BF16)
                parts = dot(ds, k * mark), dot_tn(ds, qm), dot_tn(p.astype(BF16), dm)
                if dq is None:
                    dq, dk, dv = parts
                else:
                    dq, dk, dv = dq + parts[0], dk + parts[1], dv + parts[2]
            dqkv[0, at, :] = (dq * SCALE).astype(BF16)
            dqkv[1, at, :] = (dk * SCALE).astype(BF16)
            dqkv[2, at, :] = dv.astype(BF16)
        gp = None
        for j in range(3):
            part = dqkv[j]
            a[j * cols : (j + 1) * cols, :] = dot_tn(part, n1[...]).astype(BF16)
            gj = dot(part, w[j])
            gp = gj if gp is None else gp + gj
            if j != 1:
                gb[s : s + 1, (j // 2) * cols : (j // 2 + 1) * cols] = jnp.sum(
                    part.astype(F32), axis=0, keepdims=True
                )
        a[3 * cols : 4 * cols, :] = dot_tn(atts[s][...], rl[...]).astype(BF16)
        if s == 0 and first:
            g[...] = gp
        elif s == 0:
            g[...] = g_in[...] + gp
        else:
            g[...] += gp


def last_body(tok, msk, vec, gain, g, rg, out, sums):
    rows, width = tok.shape

    def body(at):
        chosen = msk[at, :]
        hat, scale = normalize(mix(chosen, vec[...], tok[at, :]))
        grad = g[at, :]
        full = rg[at, :] + norm_back(grad, gain[...], hat, scale)
        out[at, :] = jnp.where(chosen > 0.5, 0.0, full)
        return (jnp.where(chosen > 0.5, full, 0.0), grad * hat, grad)

    for i, total in enumerate(row_loop(rows, width, 3, body)):
        sums[i : i + 1, :] = total


def swap(v, axis, size, bit):
    return lax.ppermute(v, axis, [(i, i ^ bit) for i in range(size)])


def halves(v, axis, bit):
    n = v.shape[0] // 2
    mine = lax.bitwise_and(lax.div(lax.axis_index(axis), bit), 1)
    keep = lax.dynamic_slice_in_dim(v, mine * n, n)
    give = lax.dynamic_slice_in_dim(v, (1 - mine) * n, n)
    return keep, give


def joined(a, b, axis, bit):
    mine = lax.bitwise_and(lax.div(lax.axis_index(axis), bit), 1)
    return jnp.where(mine == 0, jnp.concatenate((a, b)), jnp.concatenate((b, a)))


def sum_dp(v, size):
    bits = [1 << i for i in range(size.bit_length() - 1)]
    if not bits:
        return v
    for bit in bits[:-1]:
        keep, give = halves(v, "dp", bit)
        v = keep + swap(give.astype(BF16), "dp", size, bit).astype(F32)
    low = v.astype(BF16)
    v = (low.astype(F32) + swap(low, "dp", size, bits[-1]).astype(F32)).astype(BF16)
    for bit in bits[-2::-1]:
        v = joined(v, swap(v, "dp", size, bit), "dp", bit)
    return v.astype(F32)


def per_device(
    n_dp,
    n_tensor,
    tokens,
    mask_bits,
    cotangent,
    mask_vector,
    first_gain,
    first_shift,
    attn_weight,
    attn_bias,
    merge_weight,
    merge_bias,
    second_gain,
    second_shift,
    up_weight,
    up_bias,
    down_weight,
    down_bias,
):
    rows, width = tokens.shape
    cols = attn_weight.shape[2]
    hidden = up_weight.shape[1]
    row = lambda v: v[None, :]
    core = lambda v: swap(v, "tensor", n_tensor, 1)
    across = lambda v: swap(v, "tensor", n_tensor, 2)

    def gather(v):
        far = across(v)
        return [v, core(v), far, core(far)]

    bias_pack = jnp.concatenate(
        (row(up_bias), jnp.pad(attn_bias.reshape(1, 2 * cols), ((0, 0), (0, hidden - 2 * cols))))
    )
    wb = gather(bias_pack)
    wa = gather(jnp.transpose(attn_weight, (1, 2, 0)))
    wm = gather(merge_weight)
    wu = gather(up_weight)
    wd = gather(down_weight)
    up_biases = [b[0:1] for b in wb]
    attn_biases = [b[1:2] for b in wb]

    chosen = (mask_bits == 1).astype(F32)[:, None]
    vec, gain1, shift1 = row(mask_vector), row(first_gain), row(first_shift)
    gain2, shift2 = row(second_gain), row(second_shift)
    big = 2.0 * rows * width

    n1, top, topt, gdb = call(
        prep_body,
        [((rows, width), BF16), ((rows, width), BF16), ((width, rows), BF16), ((1, width), F32)],
        "prep",
        big * 8,
    )(tokens, chosen, cotangent, vec, gain1, shift1)

    def attn_fwd(js):
        outs = []
        for _ in js:
            outs += [((3, rows, cols), BF16), ((rows, cols), BF16)]
        r = call(
            functools.partial(attn_fwd_body, len(js)),
            outs,
            "attn_fwd",
            len(js) * (big * 3 * cols + big * WIN),
        )(n1, jnp.concatenate([attn_biases[j] for j in js]), *[wa[j] for j in js])
        return r[0::2], r[1::2]

    qkv_a, att_a = attn_fwd((0, 1))
    qkv_b, att_b = attn_fwd((2, 3))
    qkv, att = (*qkv_a, *qkv_b), (*att_a, *att_b)

    res, n2, n2t = call(
        functools.partial(mid_body, 4),
        [((rows, width), F32), ((rows, width), BF16), ((width, rows), BF16)],
        "mid",
        big * width,
    )(tokens, chosen, vec, row(merge_bias), gain2, shift2, *att, *wm)

    def ffn(js, prev):
        outs = [((width, hidden), BF16)] * (2 * len(js))
        outs += [((rows, width), F32)] * 2 + [((len(js), hidden), F32)]
        body = functools.partial(ffn_body, len(js), not prev)
        shapes = tuple(jax.ShapeDtypeStruct(s, d) for s, d in outs)
        args = (n2, n2t, top, topt, jnp.concatenate([up_biases[j] for j in js]))
        args += tuple(wu[j] for j in js) + tuple(wd[j] for j in js) + tuple(prev)
        r = pl.pallas_call(
            body,
            out_shape=shapes,
            in_specs=[pl.BlockSpec(memory_space=pltpu.VMEM)] * len(args),
            out_specs=tuple(pl.BlockSpec(memory_space=pltpu.VMEM) for _ in shapes),
            scratch_shapes=[pltpu.VMEM((rows, hidden), BF16)] * 2,
            compiler_params=pltpu.CompilerParams(vmem_limit_bytes=24 << 20),
            cost_estimate=pl.CostEstimate(
                flops=int(6 * big * hidden * len(js)), bytes_accessed=8 << 20, transcendentals=0
            ),
            name="ffn",
        )(*args)
        n = 2 * len(js)
        return r[0:n:2], r[1:n:2], r[n], r[n + 1], r[n + 2]

    gd_a, gu_a, y, g2, gb_a = ffn((0, 1), ())
    gd_b, gu_b, y, g2, gb_b = ffn((2, 3), (y, g2))
    gd, gu = (*gd_a, *gd_b), (*gu_a, *gu_b)

    layer_out, res_grad, res_low, sums2 = call(
        turn_body,
        [((rows, width), BF16), ((rows, width), F32), ((rows, width), BF16), ((3, width), F32)],
        "turn",
        big * 16,
    )(res, y, g2, top, row(down_bias), gain2)

    def attn_bwd(js, prev):
        outs = [((4 * cols, width), BF16)] * len(js)
        outs += [((rows, width), F32), ((len(js), 2 * cols), F32)]
        args = (n1, res_low, *[wa[j] for j in js], *[wm[j] for j in js])
        args += (*[qkv[j] for j in js], *[att[j] for j in js], *prev)
        shapes = tuple(jax.ShapeDtypeStruct(s, d) for s, d in outs)
        return pl.pallas_call(
            functools.partial(attn_bwd_body, len(js), not prev),
            out_shape=shapes,
            in_specs=[pl.BlockSpec(memory_space=pltpu.VMEM)] * len(args),
            out_specs=tuple(pl.BlockSpec(memory_space=pltpu.VMEM) for _ in shapes),
            scratch_shapes=[pltpu.VMEM((rows, cols), BF16), pltpu.VMEM((3, rows, cols), BF16)],
            compiler_params=pltpu.CompilerParams(vmem_limit_bytes=24 << 20),
            cost_estimate=pl.CostEstimate(
                flops=int(len(js) * (8 * big * cols + 3 * big * WIN)),
                bytes_accessed=8 << 20,
                transcendentals=0,
            ),
            name="attn_bwd",
        )(*args)

    ga1, ga3, g1, ab_a = attn_bwd((1, 3), ())
    ga2, ga0, g1, ab_b = attn_bwd((2, 0), (g1,))

    grad_tokens, sums1 = call(
        last_body, [((rows, width), F32), ((3, width), F32)], "last", big * 16
    )(tokens, chosen, vec, gain1, g1, res_grad)

    def reduce(p0, p1, p2, p3):
        far = (p2.astype(F32) + core(p3).astype(F32)).astype(BF16)
        near = p0.astype(F32) + core(p1).astype(F32)
        return sum_dp(near + across(far).astype(F32), n_dp)

    sum_d = reduce(*gd)
    sum_u = reduce(*gu)
    sum_a = reduce(ga0, ga1, ga2, ga3)

    pad = ((0, 0), (0, width - 2 * cols))
    small = {
        0: (gb_a[0:1], ab_b[1:2]),
        1: (gb_a[1:2], ab_a[0:1]),
        2: (gb_b[0:1], ab_b[0:1]),
        3: (gb_b[1:2], ab_a[1:2]),
    }
    packs = [jnp.concatenate((u, jnp.pad(a, pad))) for u, a in (small[j] for j in range(4))]
    vecs = jnp.concatenate((sums1, sums2, gdb))
    near = jnp.concatenate((vecs, packs[0], packs[2]))
    near = near + core(jnp.concatenate((vecs, packs[1], packs[3])))
    nv = vecs.shape[0]
    mine = near[: nv + 2]
    mine = mine + across(jnp.concatenate((near[:nv], near[nv + 2 :])))
    for i in range(n_dp.bit_length() - 1):
        mine = mine + swap(mine, "dp", n_dp, 1 << i)

    grad_attn = jnp.transpose(sum_a[: 3 * cols].reshape(3, cols, width), (2, 0, 1))
    return (
        layer_out,
        grad_tokens,
        mine[0],
        mine[1],
        mine[2],
        grad_attn,
        mine[nv + 1, : 2 * cols].reshape(2, cols),
        sum_a[3 * cols :],
        mine[5],
        mine[3],
        mine[4],
        sum_u,
        mine[nv],
        sum_d.T,
        mine[6],
    )


def solution(mesh):
    split = P(("dp", "tensor"), None)
    return jax.shard_map(
        functools.partial(per_device, mesh.shape["dp"], mesh.shape["tensor"]),
        mesh=mesh,
        in_specs=(
            split,
            P(("dp", "tensor")),
            split,
            P(),
            P(),
            P(),
            P(None, None, "tensor"),
            P(None, "tensor"),
            P("tensor", None),
            P(),
            P(),
            P(),
            P(None, "tensor"),
            P("tensor"),
            P("tensor", None),
            P(),
        ),
        out_specs=(
            split,
            split,
            P(),
            P(),
            P(),
            P(None, None, "tensor"),
            P(None, "tensor"),
            P("tensor", None),
            P(),
            P(),
            P(),
            P(None, "tensor"),
            P("tensor"),
            P("tensor", None),
            P(),
        ),
        check_vma=False,
    )
```

```python
import functools

import jax
import jax.numpy as jnp
from jax import lax
from jax.experimental import pallas as pl
from jax.experimental.pallas import tpu as pltpu
from jax.sharding import PartitionSpec as P

HEAD = 64
WIN = 256
EPS = 1e-06
SCALE = HEAD**-0.5
ROWS = 64
F32 = jnp.float32
BF16 = jnp.bfloat16


def dot(a, b):
    return lax.dot_general(a, b, (((1,), (0,)), ((), ())), preferred_element_type=F32)


def dot_nt(a, b):
    return lax.dot_general(a, b, (((1,), (1,)), ((), ())), preferred_element_type=F32)


def dot_tn(a, b):
    return lax.dot_general(a, b, (((0,), (0,)), ((), ())), preferred_element_type=F32)


def call(body, args, outs, name, us, scratch=(), vmem=16, after=()):
    shapes = tuple(jax.ShapeDtypeStruct(s, d) for s, d in outs)
    n, m = len(args), len(after)

    def wrapped(*refs):
        body(*refs[:n], *refs[n + m :])

    moved = sum(a.size * a.dtype.itemsize for a in args)
    return pl.pallas_call(
        wrapped,
        out_shape=shapes,
        in_specs=[pl.BlockSpec(memory_space=pltpu.VMEM)] * n
        + [pl.BlockSpec(memory_space=pl.ANY)] * m,
        out_specs=tuple(pl.BlockSpec(memory_space=pltpu.VMEM) for _ in shapes),
        scratch_shapes=list(scratch),
        compiler_params=pltpu.CompilerParams(vmem_limit_bytes=vmem << 20),
        cost_estimate=pl.CostEstimate(
            flops=int(us * 1.15e9), bytes_accessed=moved, transcendentals=0
        ),
        name=name,
    )(*args, *after)


def row_loop(rows, width, sums, body):
    def step(i, carry):
        at = pl.ds(pl.multiple_of(i * ROWS, ROWS), ROWS)
        parts = body(at)
        return tuple(
            c + jnp.sum(p.reshape(ROWS // 8, 8, width), axis=0) for c, p in zip(carry, parts)
        )

    zero = tuple(jnp.zeros((8, width), F32) for _ in range(sums))
    done = lax.fori_loop(0, rows // ROWS, step, zero)
    return [jnp.sum(c, axis=0, keepdims=True) for c in done]


def normalize(v):
    centre = v - jnp.mean(v, axis=-1, keepdims=True)
    scale = lax.rsqrt(jnp.mean(centre * centre, axis=-1, keepdims=True) + EPS)
    return centre * scale, scale


def mix(chosen, vector, tokens):
    return jnp.where(chosen > 0.5, vector, tokens.astype(F32))


def prep_body(tok, msk, cot, vec, gain, shift, n1, top, topt, gdb):
    rows, width = tok.shape

    def body(at):
        chosen = msk[at, :]
        hat, _ = normalize(mix(chosen, vec[...], tok[at, :]))
        n1[at, :] = (hat * gain[...] + shift[...]).astype(BF16)
        grad = jnp.where(chosen > 0.5, cot[at, :].astype(F32), 0.0)
        top[at, :] = grad.astype(BF16)
        return (grad,)

    (total,) = row_loop(rows, width, 1, body)
    gdb[...] = total
    topt[...] = top[...].T


def head_rows(cols):
    lane = lax.broadcasted_iota(jnp.int32, (1, cols), 1)
    return [
        ((lane >= h * HEAD) & (lane < (h + 1) * HEAD)).astype(F32).astype(BF16)
        for h in range(cols // HEAD)
    ]


def attn_fwd_body(slots, n1, bias, *refs):
    ins, outs = refs[:slots], refs[slots:]
    rows = n1.shape[0]
    cols = ins[0].shape[1]
    marks = head_rows(cols)
    for s in range(slots):
        w, qkv, att = ins[s], outs[2 * s], outs[2 * s + 1]
        qkv[0] = (dot_nt(n1[...], w[0]) + bias[s : s + 1, :cols]).astype(BF16)
        qkv[1] = dot_nt(n1[...], w[1]).astype(BF16)
        qkv[2] = (dot_nt(n1[...], w[2]) + bias[s : s + 1, cols : 2 * cols]).astype(BF16)
        for i in range(rows // WIN):
            at = slice(i * WIN, (i + 1) * WIN)
            q, k, v = qkv[0, at, :], qkv[1, at, :], qkv[2, at, :]
            out = None
            for mark in marks:
                p = softmax(dot_nt(q * mark, k))[0].astype(BF16)
                part = dot(p, v * mark)
                out = part if out is None else out + part
            att[at, :] = out.astype(BF16)


def softmax(raw):
    peak = jnp.max(raw, axis=-1, keepdims=True)
    e = jnp.exp((raw - peak) * SCALE)
    return (e * (1.0 / jnp.sum(e, axis=-1, keepdims=True)),)


def mid_body(slots, tok, msk, vec, mbias, gain, shift, *refs):
    atts, merges = refs[:slots], refs[slots : 2 * slots]
    res, n2, n2t = refs[2 * slots :]
    rows, width = tok.shape
    total = dot(atts[0][...], merges[0][...])
    for s in range(1, slots):
        total = total + dot(atts[s][...], merges[s][...])
    res[...] = total

    def body(at):
        r = mix(msk[at, :], vec[...], tok[at, :]) + res[at, :] + mbias[...]
        res[at, :] = r
        hat, _ = normalize(r)
        n2[at, :] = (hat * gain[...] + shift[...]).astype(BF16)
        return ()

    row_loop(rows, width, 0, body)
    n2t[...] = n2[...].T


GELU_C = 0.7978845608028654
GELU_A = 0.044715


def ffn_up_body(slots, n2, topt, bias, *refs):
    ups, outs = refs[:slots], refs[slots:]
    hidden = ups[0].shape[1]
    tile = 256
    for s in range(slots):
        act, slope, gd = outs[3 * s : 3 * s + 3]
        for t in range(hidden // tile):
            c = slice(t * tile, (t + 1) * tile)
            pre = dot(n2[...], ups[s][:, c]) + bias[s : s + 1, c]
            sq = pre * pre
            th = jnp.tanh(GELU_C * (pre + GELU_A * (sq * pre)))
            half = 0.5 * (1.0 + th)
            a = (pre * half).astype(BF16)
            rise = half + (0.5 * GELU_C) * pre * (1.0 - th * th) * (1.0 + (3.0 * GELU_A) * sq)
            act[:, c] = a
            slope[:, c] = rise.astype(BF16)
            gd[:, c] = dot(topt[...], a).astype(BF16)


def ffn_back_body(slots, first, n2t, top, *refs):
    ups, downs, acts, slopes = (refs[i * slots : (i + 1) * slots] for i in range(4))
    refs = refs[4 * slots :]
    if not first:
        y_in, g_in = refs[:2]
        refs = refs[2:]
    gus, (y, g, gb, pg) = refs[:slots], refs[slots:]
    hidden = ups[0].shape[1]
    tile = 256
    for s in range(slots):
        up, down = ups[s], downs[s]
        for t in range(hidden // tile):
            c = slice(t * tile, (t + 1) * tile)
            p = dot_nt(top[...], down[c, :]) * slopes[s][:, c].astype(F32)
            low = p.astype(BF16)
            pg[:, c] = low
            gb[s : s + 1, c] = jnp.sum(low.astype(F32), axis=0, keepdims=True)
            gus[s][:, c] = dot(n2t[...], low).astype(BF16)
        yp = dot(acts[s][...], down[...])
        gp = dot_nt(pg[...], up[...])
        if s == 0 and first:
            y[...] = yp
            g[...] = gp
        elif s == 0:
            y[...] = y_in[...] + yp
            g[...] = g_in[...] + gp
        else:
            y[...] += yp
            g[...] += gp


def norm_back(grad, gain, hat, scale):
    e = grad * gain
    back = e - jnp.mean(e, axis=-1, keepdims=True)
    return scale * (back - hat * jnp.mean(e * hat, axis=-1, keepdims=True))


def turn_body(res, y, g, top, dbias, gain, out, rg, rl, sums):
    rows, width = res.shape

    def body(at):
        r = res[at, :]
        out[at, :] = (r + y[at, :] + dbias[...]).astype(BF16)
        hat, scale = normalize(r)
        grad = g[at, :]
        full = top[at, :].astype(F32) + norm_back(grad, gain[...], hat, scale)
        rg[at, :] = full
        rl[at, :] = full.astype(BF16)
        return (grad * hat, grad, full)

    for i, total in enumerate(row_loop(rows, width, 3, body)):
        sums[i : i + 1, :] = total


def attn_bwd_body(slots, first, n1, rl, *refs):
    ws, ms, qkvs, atts = (refs[i * slots : (i + 1) * slots] for i in range(4))
    refs = refs[4 * slots :]
    if not first:
        g_in = refs[0]
        refs = refs[1:]
    grads, (g, gb), (da, dqkv) = refs[:slots], refs[slots : slots + 2], refs[slots + 2 :]
    rows = n1.shape[0]
    cols = ws[0].shape[1]
    marks = head_rows(cols)
    for s in range(slots):
        w, qkv, a = ws[s], qkvs[s], grads[s]
        da[...] = dot_nt(rl[...], ms[s][...]).astype(BF16)
        for i in range(rows // WIN):
            at = slice(i * WIN, (i + 1) * WIN)
            q, k, v, d = qkv[0, at, :], qkv[1, at, :], qkv[2, at, :], da[at, :]
            dq = dk = dv = None
            for mark in marks:
                qm, dm = q * mark, d * mark
                (p,) = softmax(dot_nt(qm, k))
                dp = dot_nt(dm, v)
                ds = (p * (dp - jnp.sum(p * dp, axis=-1, keepdims=True))).astype(BF16)
                parts = dot(ds, k * mark), dot_tn(ds, qm), dot_tn(p.astype(BF16), dm)
                if dq is None:
                    dq, dk, dv = parts
                else:
                    dq, dk, dv = dq + parts[0], dk + parts[1], dv + parts[2]
            dqkv[0, at, :] = (dq * SCALE).astype(BF16)
            dqkv[1, at, :] = (dk * SCALE).astype(BF16)
            dqkv[2, at, :] = dv.astype(BF16)
        gp = None
        for j in range(3):
            part = dqkv[j]
            a[j * cols : (j + 1) * cols, :] = dot_tn(part, n1[...]).astype(BF16)
            gj = dot(part, w[j])
            gp = gj if gp is None else gp + gj
            if j != 1:
                gb[s : s + 1, (j // 2) * cols : (j // 2 + 1) * cols] = jnp.sum(
                    part.astype(F32), axis=0, keepdims=True
                )
        a[3 * cols : 4 * cols, :] = dot_tn(atts[s][...], rl[...]).astype(BF16)
        if s == 0 and first:
            g[...] = gp
        elif s == 0:
            g[...] = g_in[...] + gp
        else:
            g[...] += gp


def last_body(tok, msk, vec, gain, g, rg, out, sums):
    rows, width = tok.shape

    def body(at):
        chosen = msk[at, :]
        hat, scale = normalize(mix(chosen, vec[...], tok[at, :]))
        grad = g[at, :]
        full = rg[at, :] + norm_back(grad, gain[...], hat, scale)
        out[at, :] = jnp.where(chosen > 0.5, 0.0, full)
        return (jnp.where(chosen > 0.5, full, 0.0), grad * hat, grad)

    for i, total in enumerate(row_loop(rows, width, 3, body)):
        sums[i : i + 1, :] = total


def cut_body(pick, *refs):
    n = (len(refs) - 1) // 2
    ins, outs, sem = refs[:n], refs[n : 2 * n], refs[-1]
    copies = []
    for i in range(n):
        half = outs[i].shape[0]
        at = pl.ds(pl.multiple_of(pick[0] * half, half), half)
        copies.append(pltpu.make_async_copy(ins[i].at[at, :], outs[i], sem.at[i]))
    for c in copies:
        c.start()
    for c in copies:
        c.wait()


def cut(pick, *arrays):
    return pl.pallas_call(
        cut_body,
        out_shape=tuple(
            jax.ShapeDtypeStruct((a.shape[0] // 2, a.shape[1]), a.dtype) for a in arrays
        ),
        in_specs=[pl.BlockSpec(memory_space=pltpu.SMEM)]
        + [pl.BlockSpec(memory_space=pl.ANY)] * len(arrays),
        out_specs=tuple(pl.BlockSpec(memory_space=pltpu.VMEM) for _ in arrays),
        scratch_shapes=[pltpu.SemaphoreType.DMA((len(arrays),))],
        compiler_params=pltpu.CompilerParams(vmem_limit_bytes=1 << 20),
        name="cut",
    )(pick.astype(jnp.int32).reshape(1), *arrays)


def place_body(turned, offs, w, r1, r2, r3, *refs):
    outs, target = refs[:-1], refs[-1]
    block = w.shape[0]
    i = 0
    for part in (w, r1, r2, r3):
        for k in range(part.shape[0] // block):
            at = pl.ds(pl.multiple_of(offs[i], block), block)
            target[at, :] = part[k * block : (k + 1) * block, :].astype(F32)
            i += 1
    start = 0
    for out in outs:
        if turned:
            out[...] = target[...].T
        else:
            out[...] = target[start : start + out.shape[0], :]
            start += out.shape[0]


class Links:
    def __init__(self, n_dp, n_tensor):
        self.n_dp, self.n_tensor = n_dp, n_tensor
        d, t = lax.axis_index("dp"), lax.axis_index("tensor")
        self.core = lax.rem(t, 2)
        self.bit = lambda i: lax.rem(lax.div(d, 1 << i), 2)
        self.mixed = lax.rem(self.bit(0) + self.bit(1), 2)

    def swap(self, v, *moves):
        moves = moves * (2 // len(moves))
        pairs = []
        for d in range(self.n_dp):
            for t in range(self.n_tensor):
                fd, ft = moves[t % 2]
                pairs.append((d * self.n_tensor + t, (d ^ fd) * self.n_tensor + (t ^ ft)))
        return lax.ppermute(v, ("dp", "tensor"), pairs)

    def split(self, v, i):
        n = v.shape[0] // 2
        mine = self.bit(i)
        take = lambda k: lax.dynamic_slice_in_dim(v, k * n, n)
        return take(mine), take(1 - mine)


CORE, ACROSS = (0, 1), (0, 2)
DP0, DP1, DP2 = (1, 0), (2, 0), (4, 0)


def gather(links, v, half):
    near = links.swap(v, CORE)
    if half is None:
        far = links.swap(v, ACROSS)
    else:
        half = links.swap(half, ACROSS)
        rest = links.swap(half, DP0, DP1)
        far = jnp.where(
            links.mixed == 0, jnp.concatenate((half, rest)), jnp.concatenate((rest, half))
        )
    return [v, near, far, links.swap(far, CORE)]


class Reduce:
    def __init__(self, links, p0, p1, p2, p3):
        self.links = links
        self.near = (p0, links.swap(p1, CORE))
        self.far = (p2, links.swap(p3, CORE))
        self.rows = p0.shape[0]

    def begin(self, b00, b01, b10, b11, first, second):
        lead = self.links.core == 0
        self.give = jnp.concatenate(
            (jnp.where(lead, b10, b01).astype(BF16), b11.astype(BF16))
        )
        self.keep = jnp.where(lead, b01, b10).astype(F32)
        self.own = b00.astype(F32)
        self.got = self.links.swap(self.give, first, second)
        return self.give

    def turn(self, first, second):
        n = self.own.shape[0]
        got = self.got.astype(F32)
        self.own = self.own + got[:n]
        self.give = (self.keep + got[n:]).astype(BF16)
        self.got = self.links.swap(self.give, second, first)
        return self.give

    def stage1(self):
        s = self.links
        near, far = (a.astype(F32) + b.astype(F32) for a, b in (self.near, self.far))
        n0, n1 = s.split(near, 0)
        f0, f1 = s.split(far, 0)
        return self.begin(n0, n1, f0, f1, ACROSS, DP0)

    def stage2(self):
        return self.turn(ACROSS, DP0)

    def stage3(self):
        s = self.links
        a, b = s.split(self.own + self.got.astype(F32), 1)
        a0, a1 = s.split(a, 2)
        b0, b1 = s.split(b, 2)
        return self.begin(a0, a1, b0, b1, DP1, DP2)

    def stage4(self):
        return self.turn(DP1, DP2)

    def spread1(self):
        v = self.own + self.got.astype(F32)
        i = 3
        while (1 << i) < self.links.n_dp:
            low = v.astype(BF16)
            v = low.astype(F32) + self.links.swap(low, (1 << i, 0)).astype(F32)
            i += 1
        self.w = v.astype(BF16)
        self.r1 = self.links.swap(self.w, DP2)
        return self.w

    def spread2(self):
        self.w1 = jnp.concatenate((self.w, self.r1))
        self.r2 = self.links.swap(self.w1, DP0, DP1)
        return self.w1

    def spread3(self):
        self.w2 = jnp.concatenate((self.w1, self.r2))
        self.r3 = self.links.swap(self.w2, DP1, DP0)
        return self.w2

    def place(self, turned=False, sizes=None, after=()):
        s = self.links
        block = self.rows // 8
        i = jnp.arange(8)
        low, mid, high = i % 2, (i // 2) % 2, i // 4
        h0 = jnp.where(s.core == 0, mid, high)
        h1 = jnp.where(s.core == 0, high, mid)
        flip = lambda h, k: lax.rem(h + s.bit(k), 2)
        offs = (flip(h0, 0) * 4 + flip(h1, 1) * 2 + flip(low, 2)) * block
        width = self.w.shape[1]
        sizes = sizes or (self.rows,)
        shapes = [(width, self.rows)] if turned else [(n, width) for n in sizes]
        m = len(after)
        return pl.pallas_call(
            lambda *refs: place_body(turned, *refs[:5], *refs[5 + m :]),
            out_shape=[jax.ShapeDtypeStruct(shape, F32) for shape in shapes],
            in_specs=[pl.BlockSpec(memory_space=pltpu.SMEM)]
            + [pl.BlockSpec(memory_space=pltpu.VMEM)] * 4
            + [pl.BlockSpec(memory_space=pl.ANY)] * m,
            out_specs=[pl.BlockSpec(memory_space=pltpu.VMEM) for _ in shapes],
            scratch_shapes=[pltpu.VMEM((self.rows, width), F32)],
            compiler_params=pltpu.CompilerParams(vmem_limit_bytes=8 << 20),
            name="place",
        )(offs.astype(jnp.int32), self.w, self.r1, self.r2, self.r3, *after)


class PlainReduce(Reduce):
    def stage1(self):
        near, far = (a.astype(F32) + b.astype(F32) for a, b in (self.near, self.far))
        total = near + self.links.swap(far.astype(BF16), ACROSS).astype(F32)
        self.total = lax.psum(total, "dp")
        return self.total

    def skip(self):
        return self.total

    stage2 = stage3 = stage4 = spread1 = spread2 = spread3 = skip

    def place(self, turned=False, sizes=None, after=()):
        if turned:
            return [self.total.T]
        out, at = [], 0
        for n in sizes or (self.rows,):
            out.append(self.total[at : at + n])
            at += n
        return out


def per_device(
    n_dp,
    n_tensor,
    tokens,
    mask_bits,
    cotangent,
    mask_vector,
    first_gain,
    first_shift,
    attn_weight,
    attn_bias,
    merge_weight,
    merge_bias,
    second_gain,
    second_shift,
    up_weight,
    up_bias,
    down_weight,
    down_bias,
):
    rows, width = tokens.shape
    cols = attn_weight.shape[2]
    hidden = up_weight.shape[1]
    row = lambda v: v[None, :]
    links = Links(n_dp, n_tensor)
    power = n_dp >= 8 and n_dp & (n_dp - 1) == 0
    reducer = Reduce if power else PlainReduce

    bias_pack = jnp.concatenate(
        (row(up_bias), jnp.pad(attn_bias.reshape(1, 2 * cols), ((0, 0), (0, hidden - 2 * cols))))
    )
    far = links.swap(bias_pack, ACROSS)
    wb = [bias_pack, links.swap(bias_pack, CORE), far, links.swap(far, CORE)]
    flat = jnp.transpose(attn_weight, (1, 2, 0)).reshape(3 * cols, width)
    weights = (flat, merge_weight, up_weight, down_weight)
    cuts = cut(links.mixed, *weights) if n_dp % 4 == 0 else (None,) * 4
    wa, wm, wu, wd = (gather(links, w, c) for w, c in zip(weights, cuts))
    wa = [w.reshape(3, cols, width) for w in wa]
    up_biases = [b[0:1] for b in wb]
    attn_biases = [b[1:2] for b in wb]

    chosen = (mask_bits == 1).astype(F32)[:, None]
    vec, gain1, shift1 = row(mask_vector), row(first_gain), row(first_shift)
    gain2, shift2 = row(second_gain), row(second_shift)
    wide, tall, low = ((rows, width), F32), ((width, rows), BF16), ((rows, width), BF16)

    n1, top, topt, gdb = call(
        prep_body,
        (tokens, chosen, cotangent, vec, gain1, shift1),
        [low, low, tall, ((1, width), F32)],
        "prep",
        4,
    )

    def attn_fwd(js):
        r = call(
            functools.partial(attn_fwd_body, len(js)),
            (n1, jnp.concatenate([attn_biases[j] for j in js]), *[wa[j] for j in js]),
            [((3, rows, cols), BF16), ((rows, cols), BF16)] * len(js),
            "attn_fwd",
            3 * len(js),
        )
        return r[0::2], r[1::2]

    qkv_a, att_a = attn_fwd((0, 1))
    qkv_b, att_b = attn_fwd((2, 3))
    qkv, att = (*qkv_a, *qkv_b), (*att_a, *att_b)

    res, n2, n2t = call(
        functools.partial(mid_body, 4),
        (tokens, chosen, vec, row(merge_bias), gain2, shift2, *att, *wm),
        [wide, low, tall],
        "mid",
        5,
    )

    def ffn_up(js):
        r = call(
            functools.partial(ffn_up_body, len(js)),
            (n2, topt, jnp.concatenate([up_biases[j] for j in js]), *[wu[j] for j in js]),
            [((rows, hidden), BF16), ((rows, hidden), BF16), ((width, hidden), BF16)] * len(js),
            "ffn_up",
            2.75 * len(js),
        )
        return r[0::3], r[1::3], r[2::3]

    act_a, slope_a, gd_a = ffn_up((0, 1))
    act_b, slope_b, gd_b = ffn_up((2, 3))
    act, slope, gd = (*act_a, *act_b), (*slope_a, *slope_b), (*gd_a, *gd_b)
    red_d = reducer(links, *gd)

    def ffn_back(js, prev, after):
        args = (n2t, top)
        for group in (wu, wd, act, slope):
            args += tuple(group[j] for j in js)
        n = len(js)
        r = call(
            functools.partial(ffn_back_body, n, not prev),
            (*args, *prev),
            [((width, hidden), BF16)] * n + [wide, wide, ((n, hidden), F32)],
            "ffn_back",
            4.5 * n,
            scratch=[pltpu.VMEM((rows, hidden), BF16)],
            after=after,
        )
        return r[:n], r[n], r[n + 1], r[n + 2]

    gu_a, y, g2, gb_a = ffn_back((0, 1), (), ())
    gu_b, y, g2, gb_b = ffn_back((2, 3), (y, g2), (red_d.stage1(),))
    red_u = reducer(links, *gu_a, *gu_b)

    layer_out, res_grad, res_low, sums2 = call(
        turn_body,
        (res, y, g2, top, row(down_bias), gain2),
        [low, wide, low, ((3, width), F32)],
        "turn",
        4.5,
    )

    def attn_bwd(js, prev, after):
        args = (n1, res_low)
        for group in (wa, wm, qkv, att):
            args += tuple(group[j] for j in js)
        n = len(js)
        return call(
            functools.partial(attn_bwd_body, n, not prev),
            (*args, *prev),
            [((4 * cols, width), BF16)] * n + [wide, ((n, 2 * cols), F32)],
            "attn_bwd",
            7 * n,
            scratch=[pltpu.VMEM((rows, cols), BF16), pltpu.VMEM((3, rows, cols), BF16)],
            after=after,
        )

    ga1, ga3, g1, ab_a = attn_bwd((1, 3), (), (red_d.stage2(), red_u.stage1()))
    ga2, ga0, g1, ab_b = attn_bwd((2, 0), (g1,), (red_d.stage3(), red_u.stage2()))
    red_a = reducer(links, ga0, ga1, ga2, ga3)

    grad_tokens, sums1 = call(
        last_body,
        (tokens, chosen, vec, gain1, g1, res_grad),
        [wide, ((3, width), F32)],
        "last",
        6,
        after=(red_d.stage4(), red_u.stage3(), red_a.stage1()),
    )
    red_d.spread1()
    red_u.stage4()
    red_a.stage2()
    red_a.stage3()
    red_a.stage4()
    for red in (red_u, red_a):
        red.spread1()
    for red in (red_d, red_u, red_a):
        red.spread2()
        red.spread3()

    pad = ((0, 0), (0, width - 2 * cols))
    small = {
        0: (gb_a[0:1], ab_b[1:2]),
        1: (gb_a[1:2], ab_a[0:1]),
        2: (gb_b[0:1], ab_b[0:1]),
        3: (gb_b[1:2], ab_a[1:2]),
    }
    packs = [jnp.concatenate((u, jnp.pad(a, pad))) for u, a in (small[j] for j in range(4))]
    vecs = jnp.concatenate((sums1, sums2, gdb))
    near = jnp.concatenate((vecs, packs[0], packs[2]))
    near = near + links.swap(jnp.concatenate((vecs, packs[1], packs[3])), CORE)
    nv = vecs.shape[0]
    mine = near[: nv + 2]
    mine = mine + links.swap(jnp.concatenate((near[:nv], near[nv + 2 :])), ACROSS)
    if power:
        i = 0
        while (1 << i) < n_dp:
            mine = mine + links.swap(mine, (1 << i, 0))
            i += 1
    else:
        mine = lax.psum(mine, "dp")

    (sum_d,) = red_d.place(turned=True)
    (sum_u,) = red_u.place()
    sum_a, sum_m = red_a.place(sizes=(3 * cols, cols), after=(mine,))
    grad_attn = jnp.transpose(sum_a.reshape(3, cols, width), (2, 0, 1))
    return (
        layer_out,
        grad_tokens,
        mine[0],
        mine[1],
        mine[2],
        grad_attn,
        mine[nv + 1, : 2 * cols].reshape(2, cols),
        sum_m,
        mine[5],
        mine[3],
        mine[4],
        sum_u,
        mine[nv],
        sum_d,
        mine[6],
    )


def solution(mesh):
    split = P(("dp", "tensor"), None)
    return jax.shard_map(
        functools.partial(per_device, mesh.shape["dp"], mesh.shape["tensor"]),
        mesh=mesh,
        in_specs=(
            split,
            P(("dp", "tensor")),
            split,
            P(),
            P(),
            P(),
            P(None, None, "tensor"),
            P(None, "tensor"),
            P("tensor", None),
            P(),
            P(),
            P(),
            P(None, "tensor"),
            P("tensor"),
            P("tensor", None),
            P(),
        ),
        out_specs=(
            split,
            split,
            P(),
            P(),
            P(),
            P(None, None, "tensor"),
            P(None, "tensor"),
            P("tensor", None),
            P(),
            P(),
            P(),
            P(None, "tensor"),
            P("tensor"),
            P("tensor", None),
            P(),
        ),
        check_vma=False,
    )
```

```python
import functools

import jax
import jax.numpy as jnp
from jax import lax
from jax.experimental import pallas as pl
from jax.experimental.pallas import tpu as pltpu
from jax.sharding import PartitionSpec as P

HEAD = 64
WIN = 256
EPS = 1e-06
SCALE = HEAD**-0.5
ROWS = 64
F32 = jnp.float32
BF16 = jnp.bfloat16


def dot(a, b):
    return lax.dot_general(a, b, (((1,), (0,)), ((), ())), preferred_element_type=F32)


def dot_nt(a, b):
    return lax.dot_general(a, b, (((1,), (1,)), ((), ())), preferred_element_type=F32)


def dot_tn(a, b):
    return lax.dot_general(a, b, (((0,), (0,)), ((), ())), preferred_element_type=F32)


class Stack:
    space = pltpu.VMEM

    def __init__(self, *parts, turn=None):
        self.parts, self.turn = parts, turn
        self.shape = (sum(p.shape[0] for p in parts), *parts[0].shape[1:])
        self.dtype = parts[0].dtype


class Late(Stack):
    space = pl.ANY


class Raw:
    def __init__(self, array):
        self.array = array


class Tile:
    def __init__(self, ref, copies=(), fills=(), out=False):
        self.ref, self.copies, self.fills, self.out, self.sent = ref, copies, fills, out, False
        self.shape, self.dtype = ref.shape, ref.dtype

    def start(self):
        for c in self.copies:
            c.start()
        self.sent = True

    def wait(self):
        for c in self.copies:
            c.wait()
        for at, part in self.fills:
            self.ref[at, :] = part[...]
        self.copies = self.fills = ()
        return self.ref

    def ready(self):
        return self.ref if self.out else self.wait()

    def __getitem__(self, at):
        return self.ready()[at]

    def __setitem__(self, at, value):
        self.ref[at] = value


class Position:
    def __init__(self):
        self.dp = lax.axis_index("dp")
        self.core = lax.rem(lax.axis_index("tensor"), 2)

    def bit(self, i):
        return lax.rem(lax.div(self.dp, 1 << i), 2)

    def mixed(self):
        return lax.rem(self.bit(0) + self.bit(1), 2)


class Early:
    def __init__(self, shape, dtype):
        self.array = (shape, dtype)


def size(shape, dtype):
    shape = (*shape[:-1], -(-shape[-1] // 128) * 128)
    return functools.reduce(lambda a, b: a * b, shape) * jnp.dtype(dtype).itemsize


class Chain:
    def __init__(self):
        self.last = None

    def __call__(self, body, args, outs, name, us, scratch=(), stack=7):
        arrays, in_specs, bufs, n_sem = [], [], [], 0
        spec = lambda space: pl.BlockSpec(memory_space=space)
        for a in args:
            if isinstance(a, Stack):
                arrays += a.parts
                in_specs += [spec(a.space)] * len(a.parts)
                bufs.append((a.shape, a.dtype))
                n_sem += isinstance(a, Late)
            else:
                raw = isinstance(a, Raw)
                arrays.append(a.array if raw else a)
                in_specs.append(spec(pltpu.HBM if raw else pltpu.VMEM))
        shapes, out_specs = [], []
        for o in outs:
            raw, early = isinstance(o, Raw), isinstance(o, Early)
            o = o.array if raw or early else o
            shapes.append(jax.ShapeDtypeStruct(*o))
            out_specs.append(spec(pl.ANY if raw or early else pltpu.VMEM))
            if early:
                bufs.append(o)
                n_sem += 1
        order = () if self.last is None else (self.last,)
        n_in, n_out, n_buf = len(arrays), len(shapes), len(bufs)

        def kernel(*refs):
            ins = list(refs[:n_in])
            refs = refs[n_in + len(order) :]
            results, refs = list(refs[:n_out]), refs[n_out:]
            spare, refs = list(refs[:n_buf]), refs[n_buf:]
            sems = refs[0] if n_sem else None
            extra = refs[1:] if n_sem else refs
            used = iter(range(n_sem))
            tiles = []
            for a in args:
                if isinstance(a, Stack):
                    buf, at, copies, fills = spare.pop(0), 0, [], []
                    if isinstance(a, Late):
                        copies.append(pltpu.make_async_copy(ins.pop(0), buf, sems.at[next(used)]))
                    else:
                        for part in a.parts:
                            n, row = part.shape[0], at
                            if a.turn is not None:
                                row = pl.multiple_of(jnp.where(a.turn() == 0, at, n - at), n)
                            fills.append((pl.ds(row, n), ins.pop(0)))
                            at += n
                    tiles.append(Tile(buf, copies, fills))
                    tiles[-1].start()
                else:
                    tiles.append(ins.pop(0))
            sends = []
            for o, r in zip(outs, results):
                if isinstance(o, Early):
                    buf = spare.pop(0)
                    copy = pltpu.make_async_copy(buf, r, sems.at[next(used)])
                    tiles.append(Tile(buf, [copy], out=True))
                    sends.append(tiles[-1])
                else:
                    tiles.append(r)
            body(*tiles, *extra)
            for t in sends:
                if not t.sent:
                    t.start()
            for t in tiles:
                if isinstance(t, Tile):
                    t.wait()

        room = sum(size(*b) for b in bufs)
        room += sum(size(m.shape, m.dtype) for m in scratch if m.memory_space == pltpu.VMEM)
        result = pl.pallas_call(
            kernel,
            out_shape=tuple(shapes),
            in_specs=in_specs + [spec(pl.ANY)] * len(order),
            out_specs=tuple(out_specs),
            scratch_shapes=[pltpu.VMEM(*b) for b in bufs]
            + ([pltpu.SemaphoreType.DMA((n_sem,))] if n_sem else [])
            + list(scratch),
            compiler_params=pltpu.CompilerParams(vmem_limit_bytes=(stack << 20) + room),
            cost_estimate=pl.CostEstimate(
                flops=int(us * COST), bytes_accessed=1024, transcendentals=0
            ),
            name=name,
        )(*arrays, *order)
        self.last = result[0]
        return list(result)


def ready(t):
    return t.ready() if isinstance(t, Tile) else t


def begin(*tiles):
    for t in tiles:
        if isinstance(t, Tile):
            t.start()


COST = 1.15e9


def row_loop(rows, width, sums, body):
    def step(i, carry):
        at = pl.ds(pl.multiple_of(i * ROWS, ROWS), ROWS)
        parts = body(at)
        return tuple(
            c + jnp.sum(p.reshape(ROWS // 8, 8, width), axis=0) for c, p in zip(carry, parts)
        )

    zero = tuple(jnp.zeros((8, width), F32) for _ in range(sums))
    done = lax.fori_loop(0, rows // ROWS, step, zero)
    return [jnp.sum(c, axis=0, keepdims=True) for c in done]


def normalize(v):
    centre = v - jnp.mean(v, axis=-1, keepdims=True)
    scale = lax.rsqrt(jnp.mean(centre * centre, axis=-1, keepdims=True) + EPS)
    return centre * scale, scale


def mix(chosen, vector, tokens):
    return jnp.where(chosen > 0.5, vector, tokens.astype(F32))


def prep_body(vecs, msk, tok, cot, n1, top, topt, gdb):
    rows, width = tok.shape

    def body(at):
        chosen = msk[at, :]
        hat, _ = normalize(mix(chosen, vecs[0:1, :], tok[at, :]))
        n1[at, :] = (hat * vecs[1:2, :] + vecs[2:3, :]).astype(BF16)
        grad = jnp.where(chosen > 0.5, cot[at, :].astype(F32), 0.0)
        top[at, :] = grad.astype(BF16)
        return (grad,)

    (total,) = row_loop(rows, width, 1, body)
    gdb[...] = total
    topt[...] = top[...].T


def copy_body(*refs):
    n = len(refs) // 2
    for src, dst in zip(refs[:n], refs[n:]):
        dst[...] = src[...]


def head_rows(cols):
    lane = lax.broadcasted_iota(jnp.int32, (1, cols), 1)
    return [
        ((lane >= h * HEAD) & (lane < (h + 1) * HEAD)).astype(F32).astype(BF16)
        for h in range(cols // HEAD)
    ]


def softmax(raw):
    peak = jnp.max(raw, axis=-1, keepdims=True)
    e = jnp.exp((raw - peak) * SCALE)
    return e * (1.0 / jnp.sum(e, axis=-1, keepdims=True))


def attn_fwd_body(slots, n1, bias, *refs):
    ins, outs = refs[:slots], refs[slots:]
    rows = n1.shape[0]
    cols = ins[0].shape[0] // 3
    marks = head_rows(cols)
    for s in range(slots):
        w, qkv, att = ins[s], outs[2 * s], outs[2 * s + 1]
        for j in range(3):
            y = dot_nt(n1[...], w[j * cols : (j + 1) * cols, :])
            if j != 1:
                y = y + bias[s : s + 1, (j // 2) * cols : (j // 2 + 1) * cols]
            qkv[j] = y.astype(BF16)
        begin(qkv)
        for i in range(rows // WIN):
            at = slice(i * WIN, (i + 1) * WIN)
            q, k, v = qkv[0, at, :], qkv[1, at, :], qkv[2, at, :]
            out = None
            for mark in marks:
                part = dot(softmax(dot_nt(q * mark, k)).astype(BF16), v * mark)
                out = part if out is None else out + part
            att[at, :] = out.astype(BF16)


def mid_body(slots, vecs, msk, tok, *refs):
    atts, merges = refs[:slots], refs[slots : 2 * slots]
    res, n2, n2t = refs[2 * slots :]
    rows, width = tok.shape
    total = dot(atts[0][...], merges[0][...])
    for s in range(1, slots):
        total = total + dot(atts[s][...], merges[s][...])
    res[...] = total
    out = res
    msk, tok, res, n2 = (ready(t) for t in (msk, tok, res, n2))

    def body(at):
        r = mix(msk[at, :], vecs[0:1, :], tok[at, :]) + res[at, :] + vecs[3:4, :]
        res[at, :] = r
        hat, _ = normalize(r)
        n2[at, :] = (hat * vecs[4:5, :] + vecs[5:6, :]).astype(BF16)
        return ()

    row_loop(rows, width, 0, body)
    begin(out)
    n2t[...] = n2[...].T


GELU_C = 0.7978845608028654
GELU_A = 0.044715


def ffn_up_body(slots, bias, n2, topt, *refs):
    ups, outs = refs[:slots], refs[slots:]
    hidden = ups[0].shape[1]
    tile = 256
    for s in range(slots):
        act, slope, gd = outs[3 * s : 3 * s + 3]
        for t in range(hidden // tile):
            c = slice(t * tile, (t + 1) * tile)
            pre = dot(n2[...], ups[s][:, c]) + bias[s : s + 1, c]
            sq = pre * pre
            th = jnp.tanh(GELU_C * (pre + GELU_A * (sq * pre)))
            half = 0.5 * (1.0 + th)
            a = (pre * half).astype(BF16)
            rise = half + (0.5 * GELU_C) * pre * (1.0 - th * th) * (1.0 + (3.0 * GELU_A) * sq)
            act[:, c] = a
            slope[:, c] = rise.astype(BF16)
            gd[:, c] = dot(topt[...], a).astype(BF16)
        begin(gd, act, slope)


def ffn_back_body(slots, first, tail, top, n2t, *refs):
    downs, slopes, acts, ups = (refs[i * slots : (i + 1) * slots] for i in range(4))
    refs = refs[4 * slots :]
    if first:
        gus, (y, g, gb, pg) = refs[:slots], refs[slots:]
    else:
        y_in, g_in = refs[:2]
        ends, refs = refs[2 : 2 + tail], refs[2 + tail :]
        gus, gb, outs, (pg, y, g) = refs[:slots], refs[slots], refs[slots + 1 : -3], refs[-3:]
    hidden = ups[0].shape[1]
    tile = 256
    for s in range(slots):
        for t in range(hidden // tile):
            c = slice(t * tile, (t + 1) * tile)
            low = (dot_nt(top[...], downs[s][c, :]) * slopes[s][:, c].astype(F32)).astype(BF16)
            pg[:, c] = low
            gb[s : s + 1, c] = jnp.sum(low.astype(F32), axis=0, keepdims=True)
            gus[s][:, c] = dot(n2t[...], low).astype(BF16)
        begin(gus[s])
        yp = dot(acts[s][...], downs[s][...])
        gp = dot_nt(pg[...], ups[s][...])
        if s == 0 and first:
            y[...] = yp
            g[...] = gp
        elif s == 0:
            y[...] = y_in[...] + yp
            g[...] = g_in[...] + gp
        else:
            y[...] = y[...] + yp
            g[...] = g[...] + gp
    if not first:
        turn_body(y, g, ready(top), *ends, *outs)


def norm_back(grad, gain, hat, scale):
    e = grad * gain
    back = e - jnp.mean(e, axis=-1, keepdims=True)
    return scale * (back - hat * jnp.mean(e * hat, axis=-1, keepdims=True))


def turn_body(y, g, top, vecs, res, *refs):
    out, rg, rl, sums = refs
    rows, width = res.shape
    ends = (rg, out)
    res, out, rg = ready(res), ready(out), ready(rg)

    def body(at):
        r = res[at, :]
        out[at, :] = (r + y[at, :] + vecs[6:7, :]).astype(BF16)
        hat, scale = normalize(r)
        grad = g[at, :]
        full = top[at, :].astype(F32) + norm_back(grad, vecs[4:5, :], hat, scale)
        rg[at, :] = full
        rl[at, :] = full.astype(BF16)
        return (grad * hat, grad, full)

    for i, total in enumerate(row_loop(rows, width, 3, body)):
        sums[i : i + 1, :] = total
    begin(*ends)


def attn_bwd_body(m, rl, qkv, att, n1, a, dqkv, gb, da):
    rows = n1.shape[0]
    cols = m.shape[0]
    marks = head_rows(cols)
    da[...] = dot_nt(rl[...], m[...]).astype(BF16)
    a[3 * cols :, :] = dot_tn(att[...], rl[...]).astype(BF16)
    for i in range(rows // WIN):
        at = slice(i * WIN, (i + 1) * WIN)
        q, k, v, d = qkv[0, at, :], qkv[1, at, :], qkv[2, at, :], da[at, :]
        dq = dk = dv = None
        for mark in marks:
            qm, dm = q * mark, d * mark
            p = softmax(dot_nt(qm, k))
            dp = dot_nt(dm, v)
            ds = (p * (dp - jnp.sum(p * dp, axis=-1, keepdims=True))).astype(BF16)
            parts = dot(ds, k * mark), dot_tn(ds, qm), dot_tn(p.astype(BF16), dm)
            if dq is None:
                dq, dk, dv = parts
            else:
                dq, dk, dv = dq + parts[0], dk + parts[1], dv + parts[2]
        dqkv[0, at, :] = (dq * SCALE).astype(BF16)
        dqkv[1, at, :] = (dk * SCALE).astype(BF16)
        dqkv[2, at, :] = dv.astype(BF16)
    begin(dqkv)
    for j in range(3):
        part = dqkv[j]
        a[j * cols : (j + 1) * cols, :] = dot_tn(part, n1[...]).astype(BF16)
        if j != 1:
            gb[:, (j // 2) * cols : (j // 2 + 1) * cols] = jnp.sum(
                part.astype(F32), axis=0, keepdims=True
            )


def last_body(slots, vecs, msk, *refs):
    parts, ws = refs[:slots], refs[slots : 2 * slots]
    tok, rg, out, sums, g = refs[2 * slots :]
    rows, width = tok.shape
    cols = ws[0].shape[0] // 3
    for s in range(slots):
        total = None
        for j in range(3):
            part = dot(parts[s][j], ws[s][j * cols : (j + 1) * cols, :])
            total = part if total is None else total + part
        g[...] = total if s == 0 else g[...] + total
    msk, tok, rg, out = (ready(t) for t in (msk, tok, rg, out))

    def body(at):
        chosen = msk[at, :]
        hat, scale = normalize(mix(chosen, vecs[0:1, :], tok[at, :]))
        grad = g[at, :]
        full = rg[at, :] + norm_back(grad, vecs[1:2, :], hat, scale)
        out[at, :] = jnp.where(chosen > 0.5, 0.0, full)
        return (jnp.where(chosen > 0.5, full, 0.0), grad * hat, grad)

    for i, total in enumerate(row_loop(rows, width, 3, body)):
        sums[i : i + 1, :] = total


def pack_body(gb_a, gb_b, a0, a1, a2, a3, sums1, sums2, gdb, keep, give):
    n = a0.shape[1]
    for out, rows in ((keep, ((gb_a, 0, a0), (gb_b, 0, a2))), (give, ((gb_a, 1, a1), (gb_b, 1, a3)))):
        out[...] = jnp.zeros_like(out)
        out[0:3, :] = sums1[...]
        out[3:6, :] = sums2[...]
        out[6:7, :] = gdb[...]
        for i, (gb, row, ab) in enumerate(rows):
            out[7 + 2 * i : 8 + 2 * i, :] = gb[row : row + 1, :]
            out[8 + 2 * i : 9 + 2 * i, 0:n] = ab[...]


def pick_body(keep_in, got, keep, give):
    total = keep_in[...] + got[...]
    keep[...] = total[0:9, :]
    give[0:7, :] = total[0:7, :]
    give[7:9, :] = total[9:11, :]


def plus_body(a, b, out):
    out[...] = a[...] + b[...]


def cut_body(n, *refs):
    ins, outs, sem = refs[:n], refs[n : 2 * n], refs[-1]
    pick = Position().mixed()
    copies = []
    for i, (src, dst) in enumerate(zip(ins, outs)):
        half = dst.shape[0]
        at = pl.ds(pl.multiple_of(pick * half, half), half)
        copies.append(pltpu.make_async_copy(src.at[at], dst, sem.at[i]))
        copies[-1].start()
    for c in copies:
        c.wait()


def swap(links, v, *moves):
    n_dp, n_tensor = links
    moves = moves * (2 // len(moves))
    pairs = []
    for d in range(n_dp):
        for t in range(n_tensor):
            fd, ft = moves[t % 2]
            pairs.append((d * n_tensor + t, (d ^ fd) * n_tensor + (t ^ ft)))
    return lax.ppermute(v, ("dp", "tensor"), pairs)


CORE, ACROSS = (0, 1), (0, 2)
DP0, DP1, DP2 = (1, 0), (2, 0), (4, 0)


def add_rows(a, b, at):
    return a[at, :].astype(F32) + b[at, :].astype(F32)


def stage1_body(p0, p2, r1, r3, give, keep, own):
    here = Position()
    n = p0.shape[0] // 2
    y, lead = here.bit(0), here.core == 0
    first, other = (pl.ds(pl.multiple_of(k * n, n), n) for k in (y, 1 - y))
    near, far = add_rows(p0, r1, other), add_rows(p2, r3, first)
    give[:n, :] = jnp.where(lead, far, near).astype(BF16)
    keep[...] = jnp.where(lead, near, far)
    give[n:, :] = add_rows(p2, r3, other).astype(BF16)
    own[...] = add_rows(p0, r1, first)


def pass_body(keep, got, give):
    n = keep.shape[0]
    give[...] = (keep[...] + got[n:, :].astype(F32)).astype(BF16)


def stage3_body(own_in, got1, got2, give, keep, own, v):
    here = Position()
    n = v.shape[0] // 4
    v[...] = own_in[...] + got1[: 4 * n, :].astype(F32) + got2[...].astype(F32)
    z0, z1 = here.bit(1), here.bit(2)
    b00, b01, b10, b11 = (
        pl.multiple_of(i * 2 * n + k * n, n) for i in (z0, 1 - z0) for k in (z1, 1 - z1)
    )
    lead = here.core == 0
    take = lambda at: v[pl.ds(pl.multiple_of(at, n), n), :]
    give[:n, :] = take(jnp.where(lead, b10, b01)).astype(BF16)
    give[n:, :] = take(b11).astype(BF16)
    keep[...] = take(jnp.where(lead, b01, b10))
    own[...] = take(b00)


def sum_body(own, got1, got2, w):
    n = w.shape[0]
    w[...] = (own[...] + got1[:n, :].astype(F32) + got2[...].astype(F32)).astype(BF16)


def stack_body(a, b, out):
    n = a.shape[0]
    out[:n, :] = a[...]
    out[n:, :] = b[...]


def place_body(turned, w, r1, r2, r3, *refs):
    outs, target = refs[:-1], refs[-1]
    here = Position()
    block = w.shape[0]
    i = 0
    for part in (w, r1, r2, r3):
        for k in range(part.shape[0] // block):
            low, mid, high = i % 2, (i // 2) % 2, i // 4
            y = jnp.where(here.core == 0, mid, high)
            z0 = jnp.where(here.core == 0, high, mid)
            flip = lambda h, b: lax.rem(h + here.bit(b), 2)
            at = (flip(y, 0) * 4 + flip(z0, 1) * 2 + flip(low, 2)) * block
            target[pl.ds(pl.multiple_of(at, block), block), :] = part[
                k * block : (k + 1) * block, :
            ].astype(F32)
            i += 1
    start = 0
    for out in outs:
        if turned:
            out[...] = target[...].T
        else:
            out[...] = target[start : start + out.shape[0], :]
            start += out.shape[0]
        begin(out)


class Reduce:
    def __init__(self, links, chain, p0, p1, p2, p3):
        self.links, self.chain = links, chain
        self.parts = (p0, p2, swap(links, p1, CORE), swap(links, p3, CORE))
        self.rows, self.width = p0.shape

    def swap(self, *moves):
        self.got = swap(self.links, self.give, *moves)

    def stage1(self):
        n = self.rows // 2
        half = ((n, self.width), F32)
        self.give, self.keep, self.own = self.chain(
            stage1_body, self.parts, [((2 * n, self.width), BF16), half, half], "add1", 3
        )
        self.swap(ACROSS, DP0)

    def turn(self, first, second):
        self.first = self.got
        (self.give,) = self.chain(
            pass_body, (self.keep, self.got), [(self.keep.shape, BF16)], "add2", 1
        )
        self.swap(second, first)

    def stage2(self):
        self.turn(ACROSS, DP0)

    def stage3(self):
        n = self.rows // 8
        quarter = ((n, self.width), F32)
        self.give, self.keep, self.own = self.chain(
            stage3_body,
            (self.own, self.first, self.got),
            [((2 * n, self.width), BF16), quarter, quarter],
            "add3",
            1.5,
            scratch=[pltpu.VMEM((4 * n, self.width), F32)],
        )
        self.swap(DP1, DP2)

    def stage4(self):
        self.turn(DP1, DP2)

    def spread1(self):
        (self.w,) = self.chain(
            sum_body,
            (self.own, self.first, self.got),
            [((self.rows // 8, self.width), BF16)],
            "add5",
            1,
        )
        i = 3
        while (1 << i) < self.links[0]:
            both = self.w.astype(F32) + swap(self.links, self.w, (1 << i, 0)).astype(F32)
            self.w = both.astype(BF16)
            i += 1
        self.give = self.w
        self.swap(DP2)
        self.parts = [self.w, self.got]

    def spread(self, *moves):
        n, width = self.give.shape
        (self.give,) = self.chain(
            stack_body,
            (self.give, self.got),
            [((2 * n, width), BF16)],
            "stack",
            1,
        )
        self.swap(*moves)
        self.parts.append(self.got)

    def spread2(self):
        self.spread(DP0, DP1)

    def spread3(self):
        self.spread(DP1, DP0)

    def place(self, turned=False, sizes=None):
        sizes = sizes or (self.rows,)
        shapes = [(self.width, self.rows)] if turned else [(n, self.width) for n in sizes]
        return self.chain(
            functools.partial(place_body, turned),
            self.parts,
            [Early(shape, F32) for shape in shapes],
            "place",
            2,
            scratch=[pltpu.VMEM((self.rows, self.width), F32)],
        )


class PlainReduce(Reduce):
    def stage1(self):
        near, far = (
            self.parts[i].astype(F32) + self.parts[i + 2].astype(F32) for i in (0, 1)
        )
        total = near + swap(self.links, far.astype(BF16), ACROSS).astype(F32)
        self.total = lax.psum(total, "dp")

    def skip(self):
        pass

    stage2 = stage3 = stage4 = spread1 = spread2 = spread3 = skip

    def place(self, turned=False, sizes=None):
        if turned:
            return [self.total.T]
        out, at = [], 0
        for n in sizes or (self.rows,):
            out.append(self.total[at : at + n])
            at += n
        return out


class Gather:
    def __init__(self, links, v):
        self.links, self.own = links, v
        self.near = swap(links, v, CORE)

    def send(self, half):
        self.half = swap(self.links, half, ACROSS)

    def spread(self):
        self.rest = swap(self.links, self.half, DP0, DP1)
        self.half_near = swap(self.links, self.half, CORE)

    def slots(self):
        turn = lambda: Position().mixed()
        rest_near = swap(self.links, self.rest, CORE)
        return [
            self.own,
            self.near,
            Stack(self.half, self.rest, turn=turn),
            Stack(self.half_near, rest_near, turn=turn),
        ]


class PlainGather(Gather):
    def send(self, half):
        self.far = swap(self.links, self.own, ACROSS)

    def spread(self):
        pass

    def slots(self):
        return [self.own, self.near, self.far, swap(self.links, self.far, CORE)]


def per_device(
    n_dp,
    n_tensor,
    tokens,
    mask_bits,
    cotangent,
    mask_vector,
    first_gain,
    first_shift,
    attn_weight,
    attn_bias,
    merge_weight,
    merge_bias,
    second_gain,
    second_shift,
    up_weight,
    up_bias,
    down_weight,
    down_bias,
):
    rows, width = tokens.shape
    cols = attn_weight.shape[2]
    hidden = up_weight.shape[1]
    row = lambda v: v[None, :]
    links = (n_dp, n_tensor)
    power = n_dp >= 8 and n_dp & (n_dp - 1) == 0
    chain = Chain()
    make = functools.partial(Reduce if power else PlainReduce, links, chain)
    gather = functools.partial(PlainGather if n_dp % 4 else Gather, links)
    wide, tall, low = ((rows, width), F32), ((width, rows), BF16), ((rows, width), BF16)
    qkv_shape, att_shape = ((3, rows, cols), BF16), ((rows, cols), BF16)

    bias = jnp.concatenate(
        (row(up_bias), jnp.pad(attn_bias.reshape(1, 2 * cols), ((0, 0), (0, hidden - 2 * cols))))
    )
    bias_near, bias_far = swap(links, bias, CORE), swap(links, bias, ACROSS)
    biases = [bias, bias_near, bias_far, swap(links, bias_far, CORE)]
    some_bias = lambda i, js: jnp.concatenate([biases[j][i : i + 1] for j in js])
    vecs = jnp.stack(
        (mask_vector, first_gain, first_shift, merge_bias, second_gain, second_shift, down_bias)
    )
    chosen = (mask_bits == 1).astype(F32)[:, None]

    flat = jnp.transpose(attn_weight, (1, 2, 0)).reshape(3 * cols, width)
    g_attn, g_merge, g_up, g_down = (
        gather(w) for w in (flat, merge_weight, up_weight, down_weight)
    )
    half = lambda w: Raw(((w.shape[0] // 2, w.shape[1]), BF16))
    all_weights = (flat, merge_weight, up_weight, down_weight)
    cuts = chain(
        functools.partial(cut_body, 4),
        [Raw(w) for w in all_weights],
        [half(w) for w in all_weights],
        "cut",
        1.5,
        scratch=[pltpu.SemaphoreType.DMA((4,))],
    )
    for gat, part in zip((g_attn, g_merge, g_up, g_down), cuts):
        gat.send(part)

    def spread(*gathers):
        if n_dp % 4 == 0:
            halves = [gat.half for gat in gathers]
            halves = chain(copy_body, halves, [(h.shape, BF16) for h in halves], "hold", 0.7)
            for gat, part in zip(gathers, halves):
                gat.half = part
        for gat in gathers:
            gat.spread()

    n1, top, topt, gdb = chain(
        prep_body,
        (vecs, chosen, tokens, cotangent),
        [low, low, Early(*tall), ((1, width), F32)],
        "prep",
        4,
    )
    spread(g_attn, g_merge)

    def attn_fwd(js, ws):
        r = chain(
            functools.partial(attn_fwd_body, 2),
            (n1, some_bias(1, js), *ws),
            [Early(*qkv_shape), att_shape] * 2,
            "attn_fwd",
            6,
        )
        return r[0::2], r[1::2]

    qkv_a, att_a = attn_fwd((0, 1), (flat, g_attn.near))
    wa = g_attn.slots()
    wm = g_merge.slots()
    qkv_b, att_b = attn_fwd((2, 3), wa[2:])
    qkv, att = qkv_a + qkv_b, att_a + att_b
    spread(g_up)
    res, n2, n2t = chain(
        functools.partial(mid_body, 4),
        (vecs, chosen, tokens, *att, *wm),
        [Early(*wide), low, tall],
        "mid",
        5.5,
    )

    def ffn_up(js, ups):
        r = chain(
            functools.partial(ffn_up_body, len(js)),
            (some_bias(0, js), n2, Late(topt), *ups),
            [((rows, hidden), BF16), ((rows, hidden), BF16), ((width, hidden), BF16)] * len(js),
            "ffn_up",
            2.75 * len(js),
        )
        return r[0::3], r[1::3], r[2::3]

    act_a, slope_a, gd_a = ffn_up((0, 1), (up_weight, g_up.near))
    spread(g_down)
    wu = g_up.slots()
    act_b, slope_b, gd_b = ffn_up((2, 3), wu[2:])
    red_d = make(*gd_a, *gd_b)

    pg = [pltpu.VMEM((rows, hidden), BF16)]
    grad_up = ((width, hidden), BF16)
    *gu_a, y, g, gb_a = chain(
        functools.partial(ffn_back_body, 2, True, 0),
        (top, n2t, down_weight, g_down.near, *slope_a, *act_a, up_weight, g_up.near),
        [grad_up] * 2 + [wide, wide, ((2, hidden), F32)],
        "ffn_back",
        9,
        scratch=pg,
    )
    wd = g_down.slots()
    red_d.stage1()
    r = chain(
        functools.partial(ffn_back_body, 2, False, 2),
        (top, n2t, *wd[2:], *slope_b, *act_b, *wu[2:], y, g, vecs, Late(res)),
        [grad_up] * 2 + [((2, hidden), F32)]
        + [Early(*low), Early(*wide), low, ((3, width), F32)],
        "ffn_turn",
        14,
        scratch=pg + [pltpu.VMEM(*wide)] * 2,
    )
    gu, gb_b = (*gu_a, *r[:2]), r[2]
    layer_out, res_grad, res_low, sums2 = r[3:]
    red_u = make(*gu)
    red_d.stage2()

    def attn_bwd(j):
        return chain(
            attn_bwd_body,
            (wm[j], res_low, Late(qkv[j]), att[j], Late(n1)),
            [((4 * cols, width), BF16), Early(*qkv_shape), ((1, 2 * cols), F32)],
            "attn_bwd",
            7,
            scratch=[pltpu.VMEM((rows, cols), BF16)],
        )

    back = [None] * 4
    back[1] = attn_bwd(1)
    red_u.stage1()
    red_d.stage3()
    back[3] = attn_bwd(3)
    red_d.stage4()
    back[2] = attn_bwd(2)
    red_u.stage2()
    red_d.spread1()
    back[0] = attn_bwd(0)
    red_a = make(*[b[0] for b in back])
    red_a.stage1()
    red_u.stage3()
    red_d.spread2()
    grad_tokens, sums1 = chain(
        functools.partial(last_body, 4),
        (vecs, chosen, *[Late(b[1]) for b in back], *wa, Late(tokens), Late(res_grad)),
        [Early(*wide), ((3, width), F32)],
        "last",
        10,
        scratch=[pltpu.VMEM((rows, width), F32)],
    )
    nv = 7
    small = (gb_a, gb_b, *[b[2] for b in back], sums1, sums2, gdb)
    keep, give = chain(pack_body, small, [((11, width), F32)] * 2, "pack", 0.7)
    got = swap(links, give, CORE)
    red_a.stage2()
    red_u.stage4()
    red_d.spread3()
    keep, give = chain(
        pick_body, (keep, got), [((nv + 2, width), F32)] * 2, "pick", 0.7
    )
    got = swap(links, give, ACROSS)
    red_u.spread1()
    red_a.stage3()
    (mine,) = chain(plus_body, (keep, got), [((nv + 2, width), F32)], "plus", 0.7)
    if power:
        bits = [1 << i for i in range(n_dp.bit_length() - 1)]
    else:
        mine, bits = lax.psum(mine, "dp"), []

    def vector_step():
        if not bits:
            return mine
        got = swap(links, mine, (bits.pop(0), 0))
        return chain(plus_body, (mine, got), [((nv + 2, width), F32)], "plus", 0.7)[0]

    red_u.spread2()
    mine = vector_step()
    red_a.stage4()
    (sum_d,) = red_d.place(turned=True)
    red_a.spread1()
    mine = vector_step()
    red_u.spread3()
    red_a.spread2()
    mine = vector_step()
    (sum_u,) = red_u.place()
    red_a.spread3()
    while bits:
        mine = vector_step()
    sum_a, sum_m = red_a.place(sizes=(3 * cols, cols))
    grad_attn = jnp.transpose(sum_a.reshape(3, cols, width), (2, 0, 1))
    return (
        layer_out,
        grad_tokens,
        mine[0],
        mine[1],
        mine[2],
        grad_attn,
        mine[nv + 1, : 2 * cols].reshape(2, cols),
        sum_m,
        mine[5],
        mine[3],
        mine[4],
        sum_u,
        mine[nv],
        sum_d,
        mine[6],
    )


def solution(mesh):
    split = P(("dp", "tensor"), None)
    return jax.shard_map(
        functools.partial(per_device, mesh.shape["dp"], mesh.shape["tensor"]),
        mesh=mesh,
        in_specs=(
            split,
            P(("dp", "tensor")),
            split,
            P(),
            P(),
            P(),
            P(None, None, "tensor"),
            P(None, "tensor"),
            P("tensor", None),
            P(),
            P(),
            P(),
            P(None, "tensor"),
            P("tensor"),
            P("tensor", None),
            P(),
        ),
        out_specs=(
            split,
            split,
            P(),
            P(),
            P(),
            P(None, None, "tensor"),
            P(None, "tensor"),
            P("tensor", None),
            P(),
            P(),
            P(),
            P(None, "tensor"),
            P("tensor"),
            P("tensor", None),
            P(),
        ),
        check_vma=False,
    )
```

```python
import functools

import jax
import jax.numpy as jnp
from jax import lax
from jax.experimental import pallas as pl
from jax.experimental.pallas import tpu as pltpu
from jax.sharding import PartitionSpec as P

HEAD = 64
WIN = 256
EPS = 1e-06
SCALE = HEAD**-0.5
ROWS = 64
F32 = jnp.float32
BF16 = jnp.bfloat16


def dot(a, b):
    return lax.dot_general(a, b, (((1,), (0,)), ((), ())), preferred_element_type=F32)


def dot_nt(a, b):
    return lax.dot_general(a, b, (((1,), (1,)), ((), ())), preferred_element_type=F32)


def dot_tn(a, b):
    return lax.dot_general(a, b, (((0,), (0,)), ((), ())), preferred_element_type=F32)


class Stack:
    space = pltpu.VMEM

    def __init__(self, *parts, turn=None):
        self.parts, self.turn = parts, turn
        self.shape = (sum(p.shape[0] for p in parts), *parts[0].shape[1:])
        self.dtype = parts[0].dtype


class Late(Stack):
    space = pl.ANY


class Raw:
    def __init__(self, array):
        self.array = array


class Tile:
    def __init__(self, ref, copies=(), fills=(), out=False):
        self.ref, self.copies, self.fills, self.out, self.sent = ref, copies, fills, out, False
        self.shape, self.dtype = ref.shape, ref.dtype

    def start(self):
        for c in self.copies:
            c.start()
        self.sent = True

    def wait(self):
        for c in self.copies:
            c.wait()
        for at, part in self.fills:
            self.ref[at, :] = part[...]
        self.copies = self.fills = ()
        return self.ref

    def ready(self):
        return self.ref if self.out else self.wait()

    def __getitem__(self, at):
        return self.ready()[at]

    def __setitem__(self, at, value):
        self.ref[at] = value


class Position:
    def __init__(self):
        self.dp = lax.axis_index("dp")
        self.core = lax.rem(lax.axis_index("tensor"), 2)

    def bit(self, i):
        return lax.rem(lax.div(self.dp, 1 << i), 2)

    def mixed(self):
        return lax.rem(self.bit(0) + self.bit(1), 2)


class Early:
    def __init__(self, shape, dtype):
        self.array = (shape, dtype)


def size(shape, dtype):
    shape = (*shape[:-1], -(-shape[-1] // 128) * 128)
    return functools.reduce(lambda a, b: a * b, shape) * jnp.dtype(dtype).itemsize


class Chain:
    def __init__(self):
        self.last = None

    def __call__(self, body, args, outs, name, us, scratch=(), stack=7):
        arrays, in_specs, bufs, n_sem = [], [], [], 0
        spec = lambda space: pl.BlockSpec(memory_space=space)
        for a in args:
            if isinstance(a, Stack):
                arrays += a.parts
                in_specs += [spec(a.space)] * len(a.parts)
                bufs.append((a.shape, a.dtype))
                n_sem += isinstance(a, Late)
            else:
                raw = isinstance(a, Raw)
                arrays.append(a.array if raw else a)
                in_specs.append(spec(pltpu.HBM if raw else pltpu.VMEM))
        shapes, out_specs = [], []
        for o in outs:
            raw, early = isinstance(o, Raw), isinstance(o, Early)
            o = o.array if raw or early else o
            shapes.append(jax.ShapeDtypeStruct(*o))
            out_specs.append(spec(pl.ANY if raw or early else pltpu.VMEM))
            if early:
                bufs.append(o)
                n_sem += 1
        order = () if self.last is None else (self.last,)
        n_in, n_out, n_buf = len(arrays), len(shapes), len(bufs)

        def kernel(*refs):
            ins = list(refs[:n_in])
            refs = refs[n_in + len(order) :]
            results, refs = list(refs[:n_out]), refs[n_out:]
            spare, refs = list(refs[:n_buf]), refs[n_buf:]
            sems = refs[0] if n_sem else None
            extra = refs[1:] if n_sem else refs
            used = iter(range(n_sem))
            tiles = []
            for a in args:
                if isinstance(a, Stack):
                    buf, at, copies, fills = spare.pop(0), 0, [], []
                    if isinstance(a, Late):
                        copies.append(pltpu.make_async_copy(ins.pop(0), buf, sems.at[next(used)]))
                    else:
                        for part in a.parts:
                            n, row = part.shape[0], at
                            if a.turn is not None:
                                row = pl.multiple_of(jnp.where(a.turn() == 0, at, n - at), n)
                            fills.append((pl.ds(row, n), ins.pop(0)))
                            at += n
                    tiles.append(Tile(buf, copies, fills))
                    tiles[-1].start()
                else:
                    tiles.append(ins.pop(0))
            sends = []
            for o, r in zip(outs, results):
                if isinstance(o, Early):
                    buf = spare.pop(0)
                    copy = pltpu.make_async_copy(buf, r, sems.at[next(used)])
                    tiles.append(Tile(buf, [copy], out=True))
                    sends.append(tiles[-1])
                else:
                    tiles.append(r)
            body(*tiles, *extra)
            for t in sends:
                if not t.sent:
                    t.start()
            for t in tiles:
                if isinstance(t, Tile):
                    t.wait()

        room = sum(size(*b) for b in bufs)
        room += sum(size(m.shape, m.dtype) for m in scratch if m.memory_space == pltpu.VMEM)
        result = pl.pallas_call(
            kernel,
            out_shape=tuple(shapes),
            in_specs=in_specs + [spec(pl.ANY)] * len(order),
            out_specs=tuple(out_specs),
            scratch_shapes=[pltpu.VMEM(*b) for b in bufs]
            + ([pltpu.SemaphoreType.DMA((n_sem,))] if n_sem else [])
            + list(scratch),
            compiler_params=pltpu.CompilerParams(vmem_limit_bytes=(stack << 20) + room),
            cost_estimate=pl.CostEstimate(
                flops=int(us * COST), bytes_accessed=1024, transcendentals=0
            ),
            name=name,
        )(*arrays, *order)
        self.last = result[0]
        return list(result)


def ready(t):
    return t.ready() if isinstance(t, Tile) else t


def begin(*tiles):
    for t in tiles:
        if isinstance(t, Tile):
            t.start()


COST = 1.15e9


def row_loop(rows, width, sums, body):
    def step(i, carry):
        at = pl.ds(pl.multiple_of(i * ROWS, ROWS), ROWS)
        parts = body(at)
        return tuple(
            c + jnp.sum(p.reshape(ROWS // 8, 8, width), axis=0) for c, p in zip(carry, parts)
        )

    zero = tuple(jnp.zeros((8, width), F32) for _ in range(sums))
    done = lax.fori_loop(0, rows // ROWS, step, zero)
    return [jnp.sum(c, axis=0, keepdims=True) for c in done]


def normalize(v):
    centre = v - jnp.mean(v, axis=-1, keepdims=True)
    scale = lax.rsqrt(jnp.mean(centre * centre, axis=-1, keepdims=True) + EPS)
    return centre * scale, scale


def mix(chosen, vector, tokens):
    return jnp.where(chosen > 0.5, vector, tokens.astype(F32))


def setup_body(mask, hidden_bias, attn_bias, *refs):
    params, (msk, vecs, bias) = refs[:-3], refs[-3:]
    line = mask[...].astype(F32).reshape(1, mask.shape[0])
    msk[...] = jnp.broadcast_to(line, (8, mask.shape[0])).T
    for i, p in enumerate(params):
        vecs[i : i + 1, :] = p[...].reshape(1, p.shape[0])
    n = attn_bias.shape[1]
    bias[...] = jnp.zeros_like(bias)
    bias[0:1, :] = hidden_bias[...].reshape(1, hidden_bias.shape[0])
    bias[1:2, 0:n] = attn_bias[0:1, :]
    bias[1:2, n : 2 * n] = attn_bias[1:2, :]


def prep_body(vecs, msk, tok, cot, n1, top, topt, gdb):
    rows, width = tok.shape

    def body(at):
        chosen = msk[at, 0:1]
        hat, _ = normalize(mix(chosen, vecs[0:1, :], tok[at, :]))
        n1[at, :] = (hat * vecs[1:2, :] + vecs[2:3, :]).astype(BF16)
        grad = jnp.where(chosen > 0.5, cot[at, :].astype(F32), 0.0)
        top[at, :] = grad.astype(BF16)
        return (grad,)

    (total,) = row_loop(rows, width, 1, body)
    gdb[...] = total
    topt[...] = top[...].T


def copy_body(*refs):
    n = len(refs) // 2
    for src, dst in zip(refs[:n], refs[n:]):
        dst[...] = src[...]


def head_rows(cols):
    lane = lax.broadcasted_iota(jnp.int32, (1, cols), 1)
    return [
        ((lane >= h * HEAD) & (lane < (h + 1) * HEAD)).astype(F32).astype(BF16)
        for h in range(cols // HEAD)
    ]


def softmax(raw):
    peak = jnp.max(raw, axis=-1, keepdims=True)
    e = jnp.exp((raw - peak) * SCALE)
    return e * (1.0 / jnp.sum(e, axis=-1, keepdims=True))


def attn_fwd_body(slots, n1, bias, *refs):
    ins, outs = refs[:slots], refs[slots:]
    rows = n1.shape[0]
    cols = ins[0].shape[0] // 3
    marks = head_rows(cols)
    for s in range(slots):
        w, qkv, att = ins[s], outs[2 * s], outs[2 * s + 1]
        for j in range(3):
            y = dot_nt(n1[...], w[j * cols : (j + 1) * cols, :])
            if j != 1:
                y = y + bias[s : s + 1, (j // 2) * cols : (j // 2 + 1) * cols]
            qkv[j] = y.astype(BF16)
        begin(qkv)
        for i in range(rows // WIN):
            at = slice(i * WIN, (i + 1) * WIN)
            q, k, v = qkv[0, at, :], qkv[1, at, :], qkv[2, at, :]
            out = None
            for mark in marks:
                part = dot(softmax(dot_nt(q * mark, k)).astype(BF16), v * mark)
                out = part if out is None else out + part
            att[at, :] = out.astype(BF16)


def mid_body(slots, vecs, msk, tok, *refs):
    atts, merges = refs[:slots], refs[slots : 2 * slots]
    res, n2, n2t = refs[2 * slots :]
    rows, width = tok.shape
    total = dot(atts[0][...], merges[0][...])
    for s in range(1, slots):
        total = total + dot(atts[s][...], merges[s][...])
    res[...] = total
    out = res
    msk, tok, res, n2 = (ready(t) for t in (msk, tok, res, n2))

    def body(at):
        r = mix(msk[at, 0:1], vecs[0:1, :], tok[at, :]) + res[at, :] + vecs[3:4, :]
        res[at, :] = r
        hat, _ = normalize(r)
        n2[at, :] = (hat * vecs[4:5, :] + vecs[5:6, :]).astype(BF16)
        return ()

    row_loop(rows, width, 0, body)
    begin(out)
    n2t[...] = n2[...].T


GELU_C = 0.7978845608028654
GELU_A = 0.044715


def ffn_up_body(slots, bias, n2, topt, *refs):
    ups, outs = refs[:slots], refs[slots:]
    hidden = ups[0].shape[1]
    tile = 256
    for s in range(slots):
        act, slope, gd = outs[3 * s : 3 * s + 3]
        for t in range(hidden // tile):
            c = slice(t * tile, (t + 1) * tile)
            pre = dot(n2[...], ups[s][:, c]) + bias[s : s + 1, c]
            sq = pre * pre
            th = jnp.tanh(GELU_C * (pre + GELU_A * (sq * pre)))
            half = 0.5 * (1.0 + th)
            a = (pre * half).astype(BF16)
            rise = half + (0.5 * GELU_C) * pre * (1.0 - th * th) * (1.0 + (3.0 * GELU_A) * sq)
            act[:, c] = a
            slope[:, c] = rise.astype(BF16)
            gd[:, c] = dot(topt[...], a).astype(BF16)
        begin(gd, act, slope)


def ffn_back_body(slots, first, tail, top, n2t, *refs):
    downs, slopes, acts, ups = (refs[i * slots : (i + 1) * slots] for i in range(4))
    refs = refs[4 * slots :]
    if first:
        gus, (y, g, gb, pg) = refs[:slots], refs[slots:]
    else:
        y_in, g_in = refs[:2]
        ends, refs = refs[2 : 2 + tail], refs[2 + tail :]
        gus, gb, outs, (pg, y, g) = refs[:slots], refs[slots], refs[slots + 1 : -3], refs[-3:]
    hidden = ups[0].shape[1]
    tile = 256
    for s in range(slots):
        for t in range(hidden // tile):
            c = slice(t * tile, (t + 1) * tile)
            low = (dot_nt(top[...], downs[s][c, :]) * slopes[s][:, c].astype(F32)).astype(BF16)
            pg[:, c] = low
            gb[s : s + 1, c] = jnp.sum(low.astype(F32), axis=0, keepdims=True)
            gus[s][:, c] = dot(n2t[...], low).astype(BF16)
        begin(gus[s])
        yp = dot(acts[s][...], downs[s][...])
        gp = dot_nt(pg[...], ups[s][...])
        if s == 0 and first:
            y[...] = yp
            g[...] = gp
        elif s == 0:
            y[...] = y_in[...] + yp
            g[...] = g_in[...] + gp
        else:
            y[...] = y[...] + yp
            g[...] = g[...] + gp
    if not first:
        turn_body(y, g, ready(top), *ends, *outs)


def norm_back(grad, gain, hat, scale):
    e = grad * gain
    back = e - jnp.mean(e, axis=-1, keepdims=True)
    return scale * (back - hat * jnp.mean(e * hat, axis=-1, keepdims=True))


def turn_body(y, g, top, vecs, res, *refs):
    slots = len(refs) // 2 - 2
    atts, gms, (out, rg, rl, sums) = refs[:slots], refs[slots : 2 * slots], refs[2 * slots :]
    rows, width = res.shape
    ends = (rg, out)
    res, out, rg = ready(res), ready(out), ready(rg)

    def body(at):
        r = res[at, :]
        out[at, :] = (r + y[at, :] + vecs[6:7, :]).astype(BF16)
        hat, scale = normalize(r)
        grad = g[at, :]
        full = top[at, :].astype(F32) + norm_back(grad, vecs[4:5, :], hat, scale)
        rg[at, :] = full
        rl[at, :] = full.astype(BF16)
        return (grad * hat, grad, full)

    for i, total in enumerate(row_loop(rows, width, 3, body)):
        sums[i : i + 1, :] = total
    begin(*ends)
    for att, gm in zip(atts, gms):
        gm[...] = dot_tn(att[...], rl[...]).astype(BF16)


def attn_bwd_body(m, rl, qkv, n1, a, dqkv, gb, da):
    rows = n1.shape[0]
    cols = m.shape[0]
    marks = head_rows(cols)
    da[...] = dot_nt(rl[...], m[...]).astype(BF16)
    for i in range(rows // WIN):
        at = slice(i * WIN, (i + 1) * WIN)
        q, k, v, d = qkv[0, at, :], qkv[1, at, :], qkv[2, at, :], da[at, :]
        dq = dk = dv = None
        for mark in marks:
            qm, dm = q * mark, d * mark
            p = softmax(dot_nt(qm, k))
            dp = dot_nt(dm, v)
            ds = (p * (dp - jnp.sum(p * dp, axis=-1, keepdims=True))).astype(BF16)
            parts = dot(ds, k * mark), dot_tn(ds, qm), dot_tn(p.astype(BF16), dm)
            if dq is None:
                dq, dk, dv = parts
            else:
                dq, dk, dv = dq + parts[0], dk + parts[1], dv + parts[2]
        dqkv[0, at, :] = (dq * SCALE).astype(BF16)
        dqkv[1, at, :] = (dk * SCALE).astype(BF16)
        dqkv[2, at, :] = dv.astype(BF16)
    begin(dqkv)
    for j in range(3):
        part = dqkv[j]
        a[j * cols : (j + 1) * cols, :] = dot_tn(part, n1[...]).astype(BF16)
        if j != 1:
            gb[:, (j // 2) * cols : (j // 2 + 1) * cols] = jnp.sum(
                part.astype(F32), axis=0, keepdims=True
            )


def project_body(slots, *refs):
    parts, ws, g = refs[:slots], refs[slots : 2 * slots], refs[-1]
    cols = ws[0].shape[0] // 3
    for s in range(slots):
        total = None
        for j in range(3):
            part = dot(parts[s][j], ws[s][j * cols : (j + 1) * cols, :])
            total = part if total is None else total + part
        g[...] = total if s == 0 else g[...] + total


def last_body(vecs, msk, g, tok, rg, out, sums):
    rows, width = tok.shape
    end = out
    msk, tok, rg, out = (ready(t) for t in (msk, tok, rg, out))

    def body(at):
        chosen = msk[at, 0:1]
        hat, scale = normalize(mix(chosen, vecs[0:1, :], tok[at, :]))
        grad = g[at, :]
        full = rg[at, :] + norm_back(grad, vecs[1:2, :], hat, scale)
        out[at, :] = jnp.where(chosen > 0.5, 0.0, full)
        return (jnp.where(chosen > 0.5, full, 0.0), grad * hat, grad)

    for i, total in enumerate(row_loop(rows, width, 3, body)):
        sums[i : i + 1, :] = total


def pack_body(gb_a, gb_b, a0, a1, a2, a3, sums1, sums2, gdb, keep, give):
    n = a0.shape[1]
    for out, rows in ((keep, ((gb_a, 0, a0), (gb_b, 0, a2))), (give, ((gb_a, 1, a1), (gb_b, 1, a3)))):
        out[...] = jnp.zeros_like(out)
        out[0:3, :] = sums1[...]
        out[3:6, :] = sums2[...]
        out[6:7, :] = gdb[...]
        for i, (gb, row, ab) in enumerate(rows):
            out[7 + 2 * i : 8 + 2 * i, :] = gb[row : row + 1, :]
            out[8 + 2 * i : 9 + 2 * i, 0:n] = ab[...]


def pick_body(keep_in, got, keep, give):
    total = keep_in[...] + got[...]
    keep[...] = total[0:9, :]
    give[0:7, :] = total[0:7, :]
    give[7:9, :] = total[9:11, :]


def plus_body(a, b, out):
    out[...] = a[...] + b[...]


def cut_body(n, *refs):
    ins, outs, sem = refs[:n], refs[n : 2 * n], refs[-1]
    pick = Position().mixed()
    copies = []
    for i, (src, dst) in enumerate(zip(ins, outs)):
        half = dst.shape[0]
        at = pl.ds(pl.multiple_of(pick * half, half), half)
        copies.append(pltpu.make_async_copy(src.at[at], dst, sem.at[i]))
        copies[-1].start()
    for c in copies:
        c.wait()


def swap(links, v, *moves):
    n_dp, n_tensor = links
    moves = moves * (2 // len(moves))
    pairs = []
    for d in range(n_dp):
        for t in range(n_tensor):
            fd, ft = moves[t % 2]
            pairs.append((d * n_tensor + t, (d ^ fd) * n_tensor + (t ^ ft)))
    return lax.ppermute(v, ("dp", "tensor"), pairs)


CORE, ACROSS = (0, 1), (0, 2)
DP0, DP1, DP2 = (1, 0), (2, 0), (4, 0)


def add_rows(a, b, at):
    return a[at, :].astype(F32) + b[at, :].astype(F32)


def stage1_body(*refs):
    groups, (give, keep, own) = refs[:-3], refs[-3:]
    here = Position()
    y, lead = here.bit(0), here.core == 0
    total, low = keep.shape[0], 0
    for p0, p2, r1, r3 in zip(*[iter(groups)] * 4):
        n = p0.shape[0] // 2
        add_group(y, lead, p0, p2, r1, r3, n, low, total, give, keep, own)
        low += n


def add_group(y, lead, p0, p2, r1, r3, n, low, total, give, keep, own):
    at, later = slice(low, low + n), slice(total + low, total + low + n)
    first, other = (pl.ds(pl.multiple_of(k * n, n), n) for k in (y, 1 - y))
    near, far = add_rows(p0, r1, other), add_rows(p2, r3, first)
    give[at, :] = jnp.where(lead, far, near).astype(BF16)
    keep[at, :] = jnp.where(lead, near, far)
    give[later, :] = add_rows(p2, r3, other).astype(BF16)
    own[at, :] = add_rows(p0, r1, first)


def pass_body(keep, got, give):
    n = keep.shape[0]
    give[...] = (keep[...] + got[n:, :].astype(F32)).astype(BF16)


def stage3_body(own_in, got1, got2, give, keep, own, v):
    here = Position()
    n = v.shape[0] // 4
    v[...] = own_in[...] + got1[: 4 * n, :].astype(F32) + got2[...].astype(F32)
    z0, z1 = here.bit(1), here.bit(2)
    b00, b01, b10, b11 = (
        pl.multiple_of(i * 2 * n + k * n, n) for i in (z0, 1 - z0) for k in (z1, 1 - z1)
    )
    lead = here.core == 0
    take = lambda at: v[pl.ds(pl.multiple_of(at, n), n), :]
    give[:n, :] = take(jnp.where(lead, b10, b01)).astype(BF16)
    give[n:, :] = take(b11).astype(BF16)
    keep[...] = take(jnp.where(lead, b01, b10))
    own[...] = take(b00)


def sum_body(own, got1, got2, w):
    n = w.shape[0]
    w[...] = (own[...] + got1[:n, :].astype(F32) + got2[...].astype(F32)).astype(BF16)


def stack_body(a, b, out):
    n = a.shape[0]
    out[:n, :] = a[...]
    out[n:, :] = b[...]


def place_body(turned, w, r1, r2, r3, *refs):
    outs, target = refs[:-1], refs[-1]
    here = Position()
    block = w.shape[0]
    i = 0
    for part in (w, r1, r2, r3):
        for k in range(part.shape[0] // block):
            low, mid, high = i % 2, (i // 2) % 2, i // 4
            y = jnp.where(here.core == 0, mid, high)
            z0 = jnp.where(here.core == 0, high, mid)
            flip = lambda h, b: lax.rem(h + here.bit(b), 2)
            at = (flip(y, 0) * 4 + flip(z0, 1) * 2 + flip(low, 2)) * block
            target[pl.ds(pl.multiple_of(at, block), block), :] = part[
                k * block : (k + 1) * block, :
            ].astype(F32)
            i += 1
    low, half = 0, target.shape[0] // 2
    for out in outs:
        n = out.shape[0] // 2
        if turned:
            out[...] = target[...].T
        else:
            out[:n, :] = target[low : low + n, :]
            out[n:, :] = target[half + low : half + low + n, :]
            low += n
        begin(out)


class Reduce:
    def __init__(self, links, chain, *groups):
        self.links, self.chain, self.parts = links, chain, []
        for p0, p1, p2, p3 in groups:
            self.parts += [p0, p2, swap(links, p1, CORE), swap(links, p3, CORE)]
        self.sizes = [g[0].shape[0] for g in groups]
        self.rows, self.width = sum(self.sizes), groups[0][0].shape[1]

    def swap(self, *moves):
        self.got = swap(self.links, self.give, *moves)

    def stage1(self):
        n = self.rows // 2
        half = ((n, self.width), F32)
        self.give, self.keep, self.own = self.chain(
            stage1_body, self.parts, [((2 * n, self.width), BF16), half, half], "add1", 3
        )
        self.swap(ACROSS, DP0)

    def turn(self, first, second):
        self.first = self.got
        (self.give,) = self.chain(
            pass_body, (self.keep, self.got), [(self.keep.shape, BF16)], "add2", 1
        )
        self.swap(second, first)

    def stage2(self):
        self.turn(ACROSS, DP0)

    def stage3(self):
        n = self.rows // 8
        quarter = ((n, self.width), F32)
        self.give, self.keep, self.own = self.chain(
            stage3_body,
            (self.own, self.first, self.got),
            [((2 * n, self.width), BF16), quarter, quarter],
            "add3",
            1.5,
            scratch=[pltpu.VMEM((4 * n, self.width), F32)],
        )
        self.swap(DP1, DP2)

    def stage4(self):
        self.turn(DP1, DP2)

    def spread1(self):
        (self.w,) = self.chain(
            sum_body,
            (self.own, self.first, self.got),
            [((self.rows // 8, self.width), BF16)],
            "add5",
            1,
        )
        i = 3
        while (1 << i) < self.links[0]:
            both = self.w.astype(F32) + swap(self.links, self.w, (1 << i, 0)).astype(F32)
            self.w = both.astype(BF16)
            i += 1
        self.give = self.w
        self.swap(DP2)
        self.parts = [self.w, self.got]

    def spread(self, *moves):
        n, width = self.give.shape
        (self.give,) = self.chain(
            stack_body,
            (self.give, self.got),
            [((2 * n, width), BF16)],
            "stack",
            1,
        )
        self.swap(*moves)
        self.parts.append(self.got)

    def spread2(self):
        self.spread(DP0, DP1)

    def spread3(self):
        self.spread(DP1, DP0)

    def place(self, turned=False):
        shapes = [(self.width, self.rows)] if turned else [(n, self.width) for n in self.sizes]
        return self.chain(
            functools.partial(place_body, turned),
            self.parts,
            [Early(shape, F32) for shape in shapes],
            "place",
            2,
            scratch=[pltpu.VMEM((self.rows, self.width), F32)],
        )


class PlainReduce(Reduce):
    def stage1(self):
        self.totals = []
        for i in range(0, len(self.parts), 4):
            p0, p2, r1, r3 = (v.astype(F32) for v in self.parts[i : i + 4])
            far = swap(self.links, (p2 + r3).astype(BF16), ACROSS).astype(F32)
            self.totals.append(lax.psum(p0 + r1 + far, "dp"))

    def skip(self):
        pass

    stage2 = stage3 = stage4 = spread1 = spread2 = spread3 = skip

    def place(self, turned=False):
        return [self.totals[0].T] if turned else self.totals


class Gather:
    def __init__(self, links, v):
        self.links, self.own = links, v
        self.near = swap(links, v, CORE)

    def send(self, half):
        self.half = swap(self.links, half, ACROSS)

    def spread(self):
        self.rest = swap(self.links, self.half, DP0, DP1)
        self.half_near = swap(self.links, self.half, CORE)

    def share(self):
        self.rest_near = swap(self.links, self.rest, CORE)

    def slots(self):
        turn = lambda: Position().mixed()
        rest_near = self.rest_near
        return [
            self.own,
            self.near,
            Stack(self.half, self.rest, turn=turn),
            Stack(self.half_near, rest_near, turn=turn),
        ]


class PlainGather(Gather):
    def send(self, half):
        self.far = swap(self.links, self.own, ACROSS)

    def spread(self):
        pass

    def share(self):
        pass

    def slots(self):
        return [self.own, self.near, self.far, swap(self.links, self.far, CORE)]


def per_device(
    n_dp,
    n_tensor,
    tokens,
    mask_bits,
    cotangent,
    mask_vector,
    first_gain,
    first_shift,
    attn_weight,
    attn_bias,
    merge_weight,
    merge_bias,
    second_gain,
    second_shift,
    up_weight,
    up_bias,
    down_weight,
    down_bias,
):
    rows, width = tokens.shape
    cols = attn_weight.shape[2]
    hidden = up_weight.shape[1]
    row = lambda v: v[None, :]
    links = (n_dp, n_tensor)
    power = n_dp >= 8 and n_dp & (n_dp - 1) == 0
    chain = Chain()
    make = functools.partial(Reduce if power else PlainReduce, links, chain)
    gather = functools.partial(PlainGather if n_dp % 4 else Gather, links)
    wide, tall, low = ((rows, width), F32), ((width, rows), BF16), ((rows, width), BF16)
    qkv_shape, att_shape = ((3, rows, cols), BF16), ((rows, cols), BF16)

    some_bias = lambda i, js: jnp.concatenate([biases[j][i : i + 1] for j in js])
    flat = jnp.transpose(attn_weight, (1, 2, 0)).reshape(3 * cols, width)
    g_attn, g_merge, g_up, g_down = (
        gather(w) for w in (flat, merge_weight, up_weight, down_weight)
    )
    half = lambda w: ((w.shape[0] // 2, w.shape[1]), BF16)
    all_weights = (flat, merge_weight, up_weight, down_weight)
    cuts = chain(
        functools.partial(cut_body, 4),
        [Raw(w) for w in all_weights],
        [half(w) for w in all_weights],
        "cut",
        1.5,
        scratch=[pltpu.SemaphoreType.DMA((4,))],
        stack=57,
    )
    for gat, part in zip((g_attn, g_merge, g_up, g_down), cuts):
        gat.send(part)

    msk, vecs, bias = chain(
        setup_body,
        (mask_bits, up_bias, attn_bias, mask_vector, first_gain, first_shift, merge_bias)
        + (second_gain, second_shift, down_bias),
        [((rows, 8), F32), ((7, width), F32), ((2, hidden), F32)],
        "setup",
        1,
    )
    bias_near, bias_far = swap(links, bias, CORE), swap(links, bias, ACROSS)
    biases = [bias, bias_near, bias_far, swap(links, bias_far, CORE)]

    def spread(*gathers):
        if n_dp % 4 == 0:
            halves = [gat.half for gat in gathers]
            halves = chain(copy_body, halves, [(h.shape, BF16) for h in halves], "hold", 0.7)
            for gat, part in zip(gathers, halves):
                gat.half = part
        for gat in gathers:
            gat.spread()

    def share(gat):
        if n_dp % 4 == 0:
            (gat.rest,) = chain(copy_body, (gat.rest,), [(gat.rest.shape, BF16)], "hold", 0.7)
        gat.share()

    n1, top, topt, gdb = chain(
        prep_body,
        (vecs, msk, tokens, cotangent),
        [low, low, Early(*tall), ((1, width), F32)],
        "prep",
        4,
    )
    spread(g_attn, g_merge)

    def attn_fwd(js, ws, us):
        r = chain(
            functools.partial(attn_fwd_body, 2),
            (n1, some_bias(1, js), *ws),
            [Early(*qkv_shape), att_shape] * 2,
            "attn_fwd",
            us,
        )
        return r[0::2], r[1::2]

    qkv_a, att_a = attn_fwd((0, 1), (flat, g_attn.near), 6)
    share(g_attn)
    g_merge.share()
    wa = g_attn.slots()
    wm = g_merge.slots()
    qkv_b, att_b = attn_fwd((2, 3), wa[2:], 0.5)
    qkv, att = qkv_a + qkv_b, att_a + att_b
    spread(g_up)
    res, n2, n2t = chain(
        functools.partial(mid_body, 4),
        (vecs, msk, tokens, *att, *wm),
        [Early(*wide), low, tall],
        "mid",
        5.5,
    )

    def ffn_up(js, ups):
        r = chain(
            functools.partial(ffn_up_body, len(js)),
            (some_bias(0, js), n2, Late(topt), *ups),
            [((rows, hidden), BF16), ((rows, hidden), BF16), ((width, hidden), BF16)] * len(js),
            "ffn_up",
            2.75 * len(js),
        )
        return r[0::3], r[1::3], r[2::3]

    act_a, slope_a, gd_a = ffn_up((0, 1), (up_weight, g_up.near))
    spread(g_down)
    g_up.share()
    wu = g_up.slots()
    act_b, slope_b, gd_b = ffn_up((2, 3), wu[2:])
    red_d = make((*gd_a, *gd_b))

    pg = [pltpu.VMEM((rows, hidden), BF16)]
    grad_up = ((width, hidden), BF16)
    *gu_a, y, g, gb_a = chain(
        functools.partial(ffn_back_body, 2, True, 0),
        (top, n2t, down_weight, g_down.near, *slope_a, *act_a, up_weight, g_up.near),
        [grad_up] * 2 + [wide, wide, ((2, hidden), F32)],
        "ffn_back",
        9,
        scratch=pg,
    )
    g_down.share()
    wd = g_down.slots()
    red_d.stage1()
    r = chain(
        functools.partial(ffn_back_body, 2, False, 6),
        (top, n2t, *wd[2:], *slope_b, *act_b, *wu[2:], y, g, vecs, Late(res), *att),
        [grad_up] * 2 + [((2, hidden), F32)] + [((cols, width), BF16)] * 4
        + [Early(*low), Early(*wide), low, ((3, width), F32)],
        "ffn_turn",
        14,
        scratch=pg + [pltpu.VMEM(*wide)] * 2,
    )
    gb_b = r[2]
    layer_out, res_grad, res_low, sums2 = r[7:]
    red_u = make((*gu_a, *r[:2]), r[3:7])
    red_d.stage2()

    def attn_bwd(j):
        return chain(
            attn_bwd_body,
            (wm[j], res_low, Late(qkv[j]), Late(n1)),
            [((3 * cols, width), BF16), Early(*qkv_shape), ((1, 2 * cols), F32)],
            "attn_bwd",
            7,
            scratch=[pltpu.VMEM((rows, cols), BF16)],
        )

    back = [None] * 4
    back[1] = attn_bwd(1)
    red_u.stage1()
    red_d.stage3()
    back[3] = attn_bwd(3)
    red_d.stage4()
    back[2] = attn_bwd(2)
    red_u.stage2()
    red_d.spread1()
    back[0] = attn_bwd(0)
    red_a = make([b[0] for b in back])
    red_a.stage1()
    red_u.stage3()
    (g,) = chain(
        functools.partial(project_body, 4), (*[Late(b[1]) for b in back], *wa), [wide], "project", 6
    )
    red_a.stage2()
    red_u.stage4()
    grad_tokens, sums1 = chain(
        last_body,
        (vecs, msk, g, Late(tokens), Late(res_grad)),
        [Early(*wide), ((3, width), F32)],
        "last",
        8,
    )
    nv = 7
    small = (gb_a, gb_b, *[b[2] for b in back], sums1, sums2, gdb)
    keep, give = chain(pack_body, small, [((11, width), F32)] * 2, "pack", 0.7)
    got = swap(links, give, CORE)
    red_a.stage3()
    red_d.spread2()
    keep, give = chain(
        pick_body, (keep, got), [((nv + 2, width), F32)] * 2, "pick", 0.7
    )
    got = swap(links, give, ACROSS)
    red_u.spread1()
    red_a.stage4()
    (mine,) = chain(plus_body, (keep, got), [((nv + 2, width), F32)], "plus", 0.7)
    if power:
        bits = [1 << i for i in range(n_dp.bit_length() - 1)]
    else:
        mine, bits = lax.psum(mine, "dp"), []

    def begin_vector():
        return swap(links, mine, (bits[0], 0)) if bits else None

    def end_vector(got):
        if not bits:
            return mine
        bits.pop(0)
        return chain(plus_body, (mine, got), [((nv + 2, width), F32)], "plus", 0.7)[0]

    got = begin_vector()
    red_a.spread1()
    red_d.spread3()
    mine = end_vector(got)
    got = begin_vector()
    red_u.spread2()
    red_a.spread2()
    mine = end_vector(got)
    got = begin_vector()
    red_u.spread3()
    (sum_d,) = red_d.place(turned=True)
    red_a.spread3()
    mine = end_vector(got)
    while bits:
        mine = end_vector(begin_vector())
    sum_u, sum_m = red_u.place()
    (sum_a,) = red_a.place()
    grad_attn = jnp.transpose(sum_a.reshape(3, cols, width), (2, 0, 1))
    return (
        layer_out,
        grad_tokens,
        mine[0],
        mine[1],
        mine[2],
        grad_attn,
        mine[nv + 1, : 2 * cols].reshape(2, cols),
        sum_m,
        mine[5],
        mine[3],
        mine[4],
        sum_u,
        mine[nv],
        sum_d,
        mine[6],
    )


def solution(mesh):
    split = P(("dp", "tensor"), None)
    return jax.shard_map(
        functools.partial(per_device, mesh.shape["dp"], mesh.shape["tensor"]),
        mesh=mesh,
        in_specs=(
            split,
            P(("dp", "tensor")),
            split,
            P(),
            P(),
            P(),
            P(None, None, "tensor"),
            P(None, "tensor"),
            P("tensor", None),
            P(),
            P(),
            P(),
            P(None, "tensor"),
            P("tensor"),
            P("tensor", None),
            P(),
        ),
        out_specs=(
            split,
            split,
            P(),
            P(),
            P(),
            P(None, None, "tensor"),
            P(None, "tensor"),
            P("tensor", None),
            P(),
            P(),
            P(),
            P(None, "tensor"),
            P("tensor"),
            P("tensor", None),
            P(),
        ),
        check_vma=False,
    )
```

```python
import functools

import jax
import jax.numpy as jnp
from jax import lax
from jax.experimental import pallas as pl
from jax.experimental.pallas import tpu as pltpu
from jax.sharding import PartitionSpec as P

HEAD = 64
WIN = 256
EPS = 1e-06
SCALE = HEAD**-0.5
ROWS = 64
F32 = jnp.float32
BF16 = jnp.bfloat16


def dot(a, b):
    return lax.dot_general(a, b, (((1,), (0,)), ((), ())), preferred_element_type=F32)


def dot_nt(a, b):
    return lax.dot_general(a, b, (((1,), (1,)), ((), ())), preferred_element_type=F32)


def dot_tn(a, b):
    return lax.dot_general(a, b, (((0,), (0,)), ((), ())), preferred_element_type=F32)


class Stack:
    space = pltpu.VMEM

    def __init__(self, *parts, turn=None):
        self.parts, self.turn = parts, turn
        self.shape = (sum(p.shape[0] for p in parts), *parts[0].shape[1:])
        self.dtype = parts[0].dtype


class Late(Stack):
    space = pl.ANY


class Raw:
    def __init__(self, array):
        self.array = array


class Tile:
    def __init__(self, ref, copies=(), fills=(), out=False):
        self.ref, self.copies, self.fills, self.out, self.sent = ref, copies, fills, out, False
        self.shape, self.dtype = ref.shape, ref.dtype

    def start(self):
        for c in self.copies:
            c.start()
        self.sent = True

    def wait(self):
        for c in self.copies:
            c.wait()
        for at, part in self.fills:
            self.ref[at, :] = part[...]
        self.copies = self.fills = ()
        return self.ref

    def ready(self):
        return self.ref if self.out else self.wait()

    def __getitem__(self, at):
        return self.ready()[at]

    def __setitem__(self, at, value):
        self.ref[at] = value


class Position:
    def __init__(self):
        self.dp = lax.axis_index("dp")
        self.core = lax.rem(lax.axis_index("tensor"), 2)

    def bit(self, i):
        return lax.rem(lax.div(self.dp, 1 << i), 2)

    def mixed(self):
        return lax.rem(self.bit(0) + self.bit(1), 2)

    def half(self):
        return jnp.where(self.core == 0, self.bit(1), self.bit(2))


class Early:
    def __init__(self, shape, dtype):
        self.array = (shape, dtype)


def size(shape, dtype):
    shape = (*shape[:-1], -(-shape[-1] // 128) * 128)
    return functools.reduce(lambda a, b: a * b, shape) * jnp.dtype(dtype).itemsize


class Chain:
    def __init__(self):
        self.last = None

    def __call__(self, body, args, outs, name, us, scratch=(), stack=7, alias=()):
        arrays, in_specs, bufs, n_sem = [], [], [], 0
        spec = lambda space: pl.BlockSpec(memory_space=space)
        for a in args:
            if isinstance(a, Stack):
                arrays += a.parts
                in_specs += [spec(a.space)] * len(a.parts)
                bufs.append((a.shape, a.dtype))
                n_sem += isinstance(a, Late)
            else:
                raw = isinstance(a, Raw)
                arrays.append(a.array if raw else a)
                in_specs.append(spec(pltpu.HBM if raw else pltpu.VMEM))
        shapes, out_specs = [], []
        for o in outs:
            raw, early = isinstance(o, Raw), isinstance(o, Early)
            o = o.array if raw or early else o
            shapes.append(jax.ShapeDtypeStruct(*o))
            out_specs.append(spec(pltpu.HBM if raw or early else pltpu.VMEM))
            if early:
                bufs.append(o)
                n_sem += 1
        order = () if self.last is None else (self.last,)
        n_in, n_out, n_buf = len(arrays), len(shapes), len(bufs)

        def kernel(*refs):
            ins = list(refs[:n_in])
            refs = refs[n_in + len(order) :]
            results, refs = list(refs[:n_out]), refs[n_out:]
            spare, refs = list(refs[:n_buf]), refs[n_buf:]
            sems = refs[0] if n_sem else None
            extra = refs[1:] if n_sem else refs
            used = iter(range(n_sem))
            tiles = []
            for a in args:
                if isinstance(a, Stack):
                    buf, at, copies, fills = spare.pop(0), 0, [], []
                    if isinstance(a, Late):
                        copies.append(pltpu.make_async_copy(ins.pop(0), buf, sems.at[next(used)]))
                    else:
                        for part in a.parts:
                            n, row = part.shape[0], at
                            if a.turn is not None:
                                row = pl.multiple_of(jnp.where(a.turn() == 0, at, n - at), n)
                            fills.append((pl.ds(row, n), ins.pop(0)))
                            at += n
                    tiles.append(Tile(buf, copies, fills))
                    tiles[-1].start()
                else:
                    tiles.append(ins.pop(0))
            sends = []
            for o, r in zip(outs, results):
                if isinstance(o, Early):
                    buf = spare.pop(0)
                    copy = pltpu.make_async_copy(buf, r, sems.at[next(used)])
                    tiles.append(Tile(buf, [copy], out=True))
                    sends.append(tiles[-1])
                else:
                    tiles.append(r)
            body(*tiles, *extra)
            for t in sends:
                if not t.sent:
                    t.start()
            for t in tiles:
                if isinstance(t, Tile):
                    t.wait()

        room = sum(size(*b) for b in bufs)
        room += sum(size(m.shape, m.dtype) for m in scratch if m.memory_space == pltpu.VMEM)
        result = pl.pallas_call(
            kernel,
            out_shape=tuple(shapes),
            in_specs=in_specs + [spec(pl.ANY)] * len(order),
            out_specs=tuple(out_specs),
            input_output_aliases={
                next(i for i, a in enumerate(arrays) if a is v): o for v, o in alias
            },
            scratch_shapes=[pltpu.VMEM(*b) for b in bufs]
            + ([pltpu.SemaphoreType.DMA((n_sem,))] if n_sem else [])
            + list(scratch),
            compiler_params=pltpu.CompilerParams(vmem_limit_bytes=(stack << 20) + room),
            cost_estimate=pl.CostEstimate(
                flops=int(us * COST), bytes_accessed=1024, transcendentals=0
            ),
            name=name,
        )(*arrays, *order)
        self.last = result[0]
        return list(result)


def ready(t):
    return t.ready() if isinstance(t, Tile) else t


def begin(*tiles):
    for t in tiles:
        if isinstance(t, Tile):
            t.start()


COST = 1.15e9


def row_loop(rows, width, sums, body):
    def step(i, carry):
        at = pl.ds(pl.multiple_of(i * ROWS, ROWS), ROWS)
        parts = body(at)
        return tuple(
            c + jnp.sum(p.reshape(ROWS // 8, 8, width), axis=0) for c, p in zip(carry, parts)
        )

    zero = tuple(jnp.zeros((8, width), F32) for _ in range(sums))
    done = lax.fori_loop(0, rows // ROWS, step, zero)
    return [jnp.sum(c, axis=0, keepdims=True) for c in done]


def normalize(v):
    centre = v - jnp.mean(v, axis=-1, keepdims=True)
    scale = lax.rsqrt(jnp.mean(centre * centre, axis=-1, keepdims=True) + EPS)
    return centre * scale, scale


def mix(chosen, vector, tokens):
    return jnp.where(chosen > 0.5, vector, tokens.astype(F32))


def setup_body(mask, hidden_bias, attn_bias, *refs):
    params, (msk, vecs, bias) = refs[:-3], refs[-3:]
    line = mask[...].astype(F32).reshape(1, mask.shape[0])
    msk[...] = jnp.broadcast_to(line, (8, mask.shape[0])).T
    for i, p in enumerate(params):
        vecs[i : i + 1, :] = p[...].reshape(1, p.shape[0])
    n = attn_bias.shape[1]
    bias[...] = jnp.zeros_like(bias)
    bias[0:1, :] = hidden_bias[...].reshape(1, hidden_bias.shape[0])
    bias[1:2, 0:n] = attn_bias[0:1, :]
    bias[1:2, n : 2 * n] = attn_bias[1:2, :]


def prep_body(vecs, msk, tok, cot, n1, top, topt, gdb):
    rows, width = tok.shape

    def body(at):
        chosen = msk[at, 0:1]
        hat, _ = normalize(mix(chosen, vecs[0:1, :], tok[at, :]))
        n1[at, :] = (hat * vecs[1:2, :] + vecs[2:3, :]).astype(BF16)
        grad = jnp.where(chosen > 0.5, cot[at, :].astype(F32), 0.0)
        top[at, :] = grad.astype(BF16)
        return (grad,)

    (total,) = row_loop(rows, width, 1, body)
    gdb[...] = total
    topt[...] = top[...].T


def copy_body(*refs):
    n = len(refs) // 2
    for src, dst in zip(refs[:n], refs[n:]):
        dst[...] = src[...]


def head_rows(cols):
    lane = lax.broadcasted_iota(jnp.int32, (1, cols), 1)
    return [
        ((lane >= h * HEAD) & (lane < (h + 1) * HEAD)).astype(F32).astype(BF16)
        for h in range(cols // HEAD)
    ]


def softmax(raw):
    peak = jnp.max(raw, axis=-1, keepdims=True)
    e = jnp.exp((raw - peak) * SCALE)
    return e * (1.0 / jnp.sum(e, axis=-1, keepdims=True))


def attn_fwd_body(slots, n1, bias, *refs):
    ins, outs = refs[:slots], refs[slots:]
    rows = n1.shape[0]
    cols = ins[0].shape[0] // 3
    marks = head_rows(cols)
    for s in range(slots):
        w, qkv, att = ins[s], outs[2 * s], outs[2 * s + 1]
        for j in range(3):
            y = dot_nt(n1[...], w[j * cols : (j + 1) * cols, :])
            if j != 1:
                y = y + bias[s : s + 1, (j // 2) * cols : (j // 2 + 1) * cols]
            qkv[j] = y.astype(BF16)
        begin(qkv)
        for i in range(rows // WIN):
            at = slice(i * WIN, (i + 1) * WIN)
            q, k, v = qkv[0, at, :], qkv[1, at, :], qkv[2, at, :]
            out = None
            for mark in marks:
                part = dot(softmax(dot_nt(q * mark, k)).astype(BF16), v * mark)
                out = part if out is None else out + part
            att[at, :] = out.astype(BF16)


def mid_body(slots, vecs, msk, tok, *refs):
    atts, merges = refs[:slots], refs[slots : 2 * slots]
    res, n2, n2t = refs[2 * slots :]
    rows, width = tok.shape
    total = dot(atts[0][...], merges[0][...])
    for s in range(1, slots):
        total = total + dot(atts[s][...], merges[s][...])
    res[...] = total
    out = res
    msk, tok, res, n2 = (ready(t) for t in (msk, tok, res, n2))

    def body(at):
        r = mix(msk[at, 0:1], vecs[0:1, :], tok[at, :]) + res[at, :] + vecs[3:4, :]
        res[at, :] = r
        hat, _ = normalize(r)
        n2[at, :] = (hat * vecs[4:5, :] + vecs[5:6, :]).astype(BF16)
        return ()

    row_loop(rows, width, 0, body)
    begin(out)
    n2t[...] = n2[...].T


GELU_C = 0.7978845608028654
GELU_A = 0.044715


def ffn_up_body(slots, bias, n2, topt, *refs):
    ups, outs = refs[:slots], refs[slots:]
    hidden = ups[0].shape[1]
    tile = 256
    for s in range(slots):
        act, slope, gd = outs[3 * s : 3 * s + 3]
        for t in range(hidden // tile):
            c = slice(t * tile, (t + 1) * tile)
            pre = dot(n2[...], ups[s][:, c]) + bias[s : s + 1, c]
            sq = pre * pre
            th = jnp.tanh(GELU_C * (pre + GELU_A * (sq * pre)))
            half = 0.5 * (1.0 + th)
            a = (pre * half).astype(BF16)
            rise = half + (0.5 * GELU_C) * pre * (1.0 - th * th) * (1.0 + (3.0 * GELU_A) * sq)
            act[:, c] = a
            slope[:, c] = rise.astype(BF16)
            gd[:, c] = dot(topt[...], a).astype(BF16)
        begin(gd, act, slope)


def ffn_back_body(slots, first, top, n2t, *refs):
    downs, slopes, acts, ups = (refs[i * slots : (i + 1) * slots] for i in range(4))
    refs = refs[4 * slots :]
    if first:
        gus, (y, g, gb, pg) = refs[:slots], refs[slots:]
    else:
        y_in, g_in = refs[:2]
        gus, (y, g, gb, pg) = refs[2 : 2 + slots], refs[2 + slots :]
    hidden = ups[0].shape[1]
    tile = 256
    for s in range(slots):
        for t in range(hidden // tile):
            c = slice(t * tile, (t + 1) * tile)
            low = (dot_nt(top[...], downs[s][c, :]) * slopes[s][:, c].astype(F32)).astype(BF16)
            pg[:, c] = low
            gb[s : s + 1, c] = jnp.sum(low.astype(F32), axis=0, keepdims=True)
            gus[s][:, c] = dot(n2t[...], low).astype(BF16)
        begin(gus[s])
        yp = dot(acts[s][...], downs[s][...])
        gp = dot_nt(pg[...], ups[s][...])
        if s == 0 and first:
            y[...] = yp
            g[...] = gp
        elif s == 0:
            y[...] = y_in[...] + yp
            g[...] = g_in[...] + gp
        else:
            y[...] = y[...] + yp
            g[...] = g[...] + gp


def norm_back(grad, gain, hat, scale):
    e = grad * gain
    back = e - jnp.mean(e, axis=-1, keepdims=True)
    return scale * (back - hat * jnp.mean(e * hat, axis=-1, keepdims=True))


def turn_body(vecs, res, y, g, top, *refs):
    slots = len(refs) // 2 - 2
    atts, gms, (out, rg, rl, sums) = refs[:slots], refs[slots : 2 * slots], refs[2 * slots :]
    rows, width = res.shape
    ends = (rg, out)
    res, out, rg, top = (ready(t) for t in (res, out, rg, top))

    def body(at):
        r = res[at, :]
        out[at, :] = (r + y[at, :] + vecs[6:7, :]).astype(BF16)
        hat, scale = normalize(r)
        grad = g[at, :]
        full = top[at, :].astype(F32) + norm_back(grad, vecs[4:5, :], hat, scale)
        rg[at, :] = full
        rl[at, :] = full.astype(BF16)
        return (grad * hat, grad, full)

    for i, total in enumerate(row_loop(rows, width, 3, body)):
        sums[i : i + 1, :] = total
    begin(*ends)
    for att, gm in zip(atts, gms):
        gm[...] = dot_tn(att[...], rl[...]).astype(BF16)


def attn_bwd_body(m, rl, qkv, n1, a, dqkv, gb, da):
    rows = n1.shape[0]
    cols = m.shape[0]
    marks = head_rows(cols)
    da[...] = dot_nt(rl[...], m[...]).astype(BF16)
    for i in range(rows // WIN):
        at = slice(i * WIN, (i + 1) * WIN)
        q, k, v, d = qkv[0, at, :], qkv[1, at, :], qkv[2, at, :], da[at, :]
        dq = dk = dv = None
        for mark in marks:
            qm, dm = q * mark, d * mark
            p = softmax(dot_nt(qm, k))
            dp = dot_nt(dm, v)
            ds = (p * (dp - jnp.sum(p * dp, axis=-1, keepdims=True))).astype(BF16)
            parts = dot(ds, k * mark), dot_tn(ds, qm), dot_tn(p.astype(BF16), dm)
            if dq is None:
                dq, dk, dv = parts
            else:
                dq, dk, dv = dq + parts[0], dk + parts[1], dv + parts[2]
        dqkv[0, at, :] = (dq * SCALE).astype(BF16)
        dqkv[1, at, :] = (dk * SCALE).astype(BF16)
        dqkv[2, at, :] = dv.astype(BF16)
    begin(dqkv)
    for j in range(3):
        part = dqkv[j]
        a[j * cols : (j + 1) * cols, :] = dot_tn(part, n1[...]).astype(BF16)
        if j != 1:
            gb[:, (j // 2) * cols : (j // 2 + 1) * cols] = jnp.sum(
                part.astype(F32), axis=0, keepdims=True
            )


def project_body(slots, *refs):
    parts, ws, g = refs[:slots], refs[slots : 2 * slots], refs[-1]
    cols = ws[0].shape[0] // 3
    for s in range(slots):
        total = None
        for j in range(3):
            part = dot(parts[s][j], ws[s][j * cols : (j + 1) * cols, :])
            total = part if total is None else total + part
        g[...] = total if s == 0 else g[...] + total


def last_body(vecs, msk, g, tok, rg, out, sums):
    rows, width = tok.shape
    end = out
    msk, tok, rg, out = (ready(t) for t in (msk, tok, rg, out))

    def body(at):
        chosen = msk[at, 0:1]
        hat, scale = normalize(mix(chosen, vecs[0:1, :], tok[at, :]))
        grad = g[at, :]
        full = rg[at, :] + norm_back(grad, vecs[1:2, :], hat, scale)
        out[at, :] = jnp.where(chosen > 0.5, 0.0, full)
        return (jnp.where(chosen > 0.5, full, 0.0), grad * hat, grad)

    for i, total in enumerate(row_loop(rows, width, 3, body)):
        sums[i : i + 1, :] = total


def pack_body(gb_a, gb_b, a0, a1, a2, a3, sums1, sums2, gdb, keep, give):
    n = a0.shape[1]
    for out, rows in ((keep, ((gb_a, 0, a0), (gb_b, 0, a2))), (give, ((gb_a, 1, a1), (gb_b, 1, a3)))):
        out[...] = jnp.zeros_like(out)
        out[0:3, :] = sums1[...]
        out[3:6, :] = sums2[...]
        out[6:7, :] = gdb[...]
        for i, (gb, row, ab) in enumerate(rows):
            out[7 + 2 * i : 8 + 2 * i, :] = gb[row : row + 1, :]
            out[8 + 2 * i : 9 + 2 * i, 0:n] = ab[...]


def pick_body(keep_in, got, keep, give):
    total = keep_in[...] + got[...]
    keep[...] = total[0:9, :]
    give[0:7, :] = total[0:7, :]
    give[7:9, :] = total[9:11, :]


def plus_body(a, b, out):
    out[...] = a[...] + b[...]


def cut_body(n, *refs):
    ins, outs, sem = refs[:n], refs[n : 2 * n], refs[-1]
    pick = Position().mixed()
    copies = []
    for i, (src, dst) in enumerate(zip(ins, outs)):
        half = dst.shape[0]
        at = pl.ds(pl.multiple_of(pick * half, half), half)
        copies.append(pltpu.make_async_copy(src.at[at], dst, sem.at[i]))
        copies[-1].start()
    for c in copies:
        c.wait()


def swap(links, v, *moves):
    n_dp, n_tensor = links
    moves = moves * (2 // len(moves))
    pairs = []
    for d in range(n_dp):
        for t in range(n_tensor):
            fd, ft = moves[t % 2]
            pairs.append((d * n_tensor + t, (d ^ fd) * n_tensor + (t ^ ft)))
    return lax.ppermute(v, ("dp", "tensor"), pairs)


CORE, ACROSS = (0, 1), (0, 2)
DP0, DP1, DP2 = (1, 0), (2, 0), (4, 0)


def add_rows(a, b, at):
    return a[at, :].astype(F32) + b[at, :].astype(F32)


def stage1_body(*refs):
    groups, (give, keep, own) = refs[:-3], refs[-3:]
    here = Position()
    y, lead = here.bit(0), here.core == 0
    total, low = keep.shape[0], 0
    for p0, p2, r1, r3 in zip(*[iter(groups)] * 4):
        n = p0.shape[0] // 2
        add_group(y, lead, p0, p2, r1, r3, n, low, total, give, keep, own)
        low += n


def add_group(y, lead, p0, p2, r1, r3, n, low, total, give, keep, own):
    at, later = slice(low, low + n), slice(total + low, total + low + n)
    first, other = (pl.ds(pl.multiple_of(k * n, n), n) for k in (y, 1 - y))
    near, far = add_rows(p0, r1, other), add_rows(p2, r3, first)
    give[at, :] = jnp.where(lead, far, near).astype(BF16)
    keep[at, :] = jnp.where(lead, near, far)
    give[later, :] = add_rows(p2, r3, other).astype(BF16)
    own[at, :] = add_rows(p0, r1, first)


def pass_body(keep, got, give):
    n = keep.shape[0]
    give[...] = (keep[...] + got[n:, :].astype(F32)).astype(BF16)


def stage3_body(own_in, got1, got2, give, own, v):
    here = Position()
    n = own.shape[0]
    v[...] = own_in[...] + got1[: 2 * n, :].astype(F32) + got2[...].astype(F32)
    mine = here.half()
    take = lambda k: v[pl.ds(pl.multiple_of(k * n, n), n), :]
    give[...] = take(1 - mine).astype(BF16)
    own[...] = take(mine)


def stage4_body(own, got, give):
    give[...] = (own[...] + got[...].astype(F32)).astype(BF16)


def sum_body(a, b, w):
    w[...] = (a[...].astype(F32) + b[...].astype(F32)).astype(BF16)


def stack_body(a, b, out):
    n = a.shape[0]
    out[:n, :] = a[...]
    out[n:, :] = b[...]


def place_body(turned, w, r1, r2, *refs):
    outs, target = refs[:-1], refs[-1]
    here = Position()
    block = w.shape[0]
    lead = here.core == 0
    i = 0
    for part in (w, r1, r2):
        for k in range(part.shape[0] // block):
            y = jnp.where(lead, i % 2, i // 2)
            z = jnp.where(lead, i // 2, i % 2)
            at = lax.rem(y + here.bit(0), 2) * 2 + lax.rem(z + here.half(), 2)
            target[pl.ds(pl.multiple_of(at * block, block), block), :] = part[
                k * block : (k + 1) * block, :
            ].astype(F32)
            i += 1
    low, half = 0, target.shape[0] // 2
    for out in outs:
        n = out.shape[0] // 2
        if turned:
            out[...] = target[...].T
        else:
            out[:n, :] = target[low : low + n, :]
            out[n:, :] = target[half + low : half + low + n, :]
            low += n
        begin(out)


class Reduce:
    def __init__(self, links, chain, *groups):
        self.links, self.chain, self.parts = links, chain, []
        for p0, p1, p2, p3 in groups:
            self.parts += [p0, p2, swap(links, p1, CORE), swap(links, p3, CORE)]
        self.sizes = [g[0].shape[0] for g in groups]
        self.rows, self.width = sum(self.sizes), groups[0][0].shape[1]

    def swap(self, *moves):
        self.got = swap(self.links, self.give, *moves)

    def stage1(self):
        n = self.rows // 2
        half = ((n, self.width), F32)
        self.give, self.keep, self.own = self.chain(
            stage1_body, self.parts, [((2 * n, self.width), BF16), half, half], "add1", 3
        )
        self.swap(ACROSS, DP0)

    def stage2(self):
        self.first = self.got
        (self.give,) = self.chain(
            pass_body, (self.keep, self.got), [(self.keep.shape, BF16)], "add2", 1
        )
        self.swap(DP0, ACROSS)

    def stage3(self):
        n = self.rows // 4
        self.give, self.own = self.chain(
            stage3_body,
            (self.own, self.first, self.got),
            [((n, self.width), BF16), ((n, self.width), F32)],
            "add3",
            1.5,
            scratch=[pltpu.VMEM((2 * n, self.width), F32)],
        )
        self.swap(DP1, DP2)

    def stage4(self):
        shape = ((self.rows // 4, self.width), BF16)
        (self.give,) = self.chain(stage4_body, (self.own, self.got), [shape], "add4", 1)
        self.swap(DP2, DP1)

    def spread1(self):
        shape = ((self.rows // 4, self.width), BF16)
        i = 3
        while (1 << i) < self.links[0]:
            both = self.give.astype(F32) + self.got.astype(F32)
            self.give = both.astype(BF16)
            self.swap((1 << i, 0))
            i += 1
        (self.give,) = self.chain(sum_body, (self.give, self.got), [shape], "add5", 1)
        self.swap(DP0, DP2)
        self.parts = [self.give, self.got]

    def spread2(self):
        n, width = self.give.shape
        (self.give,) = self.chain(
            stack_body, (self.give, self.got), [((2 * n, width), BF16)], "stack", 1
        )
        self.swap(DP1, DP0)
        self.parts.append(self.got)

    def place(self, turned=False):
        shapes = [(self.width, self.rows)] if turned else [(n, self.width) for n in self.sizes]
        return self.chain(
            functools.partial(place_body, turned),
            self.parts,
            [Early(shape, F32) for shape in shapes],
            "place",
            2,
            scratch=[pltpu.VMEM((self.rows, self.width), F32)],
        )


class PlainReduce(Reduce):
    def stage1(self):
        self.totals = []
        for i in range(0, len(self.parts), 4):
            p0, p2, r1, r3 = (v.astype(F32) for v in self.parts[i : i + 4])
            far = swap(self.links, (p2 + r3).astype(BF16), ACROSS).astype(F32)
            self.totals.append(lax.psum(p0 + r1 + far, "dp"))

    def skip(self):
        pass

    stage2 = stage3 = stage4 = spread1 = spread2 = skip

    def place(self, turned=False):
        return [self.totals[0].T] if turned else self.totals


class Gather:
    def __init__(self, links, v):
        self.links, self.own = links, v
        self.near = swap(links, v, CORE)

    def send(self, half):
        self.half = swap(self.links, half, ACROSS)

    def spread(self):
        self.rest = swap(self.links, self.half, DP0, DP1)
        self.half_near = swap(self.links, self.half, CORE)

    def share(self):
        self.rest_near = swap(self.links, self.rest, CORE)

    def slots(self):
        turn = lambda: Position().mixed()
        rest_near = self.rest_near
        return [
            self.own,
            self.near,
            Stack(self.half, self.rest, turn=turn),
            Stack(self.half_near, rest_near, turn=turn),
        ]


class PlainGather(Gather):
    def send(self, half):
        self.far = swap(self.links, self.own, ACROSS)

    def spread(self):
        pass

    def share(self):
        pass

    def slots(self):
        return [self.own, self.near, self.far, swap(self.links, self.far, CORE)]


def per_device(
    n_dp,
    n_tensor,
    tokens,
    mask_bits,
    cotangent,
    mask_vector,
    first_gain,
    first_shift,
    attn_weight,
    attn_bias,
    merge_weight,
    merge_bias,
    second_gain,
    second_shift,
    up_weight,
    up_bias,
    down_weight,
    down_bias,
):
    rows, width = tokens.shape
    cols = attn_weight.shape[2]
    hidden = up_weight.shape[1]
    row = lambda v: v[None, :]
    links = (n_dp, n_tensor)
    power = n_dp >= 8 and n_dp & (n_dp - 1) == 0
    chain = Chain()
    make = functools.partial(Reduce if power else PlainReduce, links, chain)
    gather = functools.partial(PlainGather if n_dp % 4 else Gather, links)
    wide, tall, low = ((rows, width), F32), ((width, rows), BF16), ((rows, width), BF16)
    qkv_shape, att_shape = ((3, rows, cols), BF16), ((rows, cols), BF16)

    some_bias = lambda i, js: jnp.concatenate([biases[j][i : i + 1] for j in js])
    flat = jnp.transpose(attn_weight, (1, 2, 0)).reshape(3 * cols, width)
    g_attn, g_up, g_down = (gather(w) for w in (flat, up_weight, down_weight))
    g_merge = PlainGather(links, merge_weight)

    def cut(*weights):
        return chain(
            functools.partial(cut_body, len(weights)),
            [Raw(w) for w in weights],
            [((w.shape[0] // 2, w.shape[1]), BF16) for w in weights],
            "cut",
            1.5,
            scratch=[pltpu.SemaphoreType.DMA((len(weights),))],
            stack=57,
        )

    g_attn.send(*cut(flat))
    g_merge.send(None)
    for gat, part in zip((g_up, g_down), cut(up_weight, down_weight)):
        gat.send(part)

    msk, vecs, bias = chain(
        setup_body,
        (mask_bits, up_bias, attn_bias, mask_vector, first_gain, first_shift, merge_bias)
        + (second_gain, second_shift, down_bias),
        [((rows, 8), F32), ((7, width), F32), ((2, hidden), F32)],
        "setup",
        1,
    )
    bias_near, bias_far = swap(links, bias, CORE), swap(links, bias, ACROSS)
    biases = [bias, bias_near, bias_far, swap(links, bias_far, CORE)]

    def hold(*arrays):
        return chain(copy_body, arrays, [(v.shape, v.dtype) for v in arrays], "hold", 0.7)

    def spread(gat):
        if n_dp % 4 == 0:
            (gat.half,) = hold(gat.half)
        gat.spread()

    def share(gat):
        if n_dp % 4 == 0:
            (gat.rest,) = hold(gat.rest)
        gat.share()

    n1, top, topt, gdb = chain(
        prep_body,
        (vecs, msk, tokens, cotangent),
        [low, low, Early(*tall), ((1, width), F32)],
        "prep",
        4,
    )
    spread(g_attn)

    def attn_fwd(js, ws, us):
        r = chain(
            functools.partial(attn_fwd_body, 2),
            (n1, some_bias(1, js), *ws),
            [Early(*qkv_shape), att_shape] * 2,
            "attn_fwd",
            us,
        )
        return r[0::2], r[1::2]

    qkv_a, att_a = attn_fwd((0, 1), (flat, g_attn.near), 6)
    if n_dp % 4 == 0:
        g_attn.rest, g_merge.far = hold(g_attn.rest, g_merge.far)
    g_attn.share()
    wa = g_attn.slots()
    wm = g_merge.slots()
    qkv_b, att_b = attn_fwd((2, 3), wa[2:], 0.5)
    qkv, att = qkv_a + qkv_b, att_a + att_b
    spread(g_up)
    res, n2, n2t = chain(
        functools.partial(mid_body, 4),
        (vecs, msk, tokens, *att, *wm),
        [Early(*wide), low, tall],
        "mid",
        5.5,
    )

    def ffn_up(js, ups):
        r = chain(
            functools.partial(ffn_up_body, len(js)),
            (some_bias(0, js), n2, Late(topt), *ups),
            [((rows, hidden), BF16), ((rows, hidden), BF16), ((width, hidden), BF16)] * len(js),
            "ffn_up",
            2.75 * len(js),
        )
        return r[0::3], r[1::3], r[2::3]

    act_a, slope_a, gd_a = ffn_up((0, 1), (up_weight, g_up.near))
    share(g_up)
    spread(g_down)
    wu = g_up.slots()
    act_b, slope_b, gd_b = ffn_up((2, 3), wu[2:])
    red_d = make((*gd_a, *gd_b))

    share(g_down)
    pg = [pltpu.VMEM((rows, hidden), BF16)]
    grad_up = ((width, hidden), BF16)
    *gu_a, y, g, gb_a = chain(
        functools.partial(ffn_back_body, 2, True),
        (top, n2t, down_weight, g_down.near, *slope_a, *act_a, up_weight, g_up.near),
        [grad_up] * 2 + [wide, wide, ((2, hidden), F32)],
        "ffn_back",
        9,
        scratch=pg,
    )
    wd = g_down.slots()
    red_d.stage1()
    *gu_b, y, g, gb_b = chain(
        functools.partial(ffn_back_body, 2, False),
        (top, n2t, *wd[2:], *slope_b, *act_b, *wu[2:], y, g),
        [grad_up] * 2 + [wide, wide, ((2, hidden), F32)],
        "ffn_back",
        9,
        scratch=pg,
        alias=((y, 2), (g, 3)),
    )
    *gm, layer_out, res_grad, res_low, sums2 = chain(
        turn_body,
        (vecs, Late(res), y, g, top, *att),
        [((cols, width), BF16)] * 4 + [Early(*low), Early(*wide), low, ((3, width), F32)],
        "turn",
        5,
    )
    red_u = make((*gu_a, *gu_b), gm)
    red_d.stage2()

    def attn_bwd(j):
        return chain(
            attn_bwd_body,
            (wm[j], res_low, Late(qkv[j]), Late(n1)),
            [((3 * cols, width), BF16), Early(*qkv_shape), ((1, 2 * cols), F32)],
            "attn_bwd",
            7,
            scratch=[pltpu.VMEM((rows, cols), BF16)],
        )

    back = [None] * 4
    back[1] = attn_bwd(1)
    red_u.stage1()
    red_d.stage3()
    back[3] = attn_bwd(3)
    red_d.stage4()
    back[2] = attn_bwd(2)
    red_u.stage2()
    red_d.spread1()
    back[0] = attn_bwd(0)
    red_a = make([b[0] for b in back])
    red_a.stage1()
    red_u.stage3()
    red_d.spread2()
    (g,) = chain(
        functools.partial(project_body, 4), (*[Late(b[1]) for b in back], *wa), [wide], "project", 6
    )
    red_a.stage2()
    red_u.stage4()
    grad_tokens, sums1 = chain(
        last_body,
        (vecs, msk, g, Late(tokens), Late(res_grad)),
        [Early(*wide), ((3, width), F32)],
        "last",
        8,
    )
    nv = 7
    small = (gb_a, gb_b, *[b[2] for b in back], sums1, sums2, gdb)
    vector = ((nv + 2, width), F32)
    red_a.stage3()
    keep, give = chain(pack_body, small, [((11, width), F32)] * 2, "pack", 0.7)
    got = swap(links, give, CORE)
    red_u.spread1()
    keep, give = chain(pick_body, (keep, got), [vector] * 2, "pick", 0.7)
    got = swap(links, give, ACROSS)
    red_a.stage4()
    (mine,) = chain(plus_body, (keep, got), [vector], "plus", 0.7)
    if power:
        bits = [1 << i for i in range(n_dp.bit_length() - 1)]
    else:
        mine, bits = lax.psum(mine, "dp"), []

    def begin_vector():
        return swap(links, mine, (bits[0], 0)) if bits else None

    def end_vector(got):
        if not bits:
            return mine
        bits.pop(0)
        return chain(plus_body, (mine, got), [vector], "plus", 0.7)[0]

    got = begin_vector()
    red_u.spread2()
    red_a.spread1()
    mine = end_vector(got)
    got = begin_vector()
    (sum_d,) = red_d.place(turned=True)
    red_a.spread2()
    mine = end_vector(got)
    while bits:
        mine = end_vector(begin_vector())
    sum_u, sum_m = red_u.place()
    (sum_a,) = red_a.place()
    grad_attn = jnp.transpose(sum_a.reshape(3, cols, width), (2, 0, 1))
    return (
        layer_out,
        grad_tokens,
        mine[0],
        mine[1],
        mine[2],
        grad_attn,
        mine[nv + 1, : 2 * cols].reshape(2, cols),
        sum_m,
        mine[5],
        mine[3],
        mine[4],
        sum_u,
        mine[nv],
        sum_d,
        mine[6],
    )


def solution(mesh):
    split = P(("dp", "tensor"), None)
    return jax.shard_map(
        functools.partial(per_device, mesh.shape["dp"], mesh.shape["tensor"]),
        mesh=mesh,
        in_specs=(
            split,
            P(("dp", "tensor")),
            split,
            P(),
            P(),
            P(),
            P(None, None, "tensor"),
            P(None, "tensor"),
            P("tensor", None),
            P(),
            P(),
            P(),
            P(None, "tensor"),
            P("tensor"),
            P("tensor", None),
            P(),
        ),
        out_specs=(
            split,
            split,
            P(),
            P(),
            P(),
            P(None, None, "tensor"),
            P(None, "tensor"),
            P("tensor", None),
            P(),
            P(),
            P(),
            P(None, "tensor"),
            P("tensor"),
            P("tensor", None),
            P(),
        ),
        check_vma=False,
    )
```

```python
import functools

import jax
import jax.numpy as jnp
from jax import lax
from jax.experimental import pallas as pl
from jax.experimental.pallas import tpu as pltpu
from jax.sharding import PartitionSpec as P

HEAD = 64
WIN = 256
EPS = 1e-06
SCALE = HEAD**-0.5
ROWS = 64
F32 = jnp.float32
BF16 = jnp.bfloat16


def dot(a, b):
    return lax.dot_general(a, b, (((1,), (0,)), ((), ())), preferred_element_type=F32)


def dot_nt(a, b):
    return lax.dot_general(a, b, (((1,), (1,)), ((), ())), preferred_element_type=F32)


def dot_tn(a, b):
    return lax.dot_general(a, b, (((0,), (0,)), ((), ())), preferred_element_type=F32)


class Stack:
    space = pltpu.VMEM

    def __init__(self, *parts, turn=None):
        self.parts, self.turn = parts, turn
        self.shape = (sum(p.shape[0] for p in parts), *parts[0].shape[1:])
        self.dtype = parts[0].dtype


class Late(Stack):
    space = pl.ANY


class Raw:
    def __init__(self, array):
        self.array = array


class Tile:
    def __init__(self, ref, copies=(), fills=(), out=False):
        self.ref, self.copies, self.fills, self.out, self.sent = ref, copies, fills, out, False
        self.shape, self.dtype = ref.shape, ref.dtype

    def start(self):
        for c in self.copies:
            c.start()
        self.sent = True

    def wait(self):
        for c in self.copies:
            c.wait()
        for at, part in self.fills:
            self.ref[at, :] = part[...]
        self.copies = self.fills = ()
        return self.ref

    def ready(self):
        return self.ref if self.out else self.wait()

    def __getitem__(self, at):
        return self.ready()[at]

    def __setitem__(self, at, value):
        self.ref[at] = value


class Position:
    def __init__(self):
        self.dp = lax.axis_index("dp")
        self.core = lax.rem(lax.axis_index("tensor"), 2)

    def bit(self, i):
        return lax.rem(lax.div(self.dp, 1 << i), 2)

    def mixed(self):
        return lax.rem(self.bit(0) + self.bit(1), 2)

    def half(self):
        return jnp.where(self.core == 0, self.bit(1), self.bit(2))


class Early:
    def __init__(self, shape, dtype):
        self.array = (shape, dtype)


def size(shape, dtype):
    shape = (*shape[:-1], -(-shape[-1] // 128) * 128)
    return functools.reduce(lambda a, b: a * b, shape) * jnp.dtype(dtype).itemsize


class Chain:
    def __init__(self):
        self.last = None

    def __call__(self, body, args, outs, name, us, scratch=(), stack=7, alias=()):
        arrays, in_specs, bufs, n_sem = [], [], [], 0
        spec = lambda space: pl.BlockSpec(memory_space=space)
        for a in args:
            if isinstance(a, Stack):
                arrays += a.parts
                in_specs += [spec(a.space)] * len(a.parts)
                bufs.append((a.shape, a.dtype))
                n_sem += isinstance(a, Late)
            else:
                raw = isinstance(a, Raw)
                arrays.append(a.array if raw else a)
                in_specs.append(spec(pltpu.HBM if raw else pltpu.VMEM))
        shapes, out_specs = [], []
        for o in outs:
            raw, early = isinstance(o, Raw), isinstance(o, Early)
            o = o.array if raw or early else o
            shapes.append(jax.ShapeDtypeStruct(*o))
            out_specs.append(spec(pltpu.HBM if raw or early else pltpu.VMEM))
            if early:
                bufs.append(o)
                n_sem += 1
        order = () if self.last is None else (self.last,)
        n_in, n_out, n_buf = len(arrays), len(shapes), len(bufs)

        def kernel(*refs):
            ins = list(refs[:n_in])
            refs = refs[n_in + len(order) :]
            results, refs = list(refs[:n_out]), refs[n_out:]
            spare, refs = list(refs[:n_buf]), refs[n_buf:]
            sems = refs[0] if n_sem else None
            extra = refs[1:] if n_sem else refs
            used = iter(range(n_sem))
            tiles = []
            for a in args:
                if isinstance(a, Stack):
                    buf, at, copies, fills = spare.pop(0), 0, [], []
                    if isinstance(a, Late):
                        copies.append(pltpu.make_async_copy(ins.pop(0), buf, sems.at[next(used)]))
                    else:
                        for part in a.parts:
                            n, row = part.shape[0], at
                            if a.turn is not None:
                                row = pl.multiple_of(jnp.where(a.turn() == 0, at, n - at), n)
                            fills.append((pl.ds(row, n), ins.pop(0)))
                            at += n
                    tiles.append(Tile(buf, copies, fills))
                    tiles[-1].start()
                else:
                    tiles.append(ins.pop(0))
            sends = []
            for o, r in zip(outs, results):
                if isinstance(o, Early):
                    buf = spare.pop(0)
                    copy = pltpu.make_async_copy(buf, r, sems.at[next(used)])
                    tiles.append(Tile(buf, [copy], out=True))
                    sends.append(tiles[-1])
                else:
                    tiles.append(r)
            body(*tiles, *extra)
            for t in sends:
                if not t.sent:
                    t.start()
            for t in tiles:
                if isinstance(t, Tile):
                    t.wait()

        room = sum(size(*b) for b in bufs)
        room += sum(size(m.shape, m.dtype) for m in scratch if m.memory_space == pltpu.VMEM)
        result = pl.pallas_call(
            kernel,
            out_shape=tuple(shapes),
            in_specs=in_specs + [spec(pl.ANY)] * len(order),
            out_specs=tuple(out_specs),
            input_output_aliases={
                next(i for i, a in enumerate(arrays) if a is v): o for v, o in alias
            },
            scratch_shapes=[pltpu.VMEM(*b) for b in bufs]
            + ([pltpu.SemaphoreType.DMA((n_sem,))] if n_sem else [])
            + list(scratch),
            compiler_params=pltpu.CompilerParams(vmem_limit_bytes=(stack << 20) + room),
            cost_estimate=pl.CostEstimate(
                flops=int(us * COST), bytes_accessed=1024, transcendentals=0
            ),
            name=name,
        )(*arrays, *order)
        self.last = result[0]
        return list(result)


def ready(t):
    return t.ready() if isinstance(t, Tile) else t


def begin(*tiles):
    for t in tiles:
        if isinstance(t, Tile):
            t.start()


COST = 1.15e9
TINY = 0.7


def row_loop(rows, width, sums, body):
    def step(i, carry):
        at = pl.ds(pl.multiple_of(i * ROWS, ROWS), ROWS)
        parts = body(at)
        return tuple(
            c + jnp.sum(p.reshape(ROWS // 8, 8, width), axis=0) for c, p in zip(carry, parts)
        )

    zero = tuple(jnp.zeros((8, width), F32) for _ in range(sums))
    done = lax.fori_loop(0, rows // ROWS, step, zero)
    return [jnp.sum(c, axis=0, keepdims=True) for c in done]


def normalize(v):
    centre = v - jnp.mean(v, axis=-1, keepdims=True)
    scale = lax.rsqrt(jnp.mean(centre * centre, axis=-1, keepdims=True) + EPS)
    return centre * scale, scale


def mix(chosen, vector, tokens):
    return jnp.where(chosen > 0.5, vector, tokens.astype(F32))


def setup_body(mask, hidden_bias, attn_bias, *refs):
    params, (msk, vecs, bias) = refs[:-3], refs[-3:]
    line = mask[...].astype(F32).reshape(1, mask.shape[0])
    msk[...] = jnp.broadcast_to(line, (8, mask.shape[0])).T
    for i, p in enumerate(params):
        vecs[i : i + 1, :] = p[...].reshape(1, p.shape[0])
    n = attn_bias.shape[1]
    bias[...] = jnp.zeros_like(bias)
    bias[0:1, :] = hidden_bias[...].reshape(1, hidden_bias.shape[0])
    bias[1:2, 0:n] = attn_bias[0:1, :]
    bias[1:2, n : 2 * n] = attn_bias[1:2, :]


def prep_body(vecs, msk, tok, cot, n1, top, topt, gdb):
    rows, width = tok.shape

    def body(at):
        chosen = msk[at, 0:1]
        hat, _ = normalize(mix(chosen, vecs[0:1, :], tok[at, :]))
        n1[at, :] = (hat * vecs[1:2, :] + vecs[2:3, :]).astype(BF16)
        grad = jnp.where(chosen > 0.5, cot[at, :].astype(F32), 0.0)
        top[at, :] = grad.astype(BF16)
        return (grad,)

    (total,) = row_loop(rows, width, 1, body)
    gdb[...] = total
    topt[...] = top[...].T


def copy_body(*refs):
    n = len(refs) // 2
    for src, dst in zip(refs[:n], refs[n:]):
        dst[...] = src[...]


def head_rows(cols):
    lane = lax.broadcasted_iota(jnp.int32, (1, cols), 1)
    return [
        ((lane >= h * HEAD) & (lane < (h + 1) * HEAD)).astype(F32).astype(BF16)
        for h in range(cols // HEAD)
    ]


def softmax(raw):
    peak = jnp.max(raw, axis=-1, keepdims=True)
    e = jnp.exp((raw - peak) * SCALE)
    return e * (1.0 / jnp.sum(e, axis=-1, keepdims=True))


def attn_fwd_body(slots, n1, bias, *refs):
    ins, outs = refs[:slots], refs[slots:]
    rows = n1.shape[0]
    cols = ins[0].shape[0] // 3
    marks = head_rows(cols)
    for s in range(slots):
        w, qkv, att = ins[s], outs[2 * s], outs[2 * s + 1]
        for j in range(3):
            y = dot_nt(n1[...], w[j * cols : (j + 1) * cols, :])
            if j != 1:
                y = y + bias[s : s + 1, (j // 2) * cols : (j // 2 + 1) * cols]
            qkv[j] = y.astype(BF16)
        begin(qkv)
        for i in range(rows // WIN):
            at = slice(i * WIN, (i + 1) * WIN)
            q, k, v = qkv[0, at, :], qkv[1, at, :], qkv[2, at, :]
            out = None
            for mark in marks:
                part = dot(softmax(dot_nt(q * mark, k)).astype(BF16), v * mark)
                out = part if out is None else out + part
            att[at, :] = out.astype(BF16)


def mid_body(slots, vecs, msk, tok, *refs):
    atts, merges = refs[:slots], refs[slots : 2 * slots]
    res, n2, n2t = refs[2 * slots :]
    rows, width = tok.shape
    total = dot(atts[0][...], merges[0][...])
    for s in range(1, slots):
        total = total + dot(atts[s][...], merges[s][...])
    res[...] = total
    out = res
    msk, tok, res, n2 = (ready(t) for t in (msk, tok, res, n2))

    def body(at):
        r = mix(msk[at, 0:1], vecs[0:1, :], tok[at, :]) + res[at, :] + vecs[3:4, :]
        res[at, :] = r
        hat, _ = normalize(r)
        n2[at, :] = (hat * vecs[4:5, :] + vecs[5:6, :]).astype(BF16)
        return ()

    row_loop(rows, width, 0, body)
    begin(out)
    n2t[...] = n2[...].T


GELU_C = 0.7978845608028654
GELU_A = 0.044715


def ffn_up_body(slots, bias, n2, topt, *refs):
    ups, outs = refs[:slots], refs[slots:]
    hidden = ups[0].shape[1]
    tile = 256
    for s in range(slots):
        act, slope, gd = outs[3 * s : 3 * s + 3]
        for t in range(hidden // tile):
            c = slice(t * tile, (t + 1) * tile)
            pre = dot(n2[...], ups[s][:, c]) + bias[s : s + 1, c]
            sq = pre * pre
            th = jnp.tanh(GELU_C * (pre + GELU_A * (sq * pre)))
            half = 0.5 * (1.0 + th)
            a = (pre * half).astype(BF16)
            rise = half + (0.5 * GELU_C) * pre * (1.0 - th * th) * (1.0 + (3.0 * GELU_A) * sq)
            act[:, c] = a
            slope[:, c] = rise.astype(BF16)
            gd[:, c] = dot(topt[...], a).astype(BF16)
        begin(gd, act, slope)


def ffn_back_body(slots, first, top, n2t, *refs):
    downs, slopes, acts, ups = (refs[i * slots : (i + 1) * slots] for i in range(4))
    refs = refs[4 * slots :]
    if first:
        gus, (y, g, gb, pg) = refs[:slots], refs[slots:]
    else:
        y_in, g_in = refs[:2]
        gus, (y, g, gb, pg) = refs[2 : 2 + slots], refs[2 + slots :]
    hidden = ups[0].shape[1]
    tile = 256
    for s in range(slots):
        for t in range(hidden // tile):
            c = slice(t * tile, (t + 1) * tile)
            low = (dot_nt(top[...], downs[s][c, :]) * slopes[s][:, c].astype(F32)).astype(BF16)
            pg[:, c] = low
            gb[s : s + 1, c] = jnp.sum(low.astype(F32), axis=0, keepdims=True)
            gus[s][:, c] = dot(n2t[...], low).astype(BF16)
        begin(gus[s])
        yp = dot(acts[s][...], downs[s][...])
        gp = dot_nt(pg[...], ups[s][...])
        if s == 0 and first:
            y[...] = yp
            g[...] = gp
        elif s == 0:
            y[...] = y_in[...] + yp
            g[...] = g_in[...] + gp
        else:
            y[...] = y[...] + yp
            g[...] = g[...] + gp


def norm_back(grad, gain, hat, scale):
    e = grad * gain
    back = e - jnp.mean(e, axis=-1, keepdims=True)
    return scale * (back - hat * jnp.mean(e * hat, axis=-1, keepdims=True))


def turn_body(vecs, res, y, g, top, *refs):
    slots = len(refs) // 2 - 2
    atts, gms, (out, rg, rl, sums) = refs[:slots], refs[slots : 2 * slots], refs[2 * slots :]
    rows, width = res.shape
    ends = (rg, out)
    res, out, rg, top = (ready(t) for t in (res, out, rg, top))

    def body(at):
        r = res[at, :]
        out[at, :] = (r + y[at, :] + vecs[6:7, :]).astype(BF16)
        hat, scale = normalize(r)
        grad = g[at, :]
        full = top[at, :].astype(F32) + norm_back(grad, vecs[4:5, :], hat, scale)
        rg[at, :] = full
        rl[at, :] = full.astype(BF16)
        return (grad * hat, grad, full)

    for i, total in enumerate(row_loop(rows, width, 3, body)):
        sums[i : i + 1, :] = total
    begin(*ends)
    for att, gm in zip(atts, gms):
        gm[...] = dot_tn(att[...], rl[...]).astype(BF16)


def stack_heads(x, marks):
    return jnp.concatenate([x * mark for mark in marks], axis=0)


def attn_bwd_body(m, rl, qkv, n1, a, dqt, dkv, gb, da):
    rows = n1.shape[0]
    cols = m.shape[0]
    marks = head_rows(cols)
    da[...] = dot_nt(rl[...], m[...]).astype(BF16)
    for i in range(rows // WIN):
        at = slice(i * WIN, (i + 1) * WIN)
        k = qkv[1, at, :]
        qs, gs = stack_heads(qkv[0, at, :], marks), stack_heads(da[at, :], marks)
        raw = dot_nt(k, qs)
        e = jnp.exp((raw - jnp.max(raw, axis=0, keepdims=True)) * SCALE)
        p = e * (1.0 / jnp.sum(e, axis=0, keepdims=True))
        dp = dot_nt(qkv[2, at, :], gs)
        dkv[1, at, :] = dot(p.astype(BF16), gs).astype(BF16)
        ds = (p * (dp - jnp.sum(p * dp, axis=0, keepdims=True))).astype(BF16)
        dkv[0, at, :] = (dot(ds, qs) * SCALE).astype(BF16)
        kt = k.T
        for h in range(cols // HEAD):
            mine = slice(h * HEAD, (h + 1) * HEAD)
            dq = dot(kt[mine, :], ds[:, h * WIN : (h + 1) * WIN])
            dqt[mine, at] = (dq * SCALE).astype(BF16)
    begin(dkv)
    a[0:cols, :] = dot(dqt[...], n1[...]).astype(BF16)
    gb[:, 0:cols] = dot_nt(jnp.ones((8, rows), BF16), dqt[...])[0:1, :]
    for j in range(2):
        a[(j + 1) * cols : (j + 2) * cols, :] = dot_tn(dkv[j], n1[...]).astype(BF16)
    gb[:, cols : 2 * cols] = jnp.sum(dkv[1].astype(F32), axis=0, keepdims=True)


def project_body(slots, *refs):
    dqs, dkvs, ws = (refs[i * slots : (i + 1) * slots] for i in range(3))
    g = refs[-1]
    cols = ws[0].shape[0] // 3
    for s in range(slots):
        w = ws[s]
        total = dot_tn(dqs[s][...], w[0:cols, :])
        total = total + dot(dkvs[s][0], w[cols : 2 * cols, :])
        total = total + dot(dkvs[s][1], w[2 * cols : 3 * cols, :])
        g[...] = total if s == 0 else g[...] + total


def last_body(vecs, msk, g, tok, rg, out, sums):
    rows, width = tok.shape
    end = out
    msk, tok, rg, out = (ready(t) for t in (msk, tok, rg, out))

    def body(at):
        chosen = msk[at, 0:1]
        hat, scale = normalize(mix(chosen, vecs[0:1, :], tok[at, :]))
        grad = g[at, :]
        full = rg[at, :] + norm_back(grad, vecs[1:2, :], hat, scale)
        out[at, :] = jnp.where(chosen > 0.5, 0.0, full)
        return (jnp.where(chosen > 0.5, full, 0.0), grad * hat, grad)

    for i, total in enumerate(row_loop(rows, width, 3, body)):
        sums[i : i + 1, :] = total


def pack_body(gb_a, gb_b, a0, a1, a2, a3, sums1, sums2, gdb, keep, give):
    n = a0.shape[1]
    for out, rows in ((keep, ((gb_a, 0, a0), (gb_b, 0, a2))), (give, ((gb_a, 1, a1), (gb_b, 1, a3)))):
        out[...] = jnp.zeros_like(out)
        out[0:3, :] = sums1[...]
        out[3:6, :] = sums2[...]
        out[6:7, :] = gdb[...]
        for i, (gb, row, ab) in enumerate(rows):
            out[7 + 2 * i : 8 + 2 * i, :] = gb[row : row + 1, :]
            out[8 + 2 * i : 9 + 2 * i, 0:n] = ab[...]


def pick_body(keep_in, got, keep, give):
    total = keep_in[...] + got[...]
    keep[...] = total[0:9, :]
    give[0:7, :] = total[0:7, :]
    give[7:9, :] = total[9:11, :]


def plus_body(a, b, out):
    out[...] = a[...] + b[...]


def half_body(*refs):
    pick = Position().mixed()
    k = len(refs) // 2
    for src, dst in zip(refs[:k], refs[k:]):
        n = dst.shape[0]
        dst[...] = src[pl.ds(pl.multiple_of(pick * n, n), n), :]


def cut_body(n, *refs):
    ins, outs, sem = refs[:n], refs[n : 2 * n], refs[-1]
    pick = Position().mixed()
    copies = []
    for i, (src, dst) in enumerate(zip(ins, outs)):
        half = dst.shape[0]
        at = pl.ds(pl.multiple_of(pick * half, half), half)
        copies.append(pltpu.make_async_copy(src.at[at], dst, sem.at[i]))
        copies[-1].start()
    for c in copies:
        c.wait()


def swap(links, v, *moves):
    n_dp, n_tensor = links
    moves = moves * (2 // len(moves))
    pairs = []
    for d in range(n_dp):
        for t in range(n_tensor):
            fd, ft = moves[t % 2]
            pairs.append((d * n_tensor + t, (d ^ fd) * n_tensor + (t ^ ft)))
    return lax.ppermute(v, ("dp", "tensor"), pairs)


CORE, ACROSS = (0, 1), (0, 2)
DP0, DP1, DP2 = (1, 0), (2, 0), (4, 0)


def add_rows(a, b, at):
    return a[at, :].astype(F32) + b[at, :].astype(F32)


def stage1_body(p0, p2, r1, r3, give, keep, own):
    here = Position()
    n = p0.shape[0] // 2
    y, lead = here.bit(0), here.core == 0
    first, other = (pl.ds(pl.multiple_of(k * n, n), n) for k in (y, 1 - y))
    near, far = add_rows(p0, r1, other), add_rows(p2, r3, first)
    give[:n, :] = jnp.where(lead, far, near).astype(BF16)
    keep[...] = jnp.where(lead, near, far)
    give[n:, :] = add_rows(p2, r3, other).astype(BF16)
    own[...] = add_rows(p0, r1, first)


def stage2_body(*refs):
    groups, give = refs[:-1], refs[-1]
    low = 0
    for keep, got in zip(groups[::2], groups[1::2]):
        n = keep.shape[0]
        give[low : low + n, :] = (keep[...] + got[n:, :].astype(F32)).astype(BF16)
        low += n


def stage3_body(*refs):
    groups, (got2, give, own, v) = refs[:-4], refs[-4:]
    low = 0
    for mine, got in zip(groups[::2], groups[1::2]):
        n = mine.shape[0]
        at = slice(low, low + n)
        v[at, :] = mine[...] + got[:n, :].astype(F32) + got2[at, :].astype(F32)
        low += n
    n = own.shape[0]
    mine = Position().half()
    take = lambda k: v[pl.ds(pl.multiple_of(k * n, n), n), :]
    give[...] = take(1 - mine).astype(BF16)
    own[...] = take(mine)


def stage4_body(own, got, give):
    give[...] = (own[...] + got[...].astype(F32)).astype(BF16)


def sum_body(a, b, w):
    w[...] = (a[...].astype(F32) + b[...].astype(F32)).astype(BF16)


def stack_body(a, b, out):
    n = a.shape[0]
    out[:n, :] = a[...]
    out[n:, :] = b[...]


def place_body(turned, w, r1, r2, *refs):
    outs, target = refs[:-1], refs[-1]
    here = Position()
    block = w.shape[0]
    lead = here.core == 0
    i = 0
    for part in (w, r1, r2):
        for k in range(part.shape[0] // block):
            y = jnp.where(lead, i % 2, i // 2)
            z = jnp.where(lead, i // 2, i % 2)
            at = lax.rem(y + here.bit(0), 2) * 2 + lax.rem(z + here.half(), 2)
            target[pl.ds(pl.multiple_of(at * block, block), block), :] = part[
                k * block : (k + 1) * block, :
            ].astype(F32)
            i += 1
    low, half = 0, target.shape[0] // 2
    for out in outs:
        n = out.shape[0] // 2
        if turned:
            out[...] = target[...].T
        else:
            out[:n, :] = target[low : low + n, :]
            out[n:, :] = target[half + low : half + low + n, :]
            low += n
        begin(out)


class Reduce:
    def __init__(self, links, chain, p0, p1, p2, p3):
        self.links, self.chain = links, chain
        self.parts = (p0, p2, swap(links, p1, CORE), swap(links, p3, CORE))
        self.rows, self.width = p0.shape
        self.sizes = [self.rows]

    def swap(self, *moves):
        self.got = swap(self.links, self.give, *moves)

    def stage1(self):
        n = self.rows // 2
        half = ((n, self.width), F32)
        self.give, keep, own = self.chain(
            stage1_body, self.parts, [((2 * n, self.width), BF16), half, half], "add1", TINY
        )
        self.swap(ACROSS, DP0)
        self.keeps, self.owns = [(keep, self.got)], [(own, self.got)]

    def join(self, other):
        self.rows += other.rows
        self.sizes += other.sizes
        self.keeps += other.keeps
        self.owns += other.owns

    def stage2(self):
        shape = ((self.rows // 2, self.width), BF16)
        (self.give,) = self.chain(stage2_body, sum(self.keeps, ()), [shape], "add2", TINY)
        self.swap(DP0, ACROSS)

    def stage3(self):
        n = self.rows // 4
        self.give, self.own = self.chain(
            stage3_body,
            (*sum(self.owns, ()), self.got),
            [((n, self.width), BF16), ((n, self.width), F32)],
            "add3",
            TINY,
            scratch=[pltpu.VMEM((2 * n, self.width), F32)],
        )
        self.swap(DP1, DP2)

    def stage4(self):
        shape = ((self.rows // 4, self.width), BF16)
        (self.give,) = self.chain(stage4_body, (self.own, self.got), [shape], "add4", TINY)
        self.swap(DP2, DP1)

    def spread1(self):
        shape = ((self.rows // 4, self.width), BF16)
        i = 3
        while (1 << i) < self.links[0]:
            both = self.give.astype(F32) + self.got.astype(F32)
            self.give = both.astype(BF16)
            self.swap((1 << i, 0))
            i += 1
        (self.give,) = self.chain(sum_body, (self.give, self.got), [shape], "add5", TINY)
        self.swap(DP0, DP2)
        self.parts = [self.give, self.got]

    def spread2(self):
        n, width = self.give.shape
        (self.give,) = self.chain(
            stack_body, (self.give, self.got), [((2 * n, width), BF16)], "stack", TINY
        )
        self.swap(DP1, DP0)
        self.parts.append(self.got)

    def place(self, turned=False):
        shapes = [(self.width, self.rows)] if turned else [(n, self.width) for n in self.sizes]
        return self.chain(
            functools.partial(place_body, turned),
            self.parts,
            [Early(shape, F32) for shape in shapes],
            "place",
            2,
            stack=7,
            scratch=[pltpu.VMEM((self.rows, self.width), F32)],
        )


class PlainReduce(Reduce):
    def stage1(self):
        p0, p2, r1, r3 = (v.astype(F32) for v in self.parts)
        far = swap(self.links, (p2 + r3).astype(BF16), ACROSS).astype(F32)
        self.totals = [lax.psum(p0 + r1 + far, "dp")]

    def join(self, other):
        self.totals += other.totals

    def skip(self):
        pass

    stage2 = stage3 = stage4 = spread1 = spread2 = skip

    def place(self, turned=False):
        return [self.totals[0].T] if turned else self.totals


class VectorSum:
    def __init__(self, links, chain, small, power):
        self.links, self.chain = links, chain
        width = small[-1].shape[1]
        self.shape = ((9, width), F32)
        self.keep, give = chain(pack_body, small, [((11, width), F32)] * 2, "pack", TINY)
        self.got = swap(links, give, CORE)
        bits = links[0].bit_length() - 1
        self.moves = [ACROSS] + [(1 << i, 0) for i in range(bits if power else 0)]
        self.power, self.first = power, True

    def step(self):
        if not self.moves:
            return
        if self.first:
            self.keep, give = self.chain(
                pick_body, (self.keep, self.got), [self.shape] * 2, "pick", TINY
            )
        else:
            self.add()
            give = self.keep
        self.first = False
        self.got = swap(self.links, give, self.moves.pop(0))

    def add(self):
        (self.keep,) = self.chain(plus_body, (self.keep, self.got), [self.shape], "plus", TINY)

    def finish(self):
        while self.moves:
            self.step()
        self.add()
        return self.keep if self.power else lax.psum(self.keep, "dp")


class Gather:
    def __init__(self, links, v):
        self.links, self.own = links, v
        self.near = swap(links, v, CORE)

    def send(self, half):
        self.half = swap(self.links, half, ACROSS)

    def spread(self):
        self.rest = swap(self.links, self.half, DP0, DP1)
        self.half_near = swap(self.links, self.half, CORE)

    def share(self):
        self.rest_near = swap(self.links, self.rest, CORE)

    def slots(self):
        turn = lambda: Position().mixed()
        rest_near = self.rest_near
        return [
            self.own,
            self.near,
            Stack(self.half, self.rest, turn=turn),
            Stack(self.half_near, rest_near, turn=turn),
        ]


class PlainGather(Gather):
    def send(self, half):
        self.far = swap(self.links, self.own, ACROSS)

    def spread(self):
        pass

    def share(self):
        pass

    def slots(self):
        return [self.own, self.near, self.far, swap(self.links, self.far, CORE)]


def per_device(
    n_dp,
    n_tensor,
    tokens,
    mask_bits,
    cotangent,
    mask_vector,
    first_gain,
    first_shift,
    attn_weight,
    attn_bias,
    merge_weight,
    merge_bias,
    second_gain,
    second_shift,
    up_weight,
    up_bias,
    down_weight,
    down_bias,
):
    rows, width = tokens.shape
    cols = attn_weight.shape[2]
    hidden = up_weight.shape[1]
    row = lambda v: v[None, :]
    links = (n_dp, n_tensor)
    power = n_dp >= 8 and n_dp & (n_dp - 1) == 0
    chain = Chain()
    make = functools.partial(Reduce if power else PlainReduce, links, chain)
    gather = functools.partial(PlainGather if n_dp % 4 else Gather, links)
    wide, tall, low = ((rows, width), F32), ((width, rows), BF16), ((rows, width), BF16)
    qkv_shape, att_shape = ((3, rows, cols), BF16), ((rows, cols), BF16)

    some_bias = lambda i, js: jnp.concatenate([biases[j][i : i + 1] for j in js])
    flat = jnp.transpose(attn_weight, (1, 2, 0)).reshape(3 * cols, width)
    g_attn, g_up, g_down = (gather(w) for w in (flat, up_weight, down_weight))
    g_merge = PlainGather(links, merge_weight)

    def cut(*weights):
        return chain(
            functools.partial(cut_body, len(weights)),
            [Raw(w) for w in weights],
            [((w.shape[0] // 2, w.shape[1]), BF16) for w in weights],
            "cut",
            1.5,
            scratch=[pltpu.SemaphoreType.DMA((len(weights),))],
            stack=57,
        )

    g_attn.send(*cut(flat))
    g_merge.send(None)

    msk, vecs, bias = chain(
        setup_body,
        (mask_bits, up_bias, attn_bias, mask_vector, first_gain, first_shift, merge_bias)
        + (second_gain, second_shift, down_bias),
        [((rows, 8), F32), ((7, width), F32), ((2, hidden), F32)],
        "setup",
        1,
    )
    bias_near, bias_far = swap(links, bias, CORE), swap(links, bias, ACROSS)
    biases = [bias, bias_near, bias_far, swap(links, bias_far, CORE)]

    def hold(*arrays):
        return chain(copy_body, arrays, [(v.shape, v.dtype) for v in arrays], "hold", TINY)

    def spread(gat):
        if n_dp % 4 == 0:
            (gat.half,) = hold(gat.half)
        gat.spread()

    def share(gat):
        if n_dp % 4 == 0:
            (gat.rest,) = hold(gat.rest)
        gat.share()

    n1, top, topt, gdb = chain(
        prep_body,
        (vecs, msk, tokens, cotangent),
        [low, low, Early(*tall), ((1, width), F32)],
        "prep",
        4,
    )
    spread(g_attn)
    parts = [((w.shape[0] // 2, w.shape[1]), BF16) for w in (up_weight, down_weight)]
    halves = chain(half_body, (up_weight, down_weight), parts, "half", 0.7)
    g_up.send(halves[0])
    g_down.send(halves[1])

    def attn_fwd(js, ws, us):
        r = chain(
            functools.partial(attn_fwd_body, 2),
            (n1, some_bias(1, js), *ws),
            [Early(*qkv_shape), att_shape] * 2,
            "attn_fwd",
            us,
        )
        return r[0::2], r[1::2]

    qkv_a, att_a = attn_fwd((0, 1), (flat, g_attn.near), 6)
    if n_dp % 4 == 0:
        g_attn.rest, g_merge.far = hold(g_attn.rest, g_merge.far)
    g_attn.share()
    wa = g_attn.slots()
    wm = g_merge.slots()
    qkv_b, att_b = attn_fwd((2, 3), wa[2:], 0.5)
    qkv, att = qkv_a + qkv_b, att_a + att_b
    spread(g_up)
    res, n2, n2t = chain(
        functools.partial(mid_body, 4),
        (vecs, msk, tokens, *att, *wm),
        [Early(*wide), low, tall],
        "mid",
        5.5,
    )

    def ffn_up(js, ups):
        r = chain(
            functools.partial(ffn_up_body, len(js)),
            (some_bias(0, js), n2, Late(topt), *ups),
            [((rows, hidden), BF16), ((rows, hidden), BF16), ((width, hidden), BF16)] * len(js),
            "ffn_up",
            2.75 * len(js),
        )
        return r[0::3], r[1::3], r[2::3]

    act_a, slope_a, gd_a = ffn_up((0, 1), (up_weight, g_up.near))
    share(g_up)
    spread(g_down)
    wu = g_up.slots()
    act_b, slope_b, gd_b = ffn_up((2, 3), wu[2:])
    red_d = make(*gd_a, *gd_b)

    share(g_down)
    pg = [pltpu.VMEM((rows, hidden), BF16)]
    grad_up = ((width, hidden), BF16)
    *gu_a, y, g, gb_a = chain(
        functools.partial(ffn_back_body, 2, True),
        (top, n2t, down_weight, g_down.near, *slope_a, *act_a, up_weight, g_up.near),
        [grad_up] * 2 + [wide, wide, ((2, hidden), F32)],
        "ffn_back",
        9,
        scratch=pg,
    )
    wd = g_down.slots()
    red_d.stage1()
    *gu_b, y, g, gb_b = chain(
        functools.partial(ffn_back_body, 2, False),
        (top, n2t, *wd[2:], *slope_b, *act_b, *wu[2:], y, g),
        [grad_up] * 2 + [wide, wide, ((2, hidden), F32)],
        "ffn_back",
        9,
        scratch=pg,
        alias=((y, 2), (g, 3)),
    )
    red_u = make(*gu_a, *gu_b)
    *gm, layer_out, res_grad, res_low, sums2 = chain(
        turn_body,
        (vecs, Late(res), y, g, top, *att),
        [((cols, width), BF16)] * 4 + [Early(*low), Early(*wide), low, ((3, width), F32)],
        "turn",
        5,
    )
    red_m = make(*gm)
    red_d.stage2()
    red_u.stage1()

    def attn_bwd(j):
        return chain(
            attn_bwd_body,
            (wm[j], res_low, Late(qkv[j]), Late(n1)),
            [((3 * cols, width), BF16), ((cols, rows), BF16), Early((2, rows, cols), BF16)]
            + [((1, 2 * cols), F32)],
            "attn_bwd",
            5,
            scratch=[pltpu.VMEM((rows, cols), BF16)],
        )

    back = [None] * 4
    back[1] = attn_bwd(1)
    red_m.stage1()
    back[3] = attn_bwd(3)
    red_d.stage3()
    back[2] = attn_bwd(2)
    red_u.join(red_m)
    red_u.stage2()
    red_d.stage4()
    back[0] = attn_bwd(0)
    red_a = make(*[b[0] for b in back])
    red_a.stage1()
    red_u.stage3()
    (g,) = chain(
        functools.partial(project_body, 4),
        (*[b[1] for b in back], *[Late(b[2]) for b in back], *wa),
        [wide],
        "project",
        6,
    )
    red_d.spread1()
    red_a.stage2()
    red_u.stage4()
    grad_tokens, sums1 = chain(
        last_body,
        (vecs, msk, g, Late(tokens), Late(res_grad)),
        [Early(*wide), ((3, width), F32)],
        "last",
        8,
        stack=7,
    )
    red_a.stage3()
    small = (gb_a, gb_b, *[b[3] for b in back], sums1, sums2, gdb)
    total = VectorSum(links, chain, small, power)
    red_d.spread2()
    red_u.spread1()
    total.step()
    red_a.stage4()
    total.step()
    red_u.spread2()
    red_a.spread1()
    total.step()
    red_a.spread2()
    (sum_d,) = red_d.place(turned=True)
    total.step()
    sum_u, sum_m = red_u.place()
    mine = total.finish()
    (sum_a,) = red_a.place()
    nv = 7
    grad_attn = jnp.transpose(sum_a.reshape(3, cols, width), (2, 0, 1))
    return (
        layer_out,
        grad_tokens,
        mine[0],
        mine[1],
        mine[2],
        grad_attn,
        mine[nv + 1, : 2 * cols].reshape(2, cols),
        sum_m,
        mine[5],
        mine[3],
        mine[4],
        sum_u,
        mine[nv],
        sum_d,
        mine[6],
    )


def solution(mesh):
    split = P(("dp", "tensor"), None)
    return jax.shard_map(
        functools.partial(per_device, mesh.shape["dp"], mesh.shape["tensor"]),
        mesh=mesh,
        in_specs=(
            split,
            P(("dp", "tensor")),
            split,
            P(),
            P(),
            P(),
            P(None, None, "tensor"),
            P(None, "tensor"),
            P("tensor", None),
            P(),
            P(),
            P(),
            P(None, "tensor"),
            P("tensor"),
            P("tensor", None),
            P(),
        ),
        out_specs=(
            split,
            split,
            P(),
            P(),
            P(),
            P(None, None, "tensor"),
            P(None, "tensor"),
            P("tensor", None),
            P(),
            P(),
            P(),
            P(None, "tensor"),
            P("tensor"),
            P("tensor", None),
            P(),
        ),
        check_vma=False,
    )
```

```python
import functools

import jax
import jax.numpy as jnp
from jax import lax
from jax.experimental import pallas as pl
from jax.experimental.pallas import tpu as pltpu
from jax.sharding import PartitionSpec as P

HEAD = 64
WIN = 256
EPS = 1e-06
SCALE = HEAD**-0.5
ROWS = 256
F32 = jnp.float32
BF16 = jnp.bfloat16


def dot(a, b):
    return lax.dot_general(a, b, (((1,), (0,)), ((), ())), preferred_element_type=F32)


def dot_nt(a, b):
    return lax.dot_general(a, b, (((1,), (1,)), ((), ())), preferred_element_type=F32)


def dot_tn(a, b):
    return lax.dot_general(a, b, (((0,), (0,)), ((), ())), preferred_element_type=F32)


class Stack:
    space = pltpu.VMEM

    def __init__(self, *parts, turn=None):
        self.parts, self.turn = parts, turn
        self.shape = (sum(p.shape[0] for p in parts), *parts[0].shape[1:])
        self.dtype = parts[0].dtype


class Late(Stack):
    space = pl.ANY


class Raw:
    def __init__(self, array):
        self.array = array


class Tile:
    def __init__(self, ref, copies=(), fills=(), out=False):
        self.ref, self.copies, self.fills, self.out, self.sent = ref, copies, fills, out, False
        self.shape, self.dtype = ref.shape, ref.dtype

    def start(self):
        for c in self.copies:
            c.start()
        self.sent = True

    def wait(self):
        for c in self.copies:
            c.wait()
        for at, part in self.fills:
            self.ref[at, :] = part[...]
        self.copies = self.fills = ()
        return self.ref

    def ready(self):
        return self.ref if self.out else self.wait()

    def __getitem__(self, at):
        return self.ready()[at]

    def __setitem__(self, at, value):
        self.ref[at] = value


class Position:
    def __init__(self):
        self.dp = lax.axis_index("dp")
        self.core = lax.rem(lax.axis_index("tensor"), 2)

    def bit(self, i):
        return lax.rem(lax.div(self.dp, 1 << i), 2)

    def mixed(self):
        return lax.rem(self.bit(0) + self.bit(1), 2)

    def half(self):
        return jnp.where(self.core == 0, self.bit(1), self.bit(2))


class Early:
    def __init__(self, shape, dtype):
        self.array = (shape, dtype)


def size(shape, dtype):
    shape = (*shape[:-1], -(-shape[-1] // 128) * 128)
    return functools.reduce(lambda a, b: a * b, shape) * jnp.dtype(dtype).itemsize


class Chain:
    def __init__(self):
        self.last = None

    def __call__(self, body, args, outs, name, us, scratch=(), stack=7, alias=()):
        arrays, in_specs, bufs, n_sem = [], [], [], 0
        spec = lambda space: pl.BlockSpec(memory_space=space)
        for a in args:
            if isinstance(a, Stack):
                arrays += a.parts
                in_specs += [spec(a.space)] * len(a.parts)
                bufs.append((a.shape, a.dtype))
                n_sem += isinstance(a, Late)
            else:
                raw = isinstance(a, Raw)
                arrays.append(a.array if raw else a)
                in_specs.append(spec(pltpu.HBM if raw else pltpu.VMEM))
        shapes, out_specs = [], []
        for o in outs:
            raw, early = isinstance(o, Raw), isinstance(o, Early)
            o = o.array if raw or early else o
            shapes.append(jax.ShapeDtypeStruct(*o))
            out_specs.append(spec(pltpu.HBM if raw or early else pltpu.VMEM))
            if early:
                bufs.append(o)
                n_sem += 1
        order = () if self.last is None else (self.last,)
        n_in, n_out, n_buf = len(arrays), len(shapes), len(bufs)

        def kernel(*refs):
            ins = list(refs[:n_in])
            refs = refs[n_in + len(order) :]
            results, refs = list(refs[:n_out]), refs[n_out:]
            spare, refs = list(refs[:n_buf]), refs[n_buf:]
            sems = refs[0] if n_sem else None
            extra = refs[1:] if n_sem else refs
            used = iter(range(n_sem))
            tiles = []
            for a in args:
                if isinstance(a, Stack):
                    buf, at, copies, fills = spare.pop(0), 0, [], []
                    if isinstance(a, Late):
                        copies.append(pltpu.make_async_copy(ins.pop(0), buf, sems.at[next(used)]))
                    else:
                        for part in a.parts:
                            n, row = part.shape[0], at
                            if a.turn is not None:
                                row = pl.multiple_of(jnp.where(a.turn() == 0, at, n - at), n)
                            fills.append((pl.ds(row, n), ins.pop(0)))
                            at += n
                    tiles.append(Tile(buf, copies, fills))
                    tiles[-1].start()
                else:
                    tiles.append(ins.pop(0))
            sends = []
            for o, r in zip(outs, results):
                if isinstance(o, Early):
                    buf = spare.pop(0)
                    copy = pltpu.make_async_copy(buf, r, sems.at[next(used)])
                    tiles.append(Tile(buf, [copy], out=True))
                    sends.append(tiles[-1])
                else:
                    tiles.append(r)
            body(*tiles, *extra)
            for t in sends:
                if not t.sent:
                    t.start()
            for t in tiles:
                if isinstance(t, Tile):
                    t.wait()

        room = sum(size(*b) for b in bufs)
        room += sum(size(m.shape, m.dtype) for m in scratch if m.memory_space == pltpu.VMEM)
        result = pl.pallas_call(
            kernel,
            out_shape=tuple(shapes),
            in_specs=in_specs + [spec(pl.ANY)] * len(order),
            out_specs=tuple(out_specs),
            input_output_aliases={
                next(i for i, a in enumerate(arrays) if a is v): o for v, o in alias
            },
            scratch_shapes=[pltpu.VMEM(*b) for b in bufs]
            + ([pltpu.SemaphoreType.DMA((n_sem,))] if n_sem else [])
            + list(scratch),
            compiler_params=pltpu.CompilerParams(vmem_limit_bytes=(stack << 20) + room),
            cost_estimate=pl.CostEstimate(
                flops=int(us * COST), bytes_accessed=1024, transcendentals=0
            ),
            name=name,
        )(*arrays, *order)
        self.last = result[0]
        return list(result)


def ready(t):
    return t.ready() if isinstance(t, Tile) else t


def begin(*tiles):
    for t in tiles:
        if isinstance(t, Tile):
            t.start()


COST = 1.15e9
TINY = 0.7


def row_loop(rows, width, sums, body):
    def step(i, carry):
        at = pl.ds(pl.multiple_of(i * ROWS, ROWS), ROWS)
        parts = body(at)
        return tuple(
            c + jnp.sum(p.reshape(ROWS // 8, 8, width), axis=0) for c, p in zip(carry, parts)
        )

    zero = tuple(jnp.zeros((8, width), F32) for _ in range(sums))
    done = lax.fori_loop(0, rows // ROWS, step, zero, unroll=3)
    return [jnp.sum(c, axis=0, keepdims=True) for c in done]


def normalize(v):
    centre = v - jnp.mean(v, axis=-1, keepdims=True)
    scale = lax.rsqrt(jnp.mean(centre * centre, axis=-1, keepdims=True) + EPS)
    return centre * scale, scale


def mix(chosen, vector, tokens):
    return jnp.where(chosen > 0.5, vector, tokens.astype(F32))


def setup_body(mask, hidden_bias, attn_bias, *refs):
    params, (msk, vecs, bias) = refs[:-3], refs[-3:]
    line = mask[...].astype(F32).reshape(1, mask.shape[0])
    msk[...] = jnp.broadcast_to(line, (8, mask.shape[0])).T
    for i, p in enumerate(params):
        vecs[i : i + 1, :] = p[...].reshape(1, p.shape[0])
    n = attn_bias.shape[1]
    bias[...] = jnp.zeros_like(bias)
    bias[0:1, :] = hidden_bias[...].reshape(1, hidden_bias.shape[0])
    bias[1:2, 0:n] = attn_bias[0:1, :]
    bias[1:2, n : 2 * n] = attn_bias[1:2, :]


def prep_body(vecs, msk, tok, cot, n1, top, topt, gdb):
    rows, width = tok.shape

    def body(at):
        chosen = msk[at, 0:1]
        hat, _ = normalize(mix(chosen, vecs[0:1, :], tok[at, :]))
        n1[at, :] = (hat * vecs[1:2, :] + vecs[2:3, :]).astype(BF16)
        grad = jnp.where(chosen > 0.5, cot[at, :].astype(F32), 0.0)
        top[at, :] = grad.astype(BF16)
        return (grad,)

    (total,) = row_loop(rows, width, 1, body)
    gdb[...] = total
    topt[...] = top[...].T


def copy_body(*refs):
    n = len(refs) // 2
    for src, dst in zip(refs[:n], refs[n:]):
        dst[...] = src[...]


def head_rows(cols):
    lane = lax.broadcasted_iota(jnp.int32, (1, cols), 1)
    return [
        ((lane >= h * HEAD) & (lane < (h + 1) * HEAD)).astype(F32).astype(BF16)
        for h in range(cols // HEAD)
    ]


def softmax(raw):
    peak = jnp.max(raw, axis=-1, keepdims=True)
    e = jnp.exp((raw - peak) * SCALE)
    return e * (1.0 / jnp.sum(e, axis=-1, keepdims=True))


def attn_fwd_body(slots, n1, bias, *refs):
    ins, outs = refs[:slots], refs[slots:]
    rows = n1.shape[0]
    cols = ins[0].shape[0] // 3
    marks = head_rows(cols)
    for s in range(slots):
        w, qkv, att = ins[s], outs[2 * s], outs[2 * s + 1]
        for j in range(3):
            y = dot_nt(n1[...], w[j * cols : (j + 1) * cols, :])
            if j != 1:
                y = y + bias[s : s + 1, (j // 2) * cols : (j // 2 + 1) * cols]
            qkv[j] = y.astype(BF16)
        begin(qkv)
        for i in range(rows // WIN):
            at = slice(i * WIN, (i + 1) * WIN)
            q, k, v = qkv[0, at, :], qkv[1, at, :], qkv[2, at, :]
            out = None
            for mark in marks:
                part = dot(softmax(dot_nt(q * mark, k)).astype(BF16), v * mark)
                out = part if out is None else out + part
            att[at, :] = out.astype(BF16)


def mid_body(slots, vecs, msk, tok, *refs):
    atts, merges = refs[:slots], refs[slots : 2 * slots]
    res, n2, n2t = refs[2 * slots :]
    rows, width = tok.shape
    total = dot(atts[0][...], merges[0][...])
    for s in range(1, slots):
        total = total + dot(atts[s][...], merges[s][...])
    res[...] = total
    out = res
    msk, tok, res, n2 = (ready(t) for t in (msk, tok, res, n2))

    def body(at):
        r = mix(msk[at, 0:1], vecs[0:1, :], tok[at, :]) + res[at, :] + vecs[3:4, :]
        res[at, :] = r
        hat, _ = normalize(r)
        n2[at, :] = (hat * vecs[4:5, :] + vecs[5:6, :]).astype(BF16)
        return ()

    row_loop(rows, width, 0, body)
    begin(out)
    n2t[...] = n2[...].T


GELU_C = 0.7978845608028654
GELU_A = 0.044715


def ffn_up_body(slots, bias, n2, topt, *refs):
    ups, outs = refs[:slots], refs[slots:]
    hidden = ups[0].shape[1]
    tile = 256
    for s in range(slots):
        act, slope, gd = outs[3 * s : 3 * s + 3]
        for t in range(hidden // tile):
            c = slice(t * tile, (t + 1) * tile)
            pre = dot(n2[...], ups[s][:, c]) + bias[s : s + 1, c]
            sq = pre * pre
            th = jnp.tanh(GELU_C * (pre + GELU_A * (sq * pre)))
            half = 0.5 * (1.0 + th)
            a = (pre * half).astype(BF16)
            rise = half + (0.5 * GELU_C) * pre * (1.0 - th * th) * (1.0 + (3.0 * GELU_A) * sq)
            act[:, c] = a
            slope[:, c] = rise.astype(BF16)
            gd[:, c] = dot(topt[...], a).astype(BF16)
        begin(gd, act, slope)


def ffn_back_body(slots, first, top, n2t, *refs):
    downs, slopes, acts, ups = (refs[i * slots : (i + 1) * slots] for i in range(4))
    refs = refs[4 * slots :]
    if first:
        gus, (y, g, gb, pg) = refs[:slots], refs[slots:]
    else:
        y_in, g_in = refs[:2]
        gus, (y, g, gb, pg) = refs[2 : 2 + slots], refs[2 + slots :]
    hidden = ups[0].shape[1]
    tile = 256
    for s in range(slots):
        for t in range(hidden // tile):
            c = slice(t * tile, (t + 1) * tile)
            low = (dot_nt(top[...], downs[s][c, :]) * slopes[s][:, c].astype(F32)).astype(BF16)
            pg[:, c] = low
            gb[s : s + 1, c] = jnp.sum(low.astype(F32), axis=0, keepdims=True)
            gus[s][:, c] = dot(n2t[...], low).astype(BF16)
        begin(gus[s])
        yp = dot(acts[s][...], downs[s][...])
        gp = dot_nt(pg[...], ups[s][...])
        if s == 0 and first:
            y[...] = yp
            g[...] = gp
        elif s == 0:
            y[...] = y_in[...] + yp
            g[...] = g_in[...] + gp
        else:
            y[...] = y[...] + yp
            g[...] = g[...] + gp


def norm_back(grad, gain, hat, scale):
    e = grad * gain
    back = e - jnp.mean(e, axis=-1, keepdims=True)
    return scale * (back - hat * jnp.mean(e * hat, axis=-1, keepdims=True))


def turn_body(vecs, res, y, g, top, *refs):
    slots = len(refs) // 2 - 2
    atts, gms, (out, rg, rl, sums) = refs[:slots], refs[slots : 2 * slots], refs[2 * slots :]
    rows, width = res.shape
    ends = (rg, out)
    res, out, rg, top = (ready(t) for t in (res, out, rg, top))

    def body(at):
        r = res[at, :]
        out[at, :] = (r + y[at, :] + vecs[6:7, :]).astype(BF16)
        hat, scale = normalize(r)
        grad = g[at, :]
        full = top[at, :].astype(F32) + norm_back(grad, vecs[4:5, :], hat, scale)
        rg[at, :] = full
        rl[at, :] = full.astype(BF16)
        return (grad * hat, grad, full)

    for i, total in enumerate(row_loop(rows, width, 3, body)):
        sums[i : i + 1, :] = total
    begin(*ends)
    for att, gm in zip(atts, gms):
        gm[...] = dot_tn(att[...], rl[...]).astype(BF16)


def stack_heads(x, marks):
    return jnp.concatenate([x * mark for mark in marks], axis=0)


def attn_bwd_body(m, rl, qkv, n1, a, dqt, dkv, gb, da):
    rows = n1.shape[0]
    cols = m.shape[0]
    marks = head_rows(cols)
    da[...] = dot_nt(rl[...], m[...]).astype(BF16)
    for i in range(rows // WIN):
        at = slice(i * WIN, (i + 1) * WIN)
        k = qkv[1, at, :]
        qs, gs = stack_heads(qkv[0, at, :], marks), stack_heads(da[at, :], marks)
        raw = dot_nt(k, qs)
        e = jnp.exp((raw - jnp.max(raw, axis=0, keepdims=True)) * SCALE)
        p = e * (1.0 / jnp.sum(e, axis=0, keepdims=True))
        dp = dot_nt(qkv[2, at, :], gs)
        dkv[1, at, :] = dot(p.astype(BF16), gs).astype(BF16)
        ds = (p * (dp - jnp.sum(p * dp, axis=0, keepdims=True))).astype(BF16)
        dkv[0, at, :] = (dot(ds, qs) * SCALE).astype(BF16)
        kt = k.T
        for h in range(cols // HEAD):
            mine = slice(h * HEAD, (h + 1) * HEAD)
            dq = dot(kt[mine, :], ds[:, h * WIN : (h + 1) * WIN])
            dqt[mine, at] = (dq * SCALE).astype(BF16)
    begin(dkv)
    a[0:cols, :] = dot(dqt[...], n1[...]).astype(BF16)
    gb[:, 0:cols] = dot_nt(jnp.ones((8, rows), BF16), dqt[...])[0:1, :]
    for j in range(2):
        a[(j + 1) * cols : (j + 2) * cols, :] = dot_tn(dkv[j], n1[...]).astype(BF16)
    gb[:, cols : 2 * cols] = jnp.sum(dkv[1].astype(F32), axis=0, keepdims=True)


def project_body(slots, *refs):
    dqs, dkvs, ws = (refs[i * slots : (i + 1) * slots] for i in range(3))
    g = refs[-1]
    cols = ws[0].shape[0] // 3
    for s in range(slots):
        w = ws[s]
        total = dot_tn(dqs[s][...], w[0:cols, :])
        total = total + dot(dkvs[s][0], w[cols : 2 * cols, :])
        total = total + dot(dkvs[s][1], w[2 * cols : 3 * cols, :])
        g[...] = total if s == 0 else g[...] + total


def last_body(vecs, msk, g, tok, rg, out, sums):
    rows, width = tok.shape
    end = out
    msk, tok, rg, out = (ready(t) for t in (msk, tok, rg, out))

    def body(at):
        chosen = msk[at, 0:1]
        hat, scale = normalize(mix(chosen, vecs[0:1, :], tok[at, :]))
        grad = g[at, :]
        full = rg[at, :] + norm_back(grad, vecs[1:2, :], hat, scale)
        out[at, :] = jnp.where(chosen > 0.5, 0.0, full)
        return (jnp.where(chosen > 0.5, full, 0.0), grad * hat, grad)

    for i, total in enumerate(row_loop(rows, width, 3, body)):
        sums[i : i + 1, :] = total


def pack_body(gb_a, gb_b, a0, a1, a2, a3, sums1, sums2, gdb, keep, give):
    n = a0.shape[1]
    for out, rows in ((keep, ((gb_a, 0, a0), (gb_b, 0, a2))), (give, ((gb_a, 1, a1), (gb_b, 1, a3)))):
        out[...] = jnp.zeros_like(out)
        out[0:3, :] = sums1[...]
        out[3:6, :] = sums2[...]
        out[6:7, :] = gdb[...]
        for i, (gb, row, ab) in enumerate(rows):
            out[7 + 2 * i : 8 + 2 * i, :] = gb[row : row + 1, :]
            out[8 + 2 * i : 9 + 2 * i, 0:n] = ab[...]


def pick_body(keep_in, got, keep, give):
    total = keep_in[...] + got[...]
    keep[...] = total[0:9, :]
    give[0:7, :] = total[0:7, :]
    give[7:9, :] = total[9:11, :]


def plus_body(a, b, out):
    out[...] = a[...] + b[...]


def half_body(*refs):
    pick = Position().mixed()
    k = len(refs) // 2
    for src, dst in zip(refs[:k], refs[k:]):
        n = dst.shape[0]
        dst[...] = src[pl.ds(pl.multiple_of(pick * n, n), n), :]


def cut_body(n, *refs):
    ins, outs, sem = refs[:n], refs[n : 2 * n], refs[-1]
    pick = Position().mixed()
    copies = []
    for i, (src, dst) in enumerate(zip(ins, outs)):
        half = dst.shape[0]
        at = pl.ds(pl.multiple_of(pick * half, half), half)
        copies.append(pltpu.make_async_copy(src.at[at], dst, sem.at[i]))
        copies[-1].start()
    for c in copies:
        c.wait()


def swap(links, v, *moves):
    n_dp, n_tensor = links
    moves = moves * (2 // len(moves))
    pairs = []
    for d in range(n_dp):
        for t in range(n_tensor):
            fd, ft = moves[t % 2]
            pairs.append((d * n_tensor + t, (d ^ fd) * n_tensor + (t ^ ft)))
    return lax.ppermute(v, ("dp", "tensor"), pairs)


CORE, ACROSS = (0, 1), (0, 2)
DP0, DP1, DP2 = (1, 0), (2, 0), (4, 0)


def add_rows(a, b, at):
    return a[at, :].astype(F32) + b[at, :].astype(F32)


def stage1_body(p0, p2, r1, r3, give, keep, own):
    here = Position()
    n = p0.shape[0] // 2
    y, lead = here.bit(0), here.core == 0
    first, other = (pl.ds(pl.multiple_of(k * n, n), n) for k in (y, 1 - y))
    near, far = add_rows(p0, r1, other), add_rows(p2, r3, first)
    give[:n, :] = jnp.where(lead, far, near).astype(BF16)
    keep[...] = jnp.where(lead, near, far)
    give[n:, :] = add_rows(p2, r3, other).astype(BF16)
    own[...] = add_rows(p0, r1, first)


def stage2_body(*refs):
    groups, give = refs[:-1], refs[-1]
    low = 0
    for keep, got in zip(groups[::2], groups[1::2]):
        n = keep.shape[0]
        give[low : low + n, :] = (keep[...] + got[n:, :].astype(F32)).astype(BF16)
        low += n


def stage3_body(*refs):
    groups, (got2, give, own, v) = refs[:-4], refs[-4:]
    low = 0
    for mine, got in zip(groups[::2], groups[1::2]):
        n = mine.shape[0]
        at = slice(low, low + n)
        v[at, :] = mine[...] + got[:n, :].astype(F32) + got2[at, :].astype(F32)
        low += n
    n = own.shape[0]
    mine = Position().half()
    take = lambda k: v[pl.ds(pl.multiple_of(k * n, n), n), :]
    give[...] = take(1 - mine).astype(BF16)
    own[...] = take(mine)


def stage4_body(own, got, give):
    give[...] = (own[...] + got[...].astype(F32)).astype(BF16)


def sum_body(a, b, w):
    w[...] = (a[...].astype(F32) + b[...].astype(F32)).astype(BF16)


def stack_body(a, b, out):
    n = a.shape[0]
    out[:n, :] = a[...]
    out[n:, :] = b[...]


def place_body(turned, w, r1, r2, *refs):
    outs, target = refs[:-1], refs[-1]
    here = Position()
    block = w.shape[0]
    lead = here.core == 0
    i = 0
    for part in (w, r1, r2):
        for k in range(part.shape[0] // block):
            y = jnp.where(lead, i % 2, i // 2)
            z = jnp.where(lead, i // 2, i % 2)
            at = lax.rem(y + here.bit(0), 2) * 2 + lax.rem(z + here.half(), 2)
            target[pl.ds(pl.multiple_of(at * block, block), block), :] = part[
                k * block : (k + 1) * block, :
            ].astype(F32)
            i += 1
    low, half = 0, target.shape[0] // 2
    for out in outs:
        n = out.shape[0] // 2
        if turned:
            out[...] = target[...].T
        else:
            out[:n, :] = target[low : low + n, :]
            out[n:, :] = target[half + low : half + low + n, :]
            low += n
        begin(out)


class Reduce:
    def __init__(self, links, chain, p0, p1, p2, p3):
        self.links, self.chain = links, chain
        self.parts = (p0, p2, swap(links, p1, CORE), swap(links, p3, CORE))
        self.rows, self.width = p0.shape
        self.sizes = [self.rows]

    def swap(self, *moves):
        self.got = swap(self.links, self.give, *moves)

    def stage1(self):
        n = self.rows // 2
        half = ((n, self.width), F32)
        self.give, keep, own = self.chain(
            stage1_body, self.parts, [((2 * n, self.width), BF16), half, half], "add1", TINY
        )
        self.swap(ACROSS, DP0)
        self.keeps, self.owns = [(keep, self.got)], [(own, self.got)]

    def join(self, other):
        self.rows += other.rows
        self.sizes += other.sizes
        self.keeps += other.keeps
        self.owns += other.owns

    def stage2(self):
        shape = ((self.rows // 2, self.width), BF16)
        (self.give,) = self.chain(stage2_body, sum(self.keeps, ()), [shape], "add2", TINY)
        self.swap(DP0, ACROSS)

    def stage3(self):
        n = self.rows // 4
        self.give, self.own = self.chain(
            stage3_body,
            (*sum(self.owns, ()), self.got),
            [((n, self.width), BF16), ((n, self.width), F32)],
            "add3",
            TINY,
            scratch=[pltpu.VMEM((2 * n, self.width), F32)],
        )
        self.swap(DP1, DP2)

    def stage4(self):
        shape = ((self.rows // 4, self.width), BF16)
        (self.give,) = self.chain(stage4_body, (self.own, self.got), [shape], "add4", TINY)
        self.swap(DP2, DP1)

    def spread1(self):
        shape = ((self.rows // 4, self.width), BF16)
        i = 3
        while (1 << i) < self.links[0]:
            both = self.give.astype(F32) + self.got.astype(F32)
            self.give = both.astype(BF16)
            self.swap((1 << i, 0))
            i += 1
        (self.give,) = self.chain(sum_body, (self.give, self.got), [shape], "add5", TINY)
        self.swap(DP0, DP2)
        self.parts = [self.give, self.got]

    def spread2(self):
        n, width = self.give.shape
        (self.give,) = self.chain(
            stack_body, (self.give, self.got), [((2 * n, width), BF16)], "stack", TINY
        )
        self.swap(DP1, DP0)
        self.parts.append(self.got)

    def place(self, turned=False):
        shapes = [(self.width, self.rows)] if turned else [(n, self.width) for n in self.sizes]
        return self.chain(
            functools.partial(place_body, turned),
            self.parts,
            [Early(shape, F32) for shape in shapes],
            "place",
            2,
            stack=7,
            scratch=[pltpu.VMEM((self.rows, self.width), F32)],
        )


class PlainReduce(Reduce):
    def stage1(self):
        p0, p2, r1, r3 = (v.astype(F32) for v in self.parts)
        far = swap(self.links, (p2 + r3).astype(BF16), ACROSS).astype(F32)
        self.totals = [lax.psum(p0 + r1 + far, "dp")]

    def join(self, other):
        self.totals += other.totals

    def skip(self):
        pass

    stage2 = stage3 = stage4 = spread1 = spread2 = skip

    def place(self, turned=False):
        return [self.totals[0].T] if turned else self.totals


class VectorSum:
    def __init__(self, links, chain, small, power):
        self.links, self.chain = links, chain
        width = small[-1].shape[1]
        self.shape = ((9, width), F32)
        self.keep, give = chain(pack_body, small, [((11, width), F32)] * 2, "pack", TINY)
        self.got = swap(links, give, CORE)
        bits = links[0].bit_length() - 1
        self.moves = [ACROSS] + [(1 << i, 0) for i in range(bits if power else 0)]
        self.power, self.first = power, True

    def step(self):
        if not self.moves:
            return
        if self.first:
            self.keep, give = self.chain(
                pick_body, (self.keep, self.got), [self.shape] * 2, "pick", TINY
            )
        else:
            self.add()
            give = self.keep
        self.first = False
        self.got = swap(self.links, give, self.moves.pop(0))

    def add(self):
        (self.keep,) = self.chain(plus_body, (self.keep, self.got), [self.shape], "plus", TINY)

    def finish(self):
        while self.moves:
            self.step()
        self.add()
        return self.keep if self.power else lax.psum(self.keep, "dp")


class Gather:
    def __init__(self, links, v):
        self.links, self.own = links, v
        self.near = swap(links, v, CORE)

    def send(self, half):
        self.half = swap(self.links, half, ACROSS)

    def spread(self):
        self.rest = swap(self.links, self.half, DP0, DP1)
        self.half_near = swap(self.links, self.half, CORE)

    def share(self):
        self.rest_near = swap(self.links, self.rest, CORE)

    def slots(self):
        turn = lambda: Position().mixed()
        rest_near = self.rest_near
        return [
            self.own,
            self.near,
            Stack(self.half, self.rest, turn=turn),
            Stack(self.half_near, rest_near, turn=turn),
        ]


class PlainGather(Gather):
    def send(self, half):
        self.far = swap(self.links, self.own, ACROSS)

    def spread(self):
        pass

    def share(self):
        pass

    def slots(self):
        return [self.own, self.near, self.far, swap(self.links, self.far, CORE)]


def per_device(
    n_dp,
    n_tensor,
    tokens,
    mask_bits,
    cotangent,
    mask_vector,
    first_gain,
    first_shift,
    attn_weight,
    attn_bias,
    merge_weight,
    merge_bias,
    second_gain,
    second_shift,
    up_weight,
    up_bias,
    down_weight,
    down_bias,
):
    rows, width = tokens.shape
    cols = attn_weight.shape[2]
    hidden = up_weight.shape[1]
    row = lambda v: v[None, :]
    links = (n_dp, n_tensor)
    power = n_dp >= 8 and n_dp & (n_dp - 1) == 0
    chain = Chain()
    make = functools.partial(Reduce if power else PlainReduce, links, chain)
    gather = functools.partial(PlainGather if n_dp % 4 else Gather, links)
    wide, tall, low = ((rows, width), F32), ((width, rows), BF16), ((rows, width), BF16)
    qkv_shape, att_shape = ((3, rows, cols), BF16), ((rows, cols), BF16)

    some_bias = lambda i, js: jnp.concatenate([biases[j][i : i + 1] for j in js])
    flat = jnp.transpose(attn_weight, (1, 2, 0)).reshape(3 * cols, width)
    g_attn, g_up, g_down = (gather(w) for w in (flat, up_weight, down_weight))
    g_merge = PlainGather(links, merge_weight)

    def cut(*weights):
        return chain(
            functools.partial(cut_body, len(weights)),
            [Raw(w) for w in weights],
            [((w.shape[0] // 2, w.shape[1]), BF16) for w in weights],
            "cut",
            1.5,
            scratch=[pltpu.SemaphoreType.DMA((len(weights),))],
            stack=57,
        )

    g_attn.send(*cut(flat))
    g_merge.send(None)

    msk, vecs, bias = chain(
        setup_body,
        (mask_bits, up_bias, attn_bias, mask_vector, first_gain, first_shift, merge_bias)
        + (second_gain, second_shift, down_bias),
        [((rows, 8), F32), ((7, width), F32), ((2, hidden), F32)],
        "setup",
        1,
    )
    bias_near, bias_far = swap(links, bias, CORE), swap(links, bias, ACROSS)
    biases = [bias, bias_near, bias_far, swap(links, bias_far, CORE)]

    def hold(*arrays):
        return chain(copy_body, arrays, [(v.shape, v.dtype) for v in arrays], "hold", TINY)

    def spread(gat):
        if n_dp % 4 == 0:
            (gat.half,) = hold(gat.half)
        gat.spread()

    def share(gat):
        if n_dp % 4 == 0:
            (gat.rest,) = hold(gat.rest)
        gat.share()

    n1, top, topt, gdb = chain(
        prep_body,
        (vecs, msk, tokens, cotangent),
        [low, low, Early(*tall), ((1, width), F32)],
        "prep",
        4,
    )
    spread(g_attn)
    parts = [((w.shape[0] // 2, w.shape[1]), BF16) for w in (up_weight, down_weight)]
    halves = chain(half_body, (up_weight, down_weight), parts, "half", 0.7)
    g_up.send(halves[0])
    g_down.send(halves[1])

    def attn_fwd(js, ws, us):
        r = chain(
            functools.partial(attn_fwd_body, 2),
            (n1, some_bias(1, js), *ws),
            [Early(*qkv_shape), att_shape] * 2,
            "attn_fwd",
            us,
        )
        return r[0::2], r[1::2]

    qkv_a, att_a = attn_fwd((0, 1), (flat, g_attn.near), 6)
    if n_dp % 4 == 0:
        g_attn.rest, g_merge.far = hold(g_attn.rest, g_merge.far)
    g_attn.share()
    wa = g_attn.slots()
    wm = g_merge.slots()
    qkv_b, att_b = attn_fwd((2, 3), wa[2:], 0.5)
    qkv, att = qkv_a + qkv_b, att_a + att_b
    spread(g_up)
    res, n2, n2t = chain(
        functools.partial(mid_body, 4),
        (vecs, msk, tokens, *att, *wm),
        [Early(*wide), low, tall],
        "mid",
        5.5,
    )

    def ffn_up(js, ups):
        r = chain(
            functools.partial(ffn_up_body, len(js)),
            (some_bias(0, js), n2, Late(topt), *ups),
            [((rows, hidden), BF16), ((rows, hidden), BF16), ((width, hidden), BF16)] * len(js),
            "ffn_up",
            2.75 * len(js),
        )
        return r[0::3], r[1::3], r[2::3]

    act_a, slope_a, gd_a = ffn_up((0, 1), (up_weight, g_up.near))
    share(g_up)
    spread(g_down)
    wu = g_up.slots()
    act_b, slope_b, gd_b = ffn_up((2, 3), wu[2:])
    red_d = make(*gd_a, *gd_b)

    share(g_down)
    pg = [pltpu.VMEM((rows, hidden), BF16)]
    grad_up = ((width, hidden), BF16)
    *gu_a, y, g, gb_a = chain(
        functools.partial(ffn_back_body, 2, True),
        (top, n2t, down_weight, g_down.near, *slope_a, *act_a, up_weight, g_up.near),
        [grad_up] * 2 + [wide, wide, ((2, hidden), F32)],
        "ffn_back",
        9,
        scratch=pg,
    )
    wd = g_down.slots()
    red_d.stage1()
    *gu_b, y, g, gb_b = chain(
        functools.partial(ffn_back_body, 2, False),
        (top, n2t, *wd[2:], *slope_b, *act_b, *wu[2:], y, g),
        [grad_up] * 2 + [wide, wide, ((2, hidden), F32)],
        "ffn_back",
        9,
        scratch=pg,
        alias=((y, 2), (g, 3)),
    )
    red_u = make(*gu_a, *gu_b)
    *gm, layer_out, res_grad, res_low, sums2 = chain(
        turn_body,
        (vecs, Late(res), y, g, top, *att),
        [((cols, width), BF16)] * 4 + [Early(*low), Early(*wide), low, ((3, width), F32)],
        "turn",
        5,
    )
    red_m = make(*gm)
    red_d.stage2()
    red_u.stage1()

    def attn_bwd(j):
        return chain(
            attn_bwd_body,
            (wm[j], res_low, Late(qkv[j]), Late(n1)),
            [((3 * cols, width), BF16), ((cols, rows), BF16), Early((2, rows, cols), BF16)]
            + [((1, 2 * cols), F32)],
            "attn_bwd",
            5,
            scratch=[pltpu.VMEM((rows, cols), BF16)],
        )

    back = [None] * 4
    back[1] = attn_bwd(1)
    red_m.stage1()
    back[3] = attn_bwd(3)
    red_d.stage3()
    back[2] = attn_bwd(2)
    red_u.join(red_m)
    red_u.stage2()
    red_d.stage4()
    back[0] = attn_bwd(0)
    red_a = make(*[b[0] for b in back])
    red_a.stage1()
    red_u.stage3()
    (g,) = chain(
        functools.partial(project_body, 4),
        (*[b[1] for b in back], *[Late(b[2]) for b in back], *wa),
        [wide],
        "project",
        6,
    )
    red_d.spread1()
    red_a.stage2()
    red_u.stage4()
    grad_tokens, sums1 = chain(
        last_body,
        (vecs, msk, g, Late(tokens), Late(res_grad)),
        [Early(*wide), ((3, width), F32)],
        "last",
        8,
        stack=7,
    )
    red_a.stage3()
    small = (gb_a, gb_b, *[b[3] for b in back], sums1, sums2, gdb)
    total = VectorSum(links, chain, small, power)
    red_d.spread2()
    red_u.spread1()
    total.step()
    red_a.stage4()
    total.step()
    red_u.spread2()
    red_a.spread1()
    total.step()
    red_a.spread2()
    (sum_d,) = red_d.place(turned=True)
    total.step()
    sum_u, sum_m = red_u.place()
    mine = total.finish()
    (sum_a,) = red_a.place()
    nv = 7
    grad_attn = jnp.transpose(sum_a.reshape(3, cols, width), (2, 0, 1))
    return (
        layer_out,
        grad_tokens,
        mine[0],
        mine[1],
        mine[2],
        grad_attn,
        mine[nv + 1, : 2 * cols].reshape(2, cols),
        sum_m,
        mine[5],
        mine[3],
        mine[4],
        sum_u,
        mine[nv],
        sum_d,
        mine[6],
    )


def solution(mesh):
    split = P(("dp", "tensor"), None)
    return jax.shard_map(
        functools.partial(per_device, mesh.shape["dp"], mesh.shape["tensor"]),
        mesh=mesh,
        in_specs=(
            split,
            P(("dp", "tensor")),
            split,
            P(),
            P(),
            P(),
            P(None, None, "tensor"),
            P(None, "tensor"),
            P("tensor", None),
            P(),
            P(),
            P(),
            P(None, "tensor"),
            P("tensor"),
            P("tensor", None),
            P(),
        ),
        out_specs=(
            split,
            split,
            P(),
            P(),
            P(),
            P(None, None, "tensor"),
            P(None, "tensor"),
            P("tensor", None),
            P(),
            P(),
            P(),
            P(None, "tensor"),
            P("tensor"),
            P("tensor", None),
            P(),
        ),
        check_vma=False,
    )
```

```python
import functools

import jax
import jax.numpy as jnp
from jax import lax
from jax.experimental import pallas as pl
from jax.experimental.pallas import tpu as pltpu
from jax.sharding import PartitionSpec as P

HEAD = 64
WIN = 256
EPS = 1e-06
SCALE = HEAD**-0.5
ROWS = 256
F32 = jnp.float32
BF16 = jnp.bfloat16


def dot(a, b):
    return lax.dot_general(a, b, (((1,), (0,)), ((), ())), preferred_element_type=F32)


def dot_nt(a, b):
    return lax.dot_general(a, b, (((1,), (1,)), ((), ())), preferred_element_type=F32)


def dot_tn(a, b):
    return lax.dot_general(a, b, (((0,), (0,)), ((), ())), preferred_element_type=F32)


class Stack:
    space = pltpu.VMEM

    def __init__(self, *parts, turn=None):
        self.parts, self.turn = parts, turn
        self.shape = (sum(p.shape[0] for p in parts), *parts[0].shape[1:])
        self.dtype = parts[0].dtype


class Late(Stack):
    space = pl.ANY


class Raw:
    def __init__(self, array):
        self.array = array


class Tile:
    def __init__(self, ref, copies=(), fills=(), out=False):
        self.ref, self.copies, self.fills, self.out, self.sent = ref, copies, fills, out, False
        self.shape, self.dtype = ref.shape, ref.dtype

    def start(self):
        for c in self.copies:
            c.start()
        self.sent = True

    def wait(self):
        for c in self.copies:
            c.wait()
        for at, part in self.fills:
            self.ref[at, :] = part[...]
        self.copies = self.fills = ()
        return self.ref

    def ready(self):
        return self.ref if self.out else self.wait()

    def __getitem__(self, at):
        return self.ready()[at]

    def __setitem__(self, at, value):
        self.ref[at] = value


class Position:
    def __init__(self):
        self.dp = lax.axis_index("dp")
        self.core = lax.rem(lax.axis_index("tensor"), 2)

    def bit(self, i):
        return lax.rem(lax.div(self.dp, 1 << i), 2)

    def mixed(self):
        return lax.rem(self.bit(0) + self.bit(1), 2)

    def half(self):
        return jnp.where(self.core == 0, self.bit(1), self.bit(2))


class Early:
    def __init__(self, shape, dtype):
        self.array = (shape, dtype)


def size(shape, dtype):
    shape = (*shape[:-1], -(-shape[-1] // 128) * 128)
    return functools.reduce(lambda a, b: a * b, shape) * jnp.dtype(dtype).itemsize


class Chain:
    def __init__(self):
        self.last = None

    def __call__(self, body, args, outs, name, us, scratch=(), stack=7, alias=()):
        arrays, in_specs, bufs, n_sem = [], [], [], 0
        spec = lambda space: pl.BlockSpec(memory_space=space)
        for a in args:
            if isinstance(a, Stack):
                arrays += a.parts
                in_specs += [spec(a.space)] * len(a.parts)
                bufs.append((a.shape, a.dtype))
                n_sem += isinstance(a, Late)
            else:
                raw = isinstance(a, Raw)
                arrays.append(a.array if raw else a)
                in_specs.append(spec(pltpu.HBM if raw else pltpu.VMEM))
        shapes, out_specs = [], []
        for o in outs:
            raw, early = isinstance(o, Raw), isinstance(o, Early)
            o = o.array if raw or early else o
            shapes.append(jax.ShapeDtypeStruct(*o))
            out_specs.append(spec(pltpu.HBM if raw or early else pltpu.VMEM))
            if early:
                bufs.append(o)
                n_sem += 1
        order = () if self.last is None else (self.last,)
        n_in, n_out, n_buf = len(arrays), len(shapes), len(bufs)

        def kernel(*refs):
            ins = list(refs[:n_in])
            refs = refs[n_in + len(order) :]
            results, refs = list(refs[:n_out]), refs[n_out:]
            spare, refs = list(refs[:n_buf]), refs[n_buf:]
            sems = refs[0] if n_sem else None
            extra = refs[1:] if n_sem else refs
            used = iter(range(n_sem))
            tiles = []
            for a in args:
                if isinstance(a, Stack):
                    buf, at, copies, fills = spare.pop(0), 0, [], []
                    if isinstance(a, Late):
                        copies.append(pltpu.make_async_copy(ins.pop(0), buf, sems.at[next(used)]))
                    else:
                        for part in a.parts:
                            n, row = part.shape[0], at
                            if a.turn is not None:
                                row = pl.multiple_of(jnp.where(a.turn() == 0, at, n - at), n)
                            fills.append((pl.ds(row, n), ins.pop(0)))
                            at += n
                    tiles.append(Tile(buf, copies, fills))
                    tiles[-1].start()
                else:
                    tiles.append(ins.pop(0))
            sends = []
            for o, r in zip(outs, results):
                if isinstance(o, Early):
                    buf = spare.pop(0)
                    copy = pltpu.make_async_copy(buf, r, sems.at[next(used)])
                    tiles.append(Tile(buf, [copy], out=True))
                    sends.append(tiles[-1])
                else:
                    tiles.append(r)
            body(*tiles, *extra)
            for t in sends:
                if not t.sent:
                    t.start()
            for t in tiles:
                if isinstance(t, Tile):
                    t.wait()

        room = sum(size(*b) for b in bufs)
        room += sum(size(m.shape, m.dtype) for m in scratch if m.memory_space == pltpu.VMEM)
        result = pl.pallas_call(
            kernel,
            out_shape=tuple(shapes),
            in_specs=in_specs + [spec(pl.ANY)] * len(order),
            out_specs=tuple(out_specs),
            input_output_aliases={
                next(i for i, a in enumerate(arrays) if a is v): o for v, o in alias
            },
            scratch_shapes=[pltpu.VMEM(*b) for b in bufs]
            + ([pltpu.SemaphoreType.DMA((n_sem,))] if n_sem else [])
            + list(scratch),
            compiler_params=pltpu.CompilerParams(vmem_limit_bytes=(stack << 20) + room),
            cost_estimate=pl.CostEstimate(
                flops=int(us * COST), bytes_accessed=1024, transcendentals=0
            ),
            name=name,
        )(*arrays, *order)
        self.last = result[0]
        return list(result)


def ready(t):
    return t.ready() if isinstance(t, Tile) else t


def begin(*tiles):
    for t in tiles:
        if isinstance(t, Tile):
            t.start()


COST = 1.15e9
TINY = 0.7


def row_loop(rows, width, sums, body):
    def step(i, carry):
        at = pl.ds(pl.multiple_of(i * ROWS, ROWS), ROWS)
        parts = body(at)
        return tuple(
            c + jnp.sum(p.reshape(ROWS // 8, 8, width), axis=0) for c, p in zip(carry, parts)
        )

    zero = tuple(jnp.zeros((8, width), F32) for _ in range(sums))
    done = lax.fori_loop(0, rows // ROWS, step, zero, unroll=3)
    return [jnp.sum(c, axis=0, keepdims=True) for c in done]


def normalize(v):
    centre = v - jnp.mean(v, axis=-1, keepdims=True)
    scale = lax.rsqrt(jnp.mean(centre * centre, axis=-1, keepdims=True) + EPS)
    return centre * scale, scale


def mix(chosen, vector, tokens):
    return jnp.where(chosen > 0.5, vector, tokens.astype(F32))


def setup_body(mask, hidden_bias, attn_bias, *refs):
    params, (msk, vecs, bias) = refs[:-3], refs[-3:]
    line = mask[...].astype(F32).reshape(1, mask.shape[0])
    msk[...] = jnp.broadcast_to(line, (8, mask.shape[0])).T
    for i, p in enumerate(params):
        vecs[i : i + 1, :] = p[...].reshape(1, p.shape[0])
    n = attn_bias.shape[1]
    bias[...] = jnp.zeros_like(bias)
    bias[0:1, :] = hidden_bias[...].reshape(1, hidden_bias.shape[0])
    bias[1:2, 0:n] = attn_bias[0:1, :]
    bias[1:2, n : 2 * n] = attn_bias[1:2, :]


def prep_body(vecs, msk, tok, cot, n1, top, topt, gdb):
    rows, width = tok.shape

    def body(at):
        chosen = msk[at, 0:1]
        hat, _ = normalize(mix(chosen, vecs[0:1, :], tok[at, :]))
        n1[at, :] = (hat * vecs[1:2, :] + vecs[2:3, :]).astype(BF16)
        grad = jnp.where(chosen > 0.5, cot[at, :].astype(F32), 0.0)
        top[at, :] = grad.astype(BF16)
        return (grad,)

    (total,) = row_loop(rows, width, 1, body)
    gdb[...] = total
    topt[...] = top[...].T


def copy_body(*refs):
    n = len(refs) // 2
    for src, dst in zip(refs[:n], refs[n:]):
        dst[...] = src[...]


def head_rows(cols):
    lane = lax.broadcasted_iota(jnp.int32, (1, cols), 1)
    return [
        ((lane >= h * HEAD) & (lane < (h + 1) * HEAD)).astype(F32).astype(BF16)
        for h in range(cols // HEAD)
    ]


def softmax(raw):
    peak = jnp.max(raw, axis=-1, keepdims=True)
    e = jnp.exp((raw - peak) * SCALE)
    return e * (1.0 / jnp.sum(e, axis=-1, keepdims=True))


def attn_fwd_body(slots, n1, bias, *refs):
    ins, outs = refs[:slots], refs[slots:]
    rows = n1.shape[0]
    cols = ins[0].shape[0] // 3
    marks = head_rows(cols)
    for s in range(slots):
        w, qkv, att = ins[s], outs[2 * s], outs[2 * s + 1]
        for j in range(3):
            y = dot_nt(n1[...], w[j * cols : (j + 1) * cols, :])
            if j != 1:
                y = y + bias[s : s + 1, (j // 2) * cols : (j // 2 + 1) * cols]
            qkv[j] = y.astype(BF16)
        begin(qkv)
        for i in range(rows // WIN):
            at = slice(i * WIN, (i + 1) * WIN)
            q, k, v = qkv[0, at, :], qkv[1, at, :], qkv[2, at, :]
            out = None
            for mark in marks:
                part = dot(softmax(dot_nt(q * mark, k)).astype(BF16), v * mark)
                out = part if out is None else out + part
            att[at, :] = out.astype(BF16)


def mid_body(slots, vecs, msk, tok, *refs):
    atts, merges = refs[:slots], refs[slots : 2 * slots]
    res, n2, n2t = refs[2 * slots :]
    rows, width = tok.shape
    total = dot(atts[0][...], merges[0][...])
    for s in range(1, slots):
        total = total + dot(atts[s][...], merges[s][...])
    res[...] = total
    out = res
    msk, tok, res, n2 = (ready(t) for t in (msk, tok, res, n2))

    def body(at):
        r = mix(msk[at, 0:1], vecs[0:1, :], tok[at, :]) + res[at, :] + vecs[3:4, :]
        res[at, :] = r
        hat, _ = normalize(r)
        n2[at, :] = (hat * vecs[4:5, :] + vecs[5:6, :]).astype(BF16)
        return ()

    row_loop(rows, width, 0, body)
    begin(out)
    n2t[...] = n2[...].T


GELU_C = 0.7978845608028654
GELU_A = 0.044715


def ffn_up_body(slots, bias, n2, topt, *refs):
    ups, outs = refs[:slots], refs[slots:]
    hidden = ups[0].shape[1]
    tile = 256
    for s in range(slots):
        act, slope, gd = outs[3 * s : 3 * s + 3]
        for t in range(hidden // tile):
            c = slice(t * tile, (t + 1) * tile)
            pre = dot(n2[...], ups[s][:, c]) + bias[s : s + 1, c]
            sq = pre * pre
            th = jnp.tanh(GELU_C * (pre + GELU_A * (sq * pre)))
            half = 0.5 * (1.0 + th)
            a = (pre * half).astype(BF16)
            rise = half + (0.5 * GELU_C) * pre * (1.0 - th * th) * (1.0 + (3.0 * GELU_A) * sq)
            act[:, c] = a
            slope[:, c] = rise.astype(BF16)
            gd[:, c] = dot(topt[...], a).astype(BF16)
        begin(gd, act, slope)


def ffn_back_body(slots, first, top, n2t, *refs):
    downs, slopes, acts, ups = (refs[i * slots : (i + 1) * slots] for i in range(4))
    refs = refs[4 * slots :]
    if first:
        gus, (y, g, gb, pg) = refs[:slots], refs[slots:]
    else:
        y_in, g_in = refs[:2]
        gus, (y, g, gb, pg) = refs[2 : 2 + slots], refs[2 + slots :]
    hidden = ups[0].shape[1]
    tile = 256
    for s in range(slots):
        for t in range(hidden // tile):
            c = slice(t * tile, (t + 1) * tile)
            low = (dot_nt(top[...], downs[s][c, :]) * slopes[s][:, c].astype(F32)).astype(BF16)
            pg[:, c] = low
            gb[s : s + 1, c] = jnp.sum(low.astype(F32), axis=0, keepdims=True)
            gus[s][:, c] = dot(n2t[...], low).astype(BF16)
        begin(gus[s])
        yp = dot(acts[s][...], downs[s][...])
        gp = dot_nt(pg[...], ups[s][...])
        if s == 0 and first:
            y[...] = yp
            g[...] = gp
        elif s == 0:
            y[...] = y_in[...] + yp
            g[...] = g_in[...] + gp
        else:
            y[...] = y[...] + yp
            g[...] = g[...] + gp


def norm_back(grad, gain, hat, scale):
    e = grad * gain
    back = e - jnp.mean(e, axis=-1, keepdims=True)
    return scale * (back - hat * jnp.mean(e * hat, axis=-1, keepdims=True))


def turn_body(vecs, res, y, g, top, *refs):
    slots = len(refs) // 2 - 2
    atts, gms, (out, rg, rl, sums) = refs[:slots], refs[slots : 2 * slots], refs[2 * slots :]
    rows, width = res.shape
    ends = (rg, out)
    res, out, rg, top = (ready(t) for t in (res, out, rg, top))

    def body(at):
        r = res[at, :]
        out[at, :] = (r + y[at, :] + vecs[6:7, :]).astype(BF16)
        hat, scale = normalize(r)
        grad = g[at, :]
        full = top[at, :].astype(F32) + norm_back(grad, vecs[4:5, :], hat, scale)
        rg[at, :] = full
        rl[at, :] = full.astype(BF16)
        return (grad * hat, grad, full)

    for i, total in enumerate(row_loop(rows, width, 3, body)):
        sums[i : i + 1, :] = total
    begin(*ends)
    for att, gm in zip(atts, gms):
        gm[...] = dot_tn(att[...], rl[...]).astype(BF16)


def stack_heads(x, marks):
    return jnp.concatenate([x * mark for mark in marks], axis=0)


def attn_bwd_body(m, rl, qkv, n1, a, dqt, dkv, gb, da):
    rows = n1.shape[0]
    cols = m.shape[0]
    marks = head_rows(cols)
    da[...] = dot_nt(rl[...], m[...]).astype(BF16)
    for i in range(rows // WIN):
        at = slice(i * WIN, (i + 1) * WIN)
        k = qkv[1, at, :]
        qs, gs = stack_heads(qkv[0, at, :], marks), stack_heads(da[at, :], marks)
        raw = dot_nt(k, qs)
        e = jnp.exp((raw - jnp.max(raw, axis=0, keepdims=True)) * SCALE)
        p = e * (1.0 / jnp.sum(e, axis=0, keepdims=True))
        dp = dot_nt(qkv[2, at, :], gs)
        dkv[1, at, :] = dot(p.astype(BF16), gs).astype(BF16)
        ds = (p * (dp - jnp.sum(p * dp, axis=0, keepdims=True))).astype(BF16)
        dkv[0, at, :] = (dot(ds, qs) * SCALE).astype(BF16)
        kt = k.T
        for h in range(cols // HEAD):
            mine = slice(h * HEAD, (h + 1) * HEAD)
            dq = dot(kt[mine, :], ds[:, h * WIN : (h + 1) * WIN])
            dqt[mine, at] = (dq * SCALE).astype(BF16)
    begin(dkv)
    a[0:cols, :] = dot(dqt[...], n1[...]).astype(BF16)
    gb[:, 0:cols] = dot_nt(jnp.ones((8, rows), BF16), dqt[...])[0:1, :]
    for j in range(2):
        a[(j + 1) * cols : (j + 2) * cols, :] = dot_tn(dkv[j], n1[...]).astype(BF16)
    gb[:, cols : 2 * cols] = jnp.sum(dkv[1].astype(F32), axis=0, keepdims=True)


def project_body(slots, *refs):
    dqs, dkvs, ws = (refs[i * slots : (i + 1) * slots] for i in range(3))
    g = refs[-1]
    cols = ws[0].shape[0] // 3
    for s in range(slots):
        w = ws[s]
        total = dot_tn(dqs[s][...], w[0:cols, :])
        total = total + dot(dkvs[s][0], w[cols : 2 * cols, :])
        total = total + dot(dkvs[s][1], w[2 * cols : 3 * cols, :])
        g[...] = total if s == 0 else g[...] + total


def last_body(vecs, msk, g, tok, rg, out, sums):
    rows, width = tok.shape
    end = out
    msk, tok, rg, out = (ready(t) for t in (msk, tok, rg, out))

    def body(at):
        chosen = msk[at, 0:1]
        hat, scale = normalize(mix(chosen, vecs[0:1, :], tok[at, :]))
        grad = g[at, :]
        full = rg[at, :] + norm_back(grad, vecs[1:2, :], hat, scale)
        out[at, :] = jnp.where(chosen > 0.5, 0.0, full)
        return (jnp.where(chosen > 0.5, full, 0.0), grad * hat, grad)

    for i, total in enumerate(row_loop(rows, width, 3, body)):
        sums[i : i + 1, :] = total


def pack_body(gb_a, gb_b, a0, a1, a2, a3, sums1, sums2, gdb, keep, give):
    n = a0.shape[1]
    for out, rows in ((keep, ((gb_a, 0, a0), (gb_b, 0, a2))), (give, ((gb_a, 1, a1), (gb_b, 1, a3)))):
        out[...] = jnp.zeros_like(out)
        out[0:3, :] = sums1[...]
        out[3:6, :] = sums2[...]
        out[6:7, :] = gdb[...]
        for i, (gb, row, ab) in enumerate(rows):
            out[7 + 2 * i : 8 + 2 * i, :] = gb[row : row + 1, :]
            out[8 + 2 * i : 9 + 2 * i, 0:n] = ab[...]


def pick_body(keep_in, got, keep, give):
    total = keep_in[...] + got[...]
    keep[...] = total[0:9, :]
    give[0:7, :] = total[0:7, :]
    give[7:9, :] = total[9:11, :]


def plus_body(a, b, out):
    out[...] = a[...] + b[...]


def half_body(*refs):
    pick = Position().mixed()
    k = len(refs) // 2
    for src, dst in zip(refs[:k], refs[k:]):
        n = dst.shape[0]
        dst[...] = src[pl.ds(pl.multiple_of(pick * n, n), n), :]


def cut_body(n, *refs):
    ins, outs, sem = refs[:n], refs[n : 2 * n], refs[-1]
    pick = Position().mixed()
    copies = []
    for i, (src, dst) in enumerate(zip(ins, outs)):
        half = dst.shape[0]
        at = pl.ds(pl.multiple_of(pick * half, half), half)
        copies.append(pltpu.make_async_copy(src.at[at], dst, sem.at[i]))
        copies[-1].start()
    for c in copies:
        c.wait()


def swap(links, v, *moves):
    n_dp, n_tensor = links
    moves = moves * (2 // len(moves))
    pairs = []
    for d in range(n_dp):
        for t in range(n_tensor):
            fd, ft = moves[t % 2]
            pairs.append((d * n_tensor + t, (d ^ fd) * n_tensor + (t ^ ft)))
    return lax.ppermute(v, ("dp", "tensor"), pairs)


CORE, ACROSS = (0, 1), (0, 2)
DP0, DP1, DP2 = (1, 0), (2, 0), (4, 0)


def add_rows(a, b, at):
    return a[at, :].astype(F32) + b[at, :].astype(F32)


def stage1_body(p0, p2, r1, r3, give, keep, own):
    here = Position()
    n = p0.shape[0] // 2
    y, lead = here.bit(0), here.core == 0
    first, other = (pl.ds(pl.multiple_of(k * n, n), n) for k in (y, 1 - y))
    near, far = add_rows(p0, r1, other), add_rows(p2, r3, first)
    give[:n, :] = jnp.where(lead, far, near).astype(BF16)
    keep[...] = jnp.where(lead, near, far)
    give[n:, :] = add_rows(p2, r3, other).astype(BF16)
    own[...] = add_rows(p0, r1, first)


def stage2_body(*refs):
    groups, give = refs[:-1], refs[-1]
    low = 0
    for keep, got in zip(groups[::2], groups[1::2]):
        n = keep.shape[0]
        give[low : low + n, :] = (keep[...] + got[n:, :].astype(F32)).astype(BF16)
        low += n


def stage3_body(*refs):
    groups, (got2, give, own, v) = refs[:-4], refs[-4:]
    low = 0
    for mine, got in zip(groups[::2], groups[1::2]):
        n = mine.shape[0]
        at = slice(low, low + n)
        v[at, :] = mine[...] + got[:n, :].astype(F32) + got2[at, :].astype(F32)
        low += n
    n = own.shape[0]
    mine = Position().half()
    take = lambda k: v[pl.ds(pl.multiple_of(k * n, n), n), :]
    give[...] = take(1 - mine).astype(BF16)
    own[...] = take(mine)


def stage4_body(own, got, give):
    give[...] = (own[...] + got[...].astype(F32)).astype(BF16)


def sum_body(a, b, w):
    w[...] = (a[...].astype(F32) + b[...].astype(F32)).astype(BF16)


def stack_body(a, b, out):
    n = a.shape[0]
    out[:n, :] = a[...]
    out[n:, :] = b[...]


def place_body(turned, w, r1, r2, *refs):
    outs, target = refs[:-1], refs[-1]
    here = Position()
    block = w.shape[0]
    lead = here.core == 0
    i = 0
    for part in (w, r1, r2):
        for k in range(part.shape[0] // block):
            y = jnp.where(lead, i % 2, i // 2)
            z = jnp.where(lead, i // 2, i % 2)
            at = lax.rem(y + here.bit(0), 2) * 2 + lax.rem(z + here.half(), 2)
            target[pl.ds(pl.multiple_of(at * block, block), block), :] = part[
                k * block : (k + 1) * block, :
            ].astype(F32)
            i += 1
    low, half = 0, target.shape[0] // 2
    for out in outs:
        n = out.shape[0] // 2
        if turned:
            out[...] = target[...].T
        else:
            out[:n, :] = target[low : low + n, :]
            out[n:, :] = target[half + low : half + low + n, :]
            low += n
        begin(out)


class Reduce:
    def __init__(self, links, chain, p0, p1, p2, p3):
        self.links, self.chain = links, chain
        self.parts = (p0, p2, swap(links, p1, CORE), swap(links, p3, CORE))
        self.rows, self.width = p0.shape
        self.sizes = [self.rows]

    def swap(self, *moves):
        self.got = swap(self.links, self.give, *moves)

    def stage1(self):
        n = self.rows // 2
        half = ((n, self.width), F32)
        self.give, keep, own = self.chain(
            stage1_body, self.parts, [((2 * n, self.width), BF16), half, half], "add1", TINY
        )
        self.swap(ACROSS, DP0)
        self.keeps, self.owns = [(keep, self.got)], [(own, self.got)]

    def join(self, other):
        self.rows += other.rows
        self.sizes += other.sizes
        self.keeps += other.keeps
        self.owns += other.owns

    def stage2(self):
        shape = ((self.rows // 2, self.width), BF16)
        (self.give,) = self.chain(stage2_body, sum(self.keeps, ()), [shape], "add2", TINY)
        self.swap(DP0, ACROSS)

    def stage3(self):
        n = self.rows // 4
        self.give, self.own = self.chain(
            stage3_body,
            (*sum(self.owns, ()), self.got),
            [((n, self.width), BF16), ((n, self.width), F32)],
            "add3",
            TINY,
            scratch=[pltpu.VMEM((2 * n, self.width), F32)],
        )
        self.swap(DP1, DP2)

    def stage4(self):
        shape = ((self.rows // 4, self.width), BF16)
        (self.give,) = self.chain(stage4_body, (self.own, self.got), [shape], "add4", TINY)
        self.swap(DP2, DP1)

    def spread1(self):
        shape = ((self.rows // 4, self.width), BF16)
        i = 3
        while (1 << i) < self.links[0]:
            both = self.give.astype(F32) + self.got.astype(F32)
            self.give = both.astype(BF16)
            self.swap((1 << i, 0))
            i += 1
        (self.give,) = self.chain(sum_body, (self.give, self.got), [shape], "add5", TINY)
        self.swap(DP0, DP2)
        self.parts = [self.give, self.got]

    def spread2(self):
        n, width = self.give.shape
        (self.give,) = self.chain(
            stack_body, (self.give, self.got), [((2 * n, width), BF16)], "stack", TINY
        )
        self.swap(DP1, DP0)
        self.parts.append(self.got)

    def place(self, turned=False):
        shapes = [(self.width, self.rows)] if turned else [(n, self.width) for n in self.sizes]
        return self.chain(
            functools.partial(place_body, turned),
            self.parts,
            [(shape, F32) for shape in shapes],
            "place",
            2,
            stack=7,
            scratch=[pltpu.VMEM((self.rows, self.width), F32)],
        )


class PlainReduce(Reduce):
    def stage1(self):
        p0, p2, r1, r3 = (v.astype(F32) for v in self.parts)
        far = swap(self.links, (p2 + r3).astype(BF16), ACROSS).astype(F32)
        self.totals = [lax.psum(p0 + r1 + far, "dp")]

    def join(self, other):
        self.totals += other.totals

    def skip(self):
        pass

    stage2 = stage3 = stage4 = spread1 = spread2 = skip

    def place(self, turned=False):
        return [self.totals[0].T] if turned else self.totals


class VectorSum:
    def __init__(self, links, chain, small, power):
        self.links, self.chain = links, chain
        width = small[-1].shape[1]
        self.shape = ((9, width), F32)
        self.keep, give = chain(pack_body, small, [((11, width), F32)] * 2, "pack", TINY)
        self.got = swap(links, give, CORE)
        bits = links[0].bit_length() - 1
        self.moves = [ACROSS] + [(1 << i, 0) for i in range(bits if power else 0)]
        self.power, self.first = power, True

    def step(self):
        if not self.moves:
            return
        if self.first:
            self.keep, give = self.chain(
                pick_body, (self.keep, self.got), [self.shape] * 2, "pick", TINY
            )
        else:
            self.add()
            give = self.keep
        self.first = False
        self.got = swap(self.links, give, self.moves.pop(0))

    def add(self):
        (self.keep,) = self.chain(plus_body, (self.keep, self.got), [self.shape], "plus", TINY)

    def finish(self):
        while self.moves:
            self.step()
        self.add()
        return self.keep if self.power else lax.psum(self.keep, "dp")


class Gather:
    def __init__(self, links, v):
        self.links, self.own = links, v
        self.near = swap(links, v, CORE)

    def send(self, half):
        self.half = swap(self.links, half, ACROSS)

    def spread(self):
        self.rest = swap(self.links, self.half, DP0, DP1)
        self.half_near = swap(self.links, self.half, CORE)

    def share(self):
        self.rest_near = swap(self.links, self.rest, CORE)

    def slots(self):
        turn = lambda: Position().mixed()
        rest_near = self.rest_near
        return [
            self.own,
            self.near,
            Stack(self.half, self.rest, turn=turn),
            Stack(self.half_near, rest_near, turn=turn),
        ]


class PlainGather(Gather):
    def send(self, half):
        self.far = swap(self.links, self.own, ACROSS)

    def spread(self):
        pass

    def share(self):
        pass

    def slots(self):
        return [self.own, self.near, self.far, swap(self.links, self.far, CORE)]


def per_device(
    n_dp,
    n_tensor,
    tokens,
    mask_bits,
    cotangent,
    mask_vector,
    first_gain,
    first_shift,
    attn_weight,
    attn_bias,
    merge_weight,
    merge_bias,
    second_gain,
    second_shift,
    up_weight,
    up_bias,
    down_weight,
    down_bias,
):
    rows, width = tokens.shape
    cols = attn_weight.shape[2]
    hidden = up_weight.shape[1]
    row = lambda v: v[None, :]
    links = (n_dp, n_tensor)
    power = n_dp >= 8 and n_dp & (n_dp - 1) == 0
    chain = Chain()
    make = functools.partial(Reduce if power else PlainReduce, links, chain)
    gather = functools.partial(PlainGather if n_dp % 4 else Gather, links)
    wide, tall, low = ((rows, width), F32), ((width, rows), BF16), ((rows, width), BF16)
    qkv_shape, att_shape = ((3, rows, cols), BF16), ((rows, cols), BF16)

    some_bias = lambda i, js: jnp.concatenate([biases[j][i : i + 1] for j in js])
    flat = jnp.transpose(attn_weight, (1, 2, 0)).reshape(3 * cols, width)
    g_attn, g_up, g_down = (gather(w) for w in (flat, up_weight, down_weight))
    g_merge = PlainGather(links, merge_weight)

    def cut(*weights):
        return chain(
            functools.partial(cut_body, len(weights)),
            [Raw(w) for w in weights],
            [((w.shape[0] // 2, w.shape[1]), BF16) for w in weights],
            "cut",
            1.5,
            scratch=[pltpu.SemaphoreType.DMA((len(weights),))],
            stack=57,
        )

    g_attn.send(*cut(flat))
    g_merge.send(None)

    msk, vecs, bias = chain(
        setup_body,
        (mask_bits, up_bias, attn_bias, mask_vector, first_gain, first_shift, merge_bias)
        + (second_gain, second_shift, down_bias),
        [((rows, 8), F32), ((7, width), F32), ((2, hidden), F32)],
        "setup",
        1,
    )
    bias_near, bias_far = swap(links, bias, CORE), swap(links, bias, ACROSS)
    biases = [bias, bias_near, bias_far, swap(links, bias_far, CORE)]

    def hold(*arrays):
        return chain(copy_body, arrays, [(v.shape, v.dtype) for v in arrays], "hold", TINY)

    def spread(gat):
        if n_dp % 4 == 0:
            (gat.half,) = hold(gat.half)
        gat.spread()

    def share(gat):
        if n_dp % 4 == 0:
            (gat.rest,) = hold(gat.rest)
        gat.share()

    n1, top, topt, gdb = chain(
        prep_body,
        (vecs, msk, tokens, cotangent),
        [low, low, Early(*tall), ((1, width), F32)],
        "prep",
        4,
    )
    spread(g_attn)
    parts = [((w.shape[0] // 2, w.shape[1]), BF16) for w in (up_weight, down_weight)]
    halves = chain(half_body, (up_weight, down_weight), parts, "half", 0.7)
    g_up.send(halves[0])
    g_down.send(halves[1])

    def attn_fwd(js, ws, us):
        r = chain(
            functools.partial(attn_fwd_body, 2),
            (n1, some_bias(1, js), *ws),
            [Early(*qkv_shape), att_shape] * 2,
            "attn_fwd",
            us,
        )
        return r[0::2], r[1::2]

    qkv_a, att_a = attn_fwd((0, 1), (flat, g_attn.near), 6)
    if n_dp % 4 == 0:
        g_attn.rest, g_merge.far = hold(g_attn.rest, g_merge.far)
    g_attn.share()
    wa = g_attn.slots()
    wm = g_merge.slots()
    qkv_b, att_b = attn_fwd((2, 3), wa[2:], 0.5)
    qkv, att = qkv_a + qkv_b, att_a + att_b
    spread(g_up)
    res, n2, n2t = chain(
        functools.partial(mid_body, 4),
        (vecs, msk, tokens, *att, *wm),
        [Early(*wide), low, tall],
        "mid",
        5.5,
    )

    def ffn_up(js, ups):
        r = chain(
            functools.partial(ffn_up_body, len(js)),
            (some_bias(0, js), n2, Late(topt), *ups),
            [((rows, hidden), BF16), ((rows, hidden), BF16), ((width, hidden), BF16)] * len(js),
            "ffn_up",
            2.75 * len(js),
        )
        return r[0::3], r[1::3], r[2::3]

    act_a, slope_a, gd_a = ffn_up((0, 1), (up_weight, g_up.near))
    share(g_up)
    spread(g_down)
    wu = g_up.slots()
    act_b, slope_b, gd_b = ffn_up((2, 3), wu[2:])
    red_d = make(*gd_a, *gd_b)

    share(g_down)
    pg = [pltpu.VMEM((rows, hidden), BF16)]
    grad_up = ((width, hidden), BF16)
    *gu_a, y, g, gb_a = chain(
        functools.partial(ffn_back_body, 2, True),
        (top, n2t, down_weight, g_down.near, *slope_a, *act_a, up_weight, g_up.near),
        [grad_up] * 2 + [wide, wide, ((2, hidden), F32)],
        "ffn_back",
        9,
        scratch=pg,
    )
    wd = g_down.slots()
    red_d.stage1()
    *gu_b, y, g, gb_b = chain(
        functools.partial(ffn_back_body, 2, False),
        (top, n2t, *wd[2:], *slope_b, *act_b, *wu[2:], y, g),
        [grad_up] * 2 + [wide, wide, ((2, hidden), F32)],
        "ffn_back",
        9,
        scratch=pg,
        alias=((y, 2), (g, 3)),
    )
    red_u = make(*gu_a, *gu_b)
    *gm, layer_out, res_grad, res_low, sums2 = chain(
        turn_body,
        (vecs, Late(res), y, g, top, *att),
        [((cols, width), BF16)] * 4 + [Early(*low), Early(*wide), low, ((3, width), F32)],
        "turn",
        5,
    )
    red_m = make(*gm)
    red_d.stage2()
    red_u.stage1()

    def attn_bwd(j):
        return chain(
            attn_bwd_body,
            (wm[j], res_low, Late(qkv[j]), Late(n1)),
            [((3 * cols, width), BF16), ((cols, rows), BF16), Early((2, rows, cols), BF16)]
            + [((1, 2 * cols), F32)],
            "attn_bwd",
            5,
            scratch=[pltpu.VMEM((rows, cols), BF16)],
        )

    back = [None] * 4
    back[1] = attn_bwd(1)
    red_m.stage1()
    back[3] = attn_bwd(3)
    red_d.stage3()
    back[2] = attn_bwd(2)
    red_u.join(red_m)
    red_u.stage2()
    red_d.stage4()
    back[0] = attn_bwd(0)
    red_a = make(*[b[0] for b in back])
    red_a.stage1()
    red_u.stage3()
    (g,) = chain(
        functools.partial(project_body, 4),
        (*[b[1] for b in back], *[Late(b[2]) for b in back], *wa),
        [wide],
        "project",
        6,
    )
    red_d.spread1()
    red_a.stage2()
    red_u.stage4()
    grad_tokens, sums1 = chain(
        last_body,
        (vecs, msk, g, Late(tokens), Late(res_grad)),
        [wide, ((3, width), F32)],
        "last",
        8,
        stack=7,
    )
    red_a.stage3()
    small = (gb_a, gb_b, *[b[3] for b in back], sums1, sums2, gdb)
    total = VectorSum(links, chain, small, power)
    red_d.spread2()
    red_u.spread1()
    total.step()
    red_a.stage4()
    total.step()
    red_u.spread2()
    red_a.spread1()
    total.step()
    red_a.spread2()
    (sum_d,) = red_d.place(turned=True)
    total.step()
    sum_u, sum_m = red_u.place()
    mine = total.finish()
    (sum_a,) = red_a.place()
    nv = 7
    grad_attn = jnp.transpose(sum_a.reshape(3, cols, width), (2, 0, 1))
    return (
        layer_out,
        grad_tokens,
        mine[0],
        mine[1],
        mine[2],
        grad_attn,
        mine[nv + 1, : 2 * cols].reshape(2, cols),
        sum_m,
        mine[5],
        mine[3],
        mine[4],
        sum_u,
        mine[nv],
        sum_d,
        mine[6],
    )


def solution(mesh):
    split = P(("dp", "tensor"), None)
    return jax.shard_map(
        functools.partial(per_device, mesh.shape["dp"], mesh.shape["tensor"]),
        mesh=mesh,
        in_specs=(
            split,
            P(("dp", "tensor")),
            split,
            P(),
            P(),
            P(),
            P(None, None, "tensor"),
            P(None, "tensor"),
            P("tensor", None),
            P(),
            P(),
            P(),
            P(None, "tensor"),
            P("tensor"),
            P("tensor", None),
            P(),
        ),
        out_specs=(
            split,
            split,
            P(),
            P(),
            P(),
            P(None, None, "tensor"),
            P(None, "tensor"),
            P("tensor", None),
            P(),
            P(),
            P(),
            P(None, "tensor"),
            P("tensor"),
            P("tensor", None),
            P(),
        ),
        check_vma=False,
    )
```
